32 devices in a mesh: dp: 8 (over z, core), tensor: 4 (over y, x).
Axes of the slice: x: 2, y: 2, z: 4, core: 2. Of those that a mesh axis runs over, the one named last changes fastest.
Arguments:
- layer_input: bfloat16 [8192, 2048], P(('dp', 'tensor')), may hold values from -6 to 6
- lengths: int32 [8], P('dp'), may hold values from 256 to 1024, as said below
- w_query: bfloat16 [2048, 2048], P('dp', 'tensor'), may hold values from -0.125 to 0.125
- w_keyvalue: bfloat16 [2048, 256], P('dp'), may hold values from -0.125 to 0.125
- w_project: bfloat16 [2048, 2048], P('tensor', 'dp'), may hold values from -1 to 1
- w_gate: bfloat16 [2048, 5632], P('dp', 'tensor'), may hold values from -0.125 to 0.125
- w_up: bfloat16 [2048, 5632], P('dp', 'tensor'), may hold values from -0.125 to 0.125
- w_down: bfloat16 [5632, 2048], P('tensor', 'dp'), may hold values from -0.078125 to 0.078125
- gain_attn: bfloat16 [2048], P('dp'), may hold values from 0.099609375 to 1.8984375
- gain_mlp: bfloat16 [2048], P('dp'), may hold values from 0.099609375 to 1.8984375
- out_grad: bfloat16 [8192, 2048], P(('dp', 'tensor')), may hold values from -6 to 6
- kv_grad: bfloat16 [8192, 256], P(('dp', 'tensor')), may hold values from -6 to 6
Outputs:
- output: bfloat16 [8192, 2048], P(('dp', 'tensor'))
- input_grad: float32 [8192, 2048], P(('dp', 'tensor'))
- grad_query: float32 [2048, 2048], P('dp', 'tensor')
- grad_keyvalue: float32 [2048, 256], P('dp')
- grad_project: float32 [2048, 2048], P('tensor', 'dp')
- grad_gate: float32 [2048, 5632], P('dp', 'tensor')
- grad_up: float32 [2048, 5632], P('dp', 'tensor')
- grad_down: float32 [5632, 2048], P('tensor', 'dp')
- grad_gain_attn: float32 [2048], P('dp')
- grad_gain_mlp: float32 [2048], P('dp')
The draws below stay inside these ranges and needn't reach their ends.
Inputs may be any that keep to these rules, and one draw needn't show every extreme that they name: Each slot's sequence fills its first lengths[s] positions; one slot holds 1024 and another 256.
All inputs are finite; a program needn't handle non-finite values.
Results may differ from the reference program's by a relative error of at most 0.015.
Values may be sent and summed in bfloat16 or wider, within the bound.
No kernel may reach another device: no remote copies, remote signals or barrier semaphores. Data moves between devices by JAX's collectives and lax.ppermute only.
A program may use at most 192 MiB of HBM per device.

```python
import math
import jax
import jax.numpy as jnp
from jax import lax

D = 2048
H = 16
HD = 128
FF = 5632
SLOT_LEN = 1024
QBLOCK = 512
MIN_LEN = 256
SLOTS = 8
TOKENS = 8192


def draw_lengths(key, part):
    random_lengths = jax.random.randint(jax.random.fold_in(key, 1), (SLOTS,), MIN_LEN, SLOT_LEN + 1)
    full_slot = jax.random.randint(jax.random.fold_in(key, 2), (), 0, SLOTS)
    offset = jax.random.randint(jax.random.fold_in(key, 3), (), 1, SLOTS)
    short_slot = (full_slot + offset) % SLOTS
    slot_ids = jnp.arange(SLOTS)
    random_lengths = jnp.where(slot_ids == full_slot, SLOT_LEN, random_lengths)
    random_lengths = jnp.where(slot_ids == short_slot, MIN_LEN, random_lengths)
    return random_lengths.astype(jnp.int32)


def steps_of(rng, shape, pieces, low, top_value):
    factor_of = 1.0
    for axis_at, blocks in pieces:
        draws = jax.random.uniform(jax.random.fold_in(jax.random.fold_in(rng, 6), axis_at), (blocks,), jnp.float32, low / len(pieces), top_value / len(pieces))
        factor_of = factor_of * jnp.repeat(jnp.exp(draws), shape[axis_at] // blocks).reshape((-1,) + (1,) * (len(shape) - 1 - axis_at))
    return factor_of


def bell_draw(own_key, extent, scale, most, pieces=(), kind=jnp.bfloat16):
    factor_of = steps_of(own_key, extent, pieces, -0.22, 0.18) if pieces else 1.0
    values = jax.random.normal(own_key, extent, jnp.float32) * scale * factor_of
    return jnp.minimum(jnp.maximum(values, -most), most).astype(kind)


def setup_inputs(seed: int = 0) -> dict:
    key_list = jax.random.split(jax.random.key(seed), 13)
    layer_input = bell_draw(key_list[0], (TOKENS, D), 1.0, 6.0, ((0, 32),))
    lengths = draw_lengths(jax.random.fold_in(key_list[12], 71), 0)
    w_query = bell_draw(key_list[2], (D, H * HD), D ** -0.5, 0.125, ((0, 8), (1, 4)))
    w_keyvalue = bell_draw(key_list[3], (D, 2 * HD), D ** -0.5, 0.125, ((0, 8),))
    w_project = bell_draw(key_list[4], (H * HD, D), (H * HD // 64) ** -0.5, 1.0, ((0, 4), (1, 8)))
    w_gate = bell_draw(key_list[5], (D, FF), D ** -0.5, 0.125, ((0, 8), (1, 4)))
    w_up = bell_draw(key_list[6], (D, FF), D ** -0.5, 0.125, ((0, 8), (1, 4)))
    w_down = bell_draw(key_list[7], (FF, D), FF ** -0.5, 0.078125, ((0, 4), (1, 8)))
    gain_attn = jnp.clip(1.0 + 0.18 * jax.random.normal(key_list[8], (D,), jnp.float32), 0.099609375, 1.8984375).astype(jnp.bfloat16)
    gain_mlp = jnp.clip(1.0 + 0.18 * jax.random.normal(key_list[9], (D,), jnp.float32), 0.099609375, 1.8984375).astype(jnp.bfloat16)
    out_grad = bell_draw(key_list[10], (TOKENS, D), 1.0, 6.0, ((0, 32),))
    kv_grad = bell_draw(key_list[11], (TOKENS, 2 * HD), 1.0, 6.0, ((0, 32),))
    return dict(layer_input=layer_input, lengths=lengths, w_query=w_query, w_keyvalue=w_keyvalue, w_project=w_project, w_gate=w_gate, w_up=w_up, w_down=w_down, gain_attn=gain_attn, gain_mlp=gain_mlp, out_grad=out_grad, kv_grad=kv_grad)


eps = 1e-05
rope_base = 10000.0
neg_big = -1e+30
highest = lax.Precision.HIGHEST

@jax.custom_vjp
def low(v):
    return lax.optimization_barrier(v.astype(jnp.bfloat16)).astype(jnp.float32)

@jax.custom_vjp
def low_back(v):
    return v

def low_keep(v):
    return (low(v), None)

def low_pass(kept, grad):
    return (grad,)

def back_keep(v):
    return (v, None)

def back_low(kept, grad):
    return (low(grad),)
low.defvjp(low_keep, low_pass)
low_back.defvjp(back_keep, back_low)

def rope_tables(positions, head_size):
    half_size = head_size // 2
    frequency = rope_base ** (-(jnp.arange(half_size, dtype=jnp.float32) * 2.0 / head_size))
    angles = positions.astype(jnp.float32)[:, None] * frequency[None, :]
    return (jnp.cos(angles), jnp.sin(angles))

def rotate(values, cosine, sine_vals):
    half_size = values.shape[-1] // 2
    first_half = values[..., :half_size]
    second_half = values[..., half_size:]
    cosine = cosine[:, None, :]
    sine_vals = sine_vals[:, None, :]
    return jnp.concatenate([first_half * cosine - second_half * sine_vals, second_half * cosine + first_half * sine_vals], axis=-1)

def norm_rows(values, gain_vec):
    inv_norm = lax.rsqrt(lax.optimization_barrier(jnp.mean(values * values, axis=-1, keepdims=True)) + eps)
    return values * inv_norm * gain_vec

def swiglu(gate_act, up_act):
    return jax.nn.silu(gate_act) * up_act

def slot_forward(params, slot_input, length):
    w_query, w_keyvalue, w_project, w_gate, w_up, w_down, gain_attn, gain_mlp = params
    position = jnp.arange(SLOT_LEN, dtype=jnp.int32)
    cos_table, sin_table = rope_tables(position, HD)
    inv_root = 1.0 / math.sqrt(HD)
    normed_one = low(norm_rows(slot_input, gain_attn))
    query_raw = low_back(jnp.dot(normed_one, w_query, precision=highest))
    keyvalue_raw = low_back(jnp.dot(normed_one, w_keyvalue, precision=highest))
    query_rot = low(rotate(query_raw.reshape(SLOT_LEN, H, HD), cos_table, sin_table))
    key_rot = low(rotate(keyvalue_raw[:, None, :HD], cos_table, sin_table)[:, 0])
    value_all = low(keyvalue_raw[:, HD:])

    def attend(block_start):
        query_block = lax.dynamic_slice_in_dim(query_rot, block_start, QBLOCK, 0)
        scores = jnp.einsum('qhd,kd->hqk', query_block, key_rot, precision=highest) * inv_root
        scores = low_back(scores)
        query_pos = block_start + jnp.arange(QBLOCK, dtype=jnp.int32)
        allowed = (position[None, :] <= query_pos[:, None]) & (position[None, :] < length)
        scores = jnp.where(allowed[None], scores, neg_big)
        attn_probs = low(jax.nn.softmax(scores, axis=-1))
        return jnp.einsum('hqk,kd->qhd', attn_probs, value_all, precision=highest)
    block_starts = jnp.arange(SLOT_LEN // QBLOCK, dtype=jnp.int32) * QBLOCK
    mixed_heads = lax.map(jax.checkpoint(attend), block_starts).reshape(SLOT_LEN, H * HD)
    mixed_heads = low(low_back(mixed_heads))
    after_attn = slot_input + low_back(jnp.dot(mixed_heads, w_project, precision=highest))
    normed_two = low(norm_rows(after_attn, gain_mlp))
    gate_act = low_back(jnp.dot(normed_two, w_gate, precision=highest))
    up_act = low_back(jnp.dot(normed_two, w_up, precision=highest))
    hidden = low(swiglu(gate_act, up_act))
    after_mlp = after_attn + low_back(jnp.dot(hidden, w_down, precision=highest))
    slot_mask = (position < length).astype(jnp.float32)[:, None]
    shared = jnp.concatenate([key_rot, value_all], axis=1) * slot_mask
    return (after_mlp * slot_mask, shared)

def reference(layer_input, lengths, w_query, w_keyvalue, w_project, w_gate, w_up, w_down, gain_attn, gain_mlp, out_grad, kv_grad):
    params = tuple((weight_arg.astype(jnp.float32) for weight_arg in (w_query, w_keyvalue, w_project, w_gate, w_up, w_down, gain_attn, gain_mlp)))
    inputs = layer_input.astype(jnp.float32).reshape(SLOTS, SLOT_LEN, D)
    grads_out = out_grad.astype(jnp.float32).reshape(SLOTS, SLOT_LEN, D)
    grads_kv = kv_grad.astype(jnp.float32).reshape(SLOTS, SLOT_LEN, 2 * HD)

    def one_slot(totals, slot_items):
        slot_input, length, slot_grad, slot_kv_grad = slot_items

        def forward(weights, values):
            return slot_forward(weights, values, length)
        (slot_out, shared_out), pullback = jax.vjp(forward, params, slot_input)
        weight_grads, input_grad = pullback((slot_grad, slot_kv_grad))
        totals = tuple((before + addend for before, addend in zip(totals, weight_grads)))
        return (totals, (slot_out.astype(jnp.bfloat16), input_grad))
    start_totals = tuple((jnp.zeros_like(weight_arg) for weight_arg in params))
    totals, (outputs, input_grads) = lax.scan(one_slot, start_totals, (inputs, lengths, grads_out, grads_kv))
    return (outputs.reshape(TOKENS, D), input_grads.reshape(TOKENS, D), totals[0], totals[1], totals[2], totals[3], totals[4], totals[5], totals[6], totals[7])
```

```python
import functools
import math

import jax
import jax.numpy as jnp
from jax import lax
from jax.experimental import pallas as pl
from jax.experimental.pallas import tpu as pltpu
from jax.sharding import PartitionSpec as P

HD = 128
eps = 1e-05
rope_base = 10000.0
neg_big = -1e30
inv_root = 1.0 / math.sqrt(HD)
f32 = jnp.float32
bf16 = jnp.bfloat16


def dot(a, b, ca, cb):
    return lax.dot_general(a, b, (((ca,), (cb,)), ((), ())), preferred_element_type=f32)


def hop(value, step):
    size = lax.axis_size("tensor")
    return lax.ppermute(value, "tensor", [(i, i ^ step) for i in range(size)])


def after(value, *others):
    return lax.optimization_barrier((value, *others))[0]


def gather_blocks(own):
    return [own] + [hop(own, j) for j in range(1, lax.axis_size("tensor"))]


def scatter_sum(blocks):
    total = blocks[0].astype(f32)
    for j in range(1, len(blocks)):
        total = total + hop(blocks[j].astype(bf16), j).astype(f32)
    return total


def gather_dp(shard):
    return lax.all_gather(shard, "dp", axis=0, tiled=True)


def scatter_dp(partial):
    return lax.psum_scatter(partial, "dp", scatter_dimension=0, tiled=True).astype(f32)


def turn(u, cos2, sin2):
    return u * cos2 + pltpu.roll(u, HD // 2, 1) * sin2


def attend_kernel(where_ref, q_ref, kv_ref, cos_ref, sin_ref, qr_ref, kvt_ref, mixed_ref, lse_ref):
    rows, width = q_ref.shape
    heads = width // HD
    ranks = kv_ref.shape[0] // rows
    j = pl.program_id(0)
    rank, length = where_ref[0], where_ref[1]
    block = jnp.bitwise_xor(rank, j)

    @pl.when(j == 0)
    def _():
        for i in range(ranks):
            here = slice(i * rows, (i + 1) * rows)
            there = pl.ds(pl.multiple_of(jnp.bitwise_xor(rank, i) * rows, rows), rows)
            key = turn(kv_ref[here, :HD], cos_ref[here, :], sin_ref[here, :])
            kvt_ref[there, :HD] = key.astype(bf16)
            kvt_ref[there, HD:] = kv_ref[here, HD:].astype(bf16)

    mine = pl.ds(pl.multiple_of(j * rows, rows), rows)
    cos2, sin2 = cos_ref[mine, :], sin_ref[mine, :]
    for h in range(heads):
        head = slice(h * HD, (h + 1) * HD)
        qr_ref[:, head] = turn(q_ref[:, head], cos2, sin2).astype(bf16)
    limit = jnp.minimum(block * rows + lax.broadcasted_iota(jnp.int32, (rows, 1), 0), length - 1)
    for w in range(ranks):

        @pl.when(block == w)
        def _(w=w):
            span = (w + 1) * rows
            allowed = lax.broadcasted_iota(jnp.int32, (rows, span), 1) <= limit
            for h in range(heads):
                head = slice(h * HD, (h + 1) * HD)
                scores = dot(qr_ref[:, head], kvt_ref[:span, :HD], 1, 1) * inv_root
                scores = jnp.where(allowed, scores, neg_big)
                top = jnp.max(scores, axis=1, keepdims=True)
                weights = jnp.exp(scores - top)
                total = jnp.sum(weights, axis=1, keepdims=True)
                probs = (weights * (1.0 / total)).astype(bf16)
                mixed_ref[:, head] = dot(probs, kvt_ref[:span, HD:], 1, 0).astype(bf16)
                lse_ref[:, h : h + 1] = top + jnp.log(total)


def attend_back_kernel(
    where_ref, qr_ref, kvt_ref, dm_ref, lse_ref, cos_ref, sin_ref, dq_ref, dkv_ref, dk_acc, dv_acc
):
    rows, width = qr_ref.shape
    heads = width // HD
    ranks = kvt_ref.shape[0] // rows
    j = pl.program_id(0)
    rank, length = where_ref[0], where_ref[1]
    block = jnp.bitwise_xor(rank, j)

    @pl.when(j == 0)
    def _():
        dk_acc[...] = jnp.zeros_like(dk_acc)
        dv_acc[...] = jnp.zeros_like(dv_acc)

    cos2, sin2 = cos_ref[...], sin_ref[...]
    limit = jnp.minimum(block * rows + lax.broadcasted_iota(jnp.int32, (rows, 1), 0), length - 1)
    for w in range(ranks):

        @pl.when(block == w)
        def _(w=w):
            span = (w + 1) * rows
            allowed = lax.broadcasted_iota(jnp.int32, (rows, span), 1) <= limit
            keys, vals = kvt_ref[:span, :HD], kvt_ref[:span, HD:]
            for h in range(heads):
                head = slice(h * HD, (h + 1) * HD)
                q, dm = qr_ref[:, head], dm_ref[:, head]
                scores = jnp.where(allowed, dot(q, keys, 1, 1) * inv_root, neg_big)
                probs = jnp.exp(scores - lse_ref[:, h : h + 1])
                dp = dot(dm, vals, 1, 1)
                center = jnp.sum(probs * dp, axis=1, keepdims=True)
                ds = (probs * (dp - center)).astype(bf16)
                dq = dot(ds, keys, 1, 0) * inv_root
                dq_ref[:, head] = turn(dq, cos2, -sin2).astype(bf16)
                dk_acc[:span, :] += dot(ds, q, 0, 0)
                dv_acc[:span, :] += dot(probs.astype(bf16), dm, 0, 0)

    @pl.when(j == ranks - 1)
    def _():
        for i in range(ranks):
            here = slice(i * rows, (i + 1) * rows)
            there = pl.ds(pl.multiple_of(jnp.bitwise_xor(rank, i) * rows, rows), rows)
            dkv_ref[here, :HD] = dk_acc[there, :] * inv_root
            dkv_ref[here, HD:] = dv_acc[there, :]


VMEM_LIMIT = 48 * 2**20


def attend(where, qkv, cos2, sin2, rows):
    slot, width = qkv.shape[0], qkv.shape[1] - 2 * HD
    heads = width // HD
    half = slot * slot * heads * HD
    return pl.pallas_call(
        attend_kernel,
        name="attend",
        grid_spec=pltpu.PrefetchScalarGridSpec(
            num_scalar_prefetch=1,
            grid=(slot // rows,),
            in_specs=[
                pl.BlockSpec((rows, width), lambda j, s: (j, 0)),
                pl.BlockSpec((slot, 2 * HD), lambda j, s: (0, width // (2 * HD))),
                pl.BlockSpec((slot, HD), lambda j, s: (0, 0)),
                pl.BlockSpec((slot, HD), lambda j, s: (0, 0)),
            ],
            out_specs=[
                pl.BlockSpec((rows, width), lambda j, s: (j, 0)),
                pl.BlockSpec((slot, 2 * HD), lambda j, s: (0, 0)),
                pl.BlockSpec((rows, width), lambda j, s: (j, 0)),
                pl.BlockSpec((rows, HD), lambda j, s: (j, 0)),
            ],
        ),
        out_shape=(
            jax.ShapeDtypeStruct((slot, width), bf16),
            jax.ShapeDtypeStruct((slot, 2 * HD), bf16),
            jax.ShapeDtypeStruct((slot, width), bf16),
            jax.ShapeDtypeStruct((slot, HD), f32),
        ),
        compiler_params=pltpu.CompilerParams(
            dimension_semantics=("arbitrary",), vmem_limit_bytes=VMEM_LIMIT
        ),
        cost_estimate=pl.CostEstimate(
            flops=4 * half, bytes_accessed=8 * 2**20, transcendentals=slot * slot * heads
        ),
    )(where, qkv, qkv, cos2, sin2)


def attend_back(where, qr, kvt, dmixed, lse, cos2, sin2, rows):
    slot, width = qr.shape
    heads = width // HD
    half = slot * slot * heads * HD
    return pl.pallas_call(
        attend_back_kernel,
        name="attend_back",
        grid_spec=pltpu.PrefetchScalarGridSpec(
            num_scalar_prefetch=1,
            grid=(slot // rows,),
            in_specs=[
                pl.BlockSpec((rows, width), lambda j, s: (j, 0)),
                pl.BlockSpec((slot, 2 * HD), lambda j, s: (0, 0)),
                pl.BlockSpec((rows, width), lambda j, s: (j, 0)),
                pl.BlockSpec((rows, HD), lambda j, s: (j, 0)),
                pl.BlockSpec((rows, HD), lambda j, s: (j, 0)),
                pl.BlockSpec((rows, HD), lambda j, s: (j, 0)),
            ],
            out_specs=[
                pl.BlockSpec((rows, width), lambda j, s: (j, 0)),
                pl.BlockSpec((slot, 2 * HD), lambda j, s: (0, 0)),
            ],
            scratch_shapes=[pltpu.VMEM((slot, HD), f32), pltpu.VMEM((slot, HD), f32)],
        ),
        out_shape=(
            jax.ShapeDtypeStruct((slot, width), bf16),
            jax.ShapeDtypeStruct((slot, 2 * HD), f32),
        ),
        compiler_params=pltpu.CompilerParams(
            dimension_semantics=("arbitrary",), vmem_limit_bytes=VMEM_LIMIT
        ),
        cost_estimate=pl.CostEstimate(
            flops=10 * half, bytes_accessed=8 * 2**20, transcendentals=slot * slot * heads
        ),
    )(where, qr, kvt, dmixed, lse, cos2, sin2)


def unrotate(values, cosine, sine_vals):
    first, second = values[:, : HD // 2], values[:, HD // 2 :]
    return jnp.concatenate(
        [first * cosine + second * sine_vals, second * cosine - first * sine_vals], axis=1
    )


def inverse_norm(values):
    return lax.rsqrt(jnp.mean(values * values, axis=-1, keepdims=True) + eps)


def rows_of(array, j, rows):
    return array[j * rows : (j + 1) * rows]


def on_device(
    layer_input,
    lengths,
    w_query,
    w_keyvalue,
    w_project,
    w_gate,
    w_up,
    w_down,
    gain_attn,
    gain_mlp,
    out_grad,
    kv_grad,
):
    rows, model_width = layer_input.shape
    ranks = lax.axis_size("tensor")
    rank = lax.axis_index("tensor").astype(jnp.int32)
    length = lengths[0]
    heads_width = w_query.shape[1]
    ff = w_gate.shape[1]
    cut = -(-ff // 256) * 128
    parts = ((0, cut), (cut, ff))

    order = jnp.bitwise_xor(rank, jnp.arange(ranks, dtype=jnp.int32))
    position = (order[:, None] * rows + jnp.arange(rows, dtype=jnp.int32)[None, :]).reshape(-1)
    frequency = rope_base ** (-(jnp.arange(HD // 2, dtype=f32) * 2.0 / HD))
    angles = position.astype(f32)[:, None] * frequency[None, :]
    cosine, sine = jnp.cos(angles), jnp.sin(angles)
    cos2 = jnp.concatenate([cosine, cosine], axis=1)
    sin2 = jnp.concatenate([-sine, sine], axis=1)
    cos_own, sin_own = cosine[:rows], sine[:rows]
    own_mask = (position[:rows] < length).astype(f32)[:, None]
    where = jnp.stack([rank, length])

    attn_shard = jnp.concatenate([w_query, w_keyvalue, w_project.T], axis=1)
    gains = lax.all_gather(jnp.stack([gain_attn, gain_mlp]), "dp", axis=1, tiled=True).astype(f32)
    gain_one, gain_two = gains[0:1], gains[1:2]
    attn_full = gather_dp(attn_shard)
    down_full = gather_dp(after(w_down.T, attn_full))
    pairs, last = [], down_full
    for a, b in parts:
        shard = jnp.concatenate([w_gate[:, a:b], w_up[:, a:b]], axis=1)
        last = gather_dp(after(shard, last))
        pairs.append(last)
    qkv_full = attn_full[:, : heads_width + 2 * HD]
    query_full = attn_full[:, :heads_width]
    keyvalue_full = attn_full[:, heads_width : heads_width + 2 * HD]
    project_full = attn_full[:, heads_width + 2 * HD :]

    residual = layer_input.astype(f32)
    inputs = gather_blocks(layer_input)

    def norm_one(block):
        block = block.astype(f32)
        return (block * inverse_norm(block) * gain_one).astype(bf16)

    normed_one = jnp.concatenate([norm_one(b) for b in inputs], axis=0)
    top = out_grad.astype(f32) * own_mask
    top_all = jnp.concatenate(gather_blocks(after(top.astype(bf16), *inputs)), axis=0)
    qkv = dot(normed_one, qkv_full, 1, 0)
    qr, kvt, mixed, lse = attend(where, qkv, cos2, sin2, rows)
    after_attn = residual + scatter_sum(
        [dot(rows_of(mixed, j, rows), project_full, 1, 1) for j in range(ranks)]
    )

    inv_two = inverse_norm(after_attn)
    normed_two_own = (after_attn * inv_two * gain_two).astype(bf16)
    normed_two = jnp.concatenate(gather_blocks(normed_two_own), axis=0)
    hidden_grad = dot(top_all, down_full, 1, 0)
    hiddens, pair_grads, pair_sums = [], [], []
    for (a, b), pair in zip(parts, pairs):
        both = dot(normed_two, pair, 1, 0)
        gate, up = both[:, : b - a], both[:, b - a :]
        sig = jax.nn.sigmoid(gate)
        grad = hidden_grad[:, a:b]
        hiddens.append((gate * sig * up).astype(bf16))
        gate_grad = (grad * up * sig * (1.0 + gate * (1.0 - sig))).astype(bf16)
        up_grad = (grad * gate * sig).astype(bf16)
        pair_grads.append(jnp.concatenate([gate_grad, up_grad], axis=1))
        pair_sums.append(scatter_dp(dot(normed_two, pair_grads[-1], 0, 0).astype(bf16)))
    hidden = jnp.concatenate(hiddens, axis=1)
    down_sum = scatter_dp(dot(top_all, hidden, 0, 0).astype(bf16))

    normed_two_grad = scatter_sum(
        [
            sum(dot(rows_of(g, j, rows), w, 1, 1) for g, w in zip(pair_grads, pairs))
            for j in range(ranks)
        ]
    )
    unit_two = after_attn * inv_two
    scaled = normed_two_grad * gain_two
    attn_top = top + inv_two * (
        scaled - unit_two * jnp.mean(scaled * unit_two, axis=-1, keepdims=True)
    )
    attn_top_all = jnp.concatenate(gather_blocks(attn_top.astype(bf16)), axis=0)
    after_mlp = after_attn + scatter_sum(
        [dot(rows_of(hidden, j, rows), down_full, 1, 1) for j in range(ranks)]
    )
    output = (after_mlp * own_mask).astype(bf16)

    mixed_grad = dot(attn_top_all, project_full, 1, 0).astype(bf16)
    project_sum = scatter_dp(dot(attn_top_all, mixed, 0, 0).astype(bf16))
    query_grad, kv_part = attend_back(where, qr, kvt, mixed_grad, lse, cos2, sin2, rows)
    shared = kv_part[:rows]
    for j in range(1, ranks):
        shared = shared + hop(rows_of(kv_part, j, rows), j)
    shared = shared + kv_grad.astype(f32) * own_mask
    kv_back = jnp.concatenate([unrotate(shared[:, :HD], cos_own, sin_own), shared[:, HD:]], axis=1)
    kv_back = kv_back.astype(bf16)
    normed_own = normed_one[:rows]
    qkv_grad = jnp.concatenate(
        [
            dot(normed_one, query_grad, 0, 0).astype(bf16),
            dot(normed_own, kv_back, 0, 0).astype(bf16),
        ],
        axis=1,
    )
    qkv_sum = scatter_dp(qkv_grad)
    normed_one_grad = scatter_sum(
        [dot(rows_of(query_grad, j, rows), query_full, 1, 1) for j in range(ranks)]
    ) + dot(kv_back, keyvalue_full, 1, 1)
    inv_one = inverse_norm(residual)
    unit_one = residual * inv_one
    scaled_one = normed_one_grad * gain_one
    input_grad = attn_top + inv_one * (
        scaled_one - unit_one * jnp.mean(scaled_one * unit_one, axis=-1, keepdims=True)
    )

    grad_query, grad_kv_part = qkv_sum[:, :heads_width], qkv_sum[:, heads_width:]
    grad_gate = jnp.concatenate([s[:, : b - a] for (a, b), s in zip(parts, pair_sums)], axis=1)
    grad_up = jnp.concatenate([s[:, b - a :] for (a, b), s in zip(parts, pair_sums)], axis=1)
    gain_one_part = jnp.sum(grad_query * w_query.astype(f32), axis=1) + jnp.sum(
        grad_kv_part * w_keyvalue.astype(f32), axis=1
    )
    gain_two_part = jnp.sum(
        grad_gate * w_gate.astype(f32) + grad_up * w_up.astype(f32), axis=1
    )
    small = jnp.concatenate(
        [grad_kv_part, gain_one_part[:, None], gain_two_part[:, None]], axis=1
    )
    step = 1
    while step < ranks:
        small = small + hop(small, step)
        step *= 2
    grad_keyvalue = small[:, : 2 * HD]
    grad_gain_one = small[:, 2 * HD] / gain_attn.astype(f32)
    grad_gain_two = small[:, 2 * HD + 1] / gain_mlp.astype(f32)
    return (
        output,
        input_grad,
        grad_query,
        grad_keyvalue,
        project_sum.T,
        grad_gate,
        grad_up,
        down_sum.T,
        grad_gain_one,
        grad_gain_two,
    )


def solution(mesh):
    placed = (
        P(("dp", "tensor"), None),
        P("dp"),
        P("dp", "tensor"),
        P("dp", None),
        P("tensor", "dp"),
        P("dp", "tensor"),
        P("dp", "tensor"),
        P("tensor", "dp"),
        P("dp"),
        P("dp"),
        P(("dp", "tensor"), None),
        P(("dp", "tensor"), None),
    )
    return jax.shard_map(
        on_device,
        mesh=mesh,
        in_specs=placed,
        out_specs=(
            P(("dp", "tensor"), None),
            P(("dp", "tensor"), None),
            P("dp", "tensor"),
            P("dp", None),
            P("tensor", "dp"),
            P("dp", "tensor"),
            P("dp", "tensor"),
            P("tensor", "dp"),
            P("dp"),
            P("dp"),
        ),
        check_vma=False,
    )
```

```python
import functools
import math

import jax
import jax.numpy as jnp
from jax import lax
from jax.experimental import pallas as pl
from jax.experimental.pallas import tpu as pltpu
from jax.sharding import PartitionSpec as P

HD = 128
eps = 1e-05
rope_base = 10000.0
neg_big = -1e30
inv_root = 1.0 / math.sqrt(HD)
f32 = jnp.float32
bf16 = jnp.bfloat16


def dot(a, b, ca, cb):
    return lax.dot_general(a, b, (((ca,), (cb,)), ((), ())), preferred_element_type=f32)


def hop(value, step):
    size = lax.axis_size("tensor")
    return lax.ppermute(value, "tensor", [(i, i ^ step) for i in range(size)])


def after(value, *others):
    return lax.optimization_barrier((value, *others))[0]


def gather_blocks(own):
    size = lax.axis_size("tensor")
    if size != 4:
        return [own] + [hop(own, j) for j in range(1, size)]
    half = own.shape[0] // 2
    near, far = hop(own, 1), hop(own, 2)
    upper, lower = hop(far[:half], 1), hop(near[half:], 2)
    return [own, near, far, upper, lower]


def scatter_sum(own, rest):
    size, rows = lax.axis_size("tensor"), own.shape[0]
    if size != 4:
        for j in range(1, size):
            own = own + hop(rows_of(rest, j - 1, rows), j).astype(f32)
        return own
    half = rows // 2
    one, two, three = (rows_of(rest, j, rows) for j in range(3))
    upper = hop(jnp.concatenate([one[:half], three[:half]], axis=0), 1).astype(f32)
    lower = hop(jnp.concatenate([two[half:], three[half:]], axis=0), 2).astype(f32)
    upper_far = hop((two[:half].astype(f32) + upper[half:]).astype(bf16), 2).astype(f32)
    lower_near = hop((one[half:].astype(f32) + lower[half:]).astype(bf16), 1).astype(f32)
    return jnp.concatenate(
        [own[:half] + upper[:half] + upper_far, own[half:] + lower[:half] + lower_near], axis=0
    )


def gather_dp(shard):
    return lax.all_gather(shard, "dp", axis=0, tiled=True)


def scatter_dp(partial):
    return lax.psum_scatter(partial, "dp", scatter_dimension=0, tiled=True).astype(f32)


def turn(u, cos2, sin2):
    return u * cos2 + pltpu.roll(u, HD // 2, 1) * sin2


def attend_kernel(where_ref, q_ref, kv_ref, cos_ref, sin_ref, qr_ref, kvt_ref, mixed_ref, lse_ref):
    rows, width = q_ref.shape
    heads = width // HD
    ranks = kv_ref.shape[0] // rows
    j = pl.program_id(0)
    rank, length = where_ref[0], where_ref[1]
    block = jnp.bitwise_xor(rank, j)

    @pl.when(j == 0)
    def _():
        for i in range(ranks):
            here = slice(i * rows, (i + 1) * rows)
            there = pl.ds(pl.multiple_of(jnp.bitwise_xor(rank, i) * rows, rows), rows)
            key = turn(kv_ref[here, :HD], cos_ref[here, :], sin_ref[here, :])
            kvt_ref[there, :HD] = key.astype(bf16)
            kvt_ref[there, HD:] = kv_ref[here, HD:].astype(bf16)

    mine = pl.ds(pl.multiple_of(j * rows, rows), rows)
    cos2, sin2 = cos_ref[mine, :], sin_ref[mine, :]
    for h in range(heads):
        head = slice(h * HD, (h + 1) * HD)
        qr_ref[:, head] = turn(q_ref[:, head], cos2, sin2).astype(bf16)
    limit = jnp.minimum(block * rows + lax.broadcasted_iota(jnp.int32, (rows, 1), 0), length - 1)
    for w in range(ranks):

        @pl.when(block == w)
        def _(w=w):
            span = (w + 1) * rows
            allowed = lax.broadcasted_iota(jnp.int32, (rows, span), 1) <= limit
            for h in range(heads):
                head = slice(h * HD, (h + 1) * HD)
                scores = dot(qr_ref[:, head], kvt_ref[:span, :HD], 1, 1) * inv_root
                scores = jnp.where(allowed, scores, neg_big)
                top = jnp.max(scores, axis=1, keepdims=True)
                weights = jnp.exp(scores - top)
                total = jnp.sum(weights, axis=1, keepdims=True)
                probs = (weights * (1.0 / total)).astype(bf16)
                mixed_ref[:, head] = dot(probs, kvt_ref[:span, HD:], 1, 0).astype(bf16)
                lse_ref[:, h : h + 1] = top + jnp.log(total)


def attend_back_kernel(
    where_ref,
    qr_ref,
    kvt_ref,
    dm_ref,
    lse_ref,
    cos_ref,
    sin_ref,
    shared_ref,
    dq_ref,
    dkv_ref,
    dk_acc,
    dv_acc,
):
    rows, width = qr_ref.shape
    heads = width // HD
    ranks = kvt_ref.shape[0] // rows
    j = pl.program_id(0)
    rank, length = where_ref[0], where_ref[1]
    block = jnp.bitwise_xor(rank, j)

    @pl.when(j == 0)
    def _():
        dk_acc[...] = jnp.zeros_like(dk_acc)
        dv_acc[...] = jnp.zeros_like(dv_acc)

    mine = pl.ds(pl.multiple_of(j * rows, rows), rows)
    cos2, sin2 = cos_ref[mine, :], sin_ref[mine, :]
    limit = jnp.minimum(block * rows + lax.broadcasted_iota(jnp.int32, (rows, 1), 0), length - 1)
    for w in range(ranks):

        @pl.when(block == w)
        def _(w=w):
            span = (w + 1) * rows
            allowed = lax.broadcasted_iota(jnp.int32, (rows, span), 1) <= limit
            keys, vals = kvt_ref[:span, :HD], kvt_ref[:span, HD:]
            for h in range(heads):
                head = slice(h * HD, (h + 1) * HD)
                q, dm = qr_ref[:, head], dm_ref[:, head]
                scores = jnp.where(allowed, dot(q, keys, 1, 1) * inv_root, neg_big)
                probs = jnp.exp(scores - lse_ref[:, h : h + 1])
                dp = dot(dm, vals, 1, 1)
                center = jnp.sum(probs * dp, axis=1, keepdims=True)
                ds = (probs * (dp - center)).astype(bf16)
                dq = dot(ds, keys, 1, 0) * inv_root
                dq_ref[:, head] = turn(dq, cos2, -sin2).astype(bf16)
                dk_acc[:span, :] += dot(ds, q, 0, 0)
                dv_acc[:span, :] += dot(probs.astype(bf16), dm, 0, 0)

    @pl.when(j == ranks - 1)
    def _():
        for i in range(ranks):
            here = slice(i * rows, (i + 1) * rows)
            there = pl.ds(pl.multiple_of(jnp.bitwise_xor(rank, i) * rows, rows), rows)
            dk, dv = dk_acc[there, :] * inv_root, dv_acc[there, :]
            if i == 0:
                dk, dv = dk + shared_ref[:, :HD], dv + shared_ref[:, HD:]
            dkv_ref[here, :HD] = turn(dk, cos_ref[here, :], -sin_ref[here, :]).astype(bf16)
            dkv_ref[here, HD:] = dv.astype(bf16)


VMEM_LIMIT = 48 * 2**20


def attend(where, qkv, cos2, sin2, rows):
    slot, width = qkv.shape[0], qkv.shape[1] - 2 * HD
    heads = width // HD
    half = slot * slot * heads * HD
    return pl.pallas_call(
        attend_kernel,
        name="attend",
        grid_spec=pltpu.PrefetchScalarGridSpec(
            num_scalar_prefetch=1,
            grid=(slot // rows,),
            in_specs=[
                pl.BlockSpec((rows, width), lambda j, s: (j, 0)),
                pl.BlockSpec((slot, 2 * HD), lambda j, s: (0, width // (2 * HD))),
                pl.BlockSpec((slot, HD), lambda j, s: (0, 0)),
                pl.BlockSpec((slot, HD), lambda j, s: (0, 0)),
            ],
            out_specs=[
                pl.BlockSpec((rows, width), lambda j, s: (j, 0)),
                pl.BlockSpec((slot, 2 * HD), lambda j, s: (0, 0)),
                pl.BlockSpec((rows, width), lambda j, s: (j, 0)),
                pl.BlockSpec((rows, HD), lambda j, s: (j, 0)),
            ],
        ),
        out_shape=(
            jax.ShapeDtypeStruct((slot, width), bf16),
            jax.ShapeDtypeStruct((slot, 2 * HD), bf16),
            jax.ShapeDtypeStruct((slot, width), bf16),
            jax.ShapeDtypeStruct((slot, HD), f32),
        ),
        compiler_params=pltpu.CompilerParams(
            dimension_semantics=("arbitrary",), vmem_limit_bytes=VMEM_LIMIT
        ),
        cost_estimate=pl.CostEstimate(
            flops=4 * half, bytes_accessed=8 * 2**20, transcendentals=slot * slot * heads
        ),
    )(where, qkv, qkv, cos2, sin2)


def attend_back(where, qr, kvt, dmixed, lse, cos2, sin2, shared, rows):
    slot, width = qr.shape
    heads = width // HD
    half = slot * slot * heads * HD
    return pl.pallas_call(
        attend_back_kernel,
        name="attend_back",
        grid_spec=pltpu.PrefetchScalarGridSpec(
            num_scalar_prefetch=1,
            grid=(slot // rows,),
            in_specs=[
                pl.BlockSpec((rows, width), lambda j, s: (j, 0)),
                pl.BlockSpec((slot, 2 * HD), lambda j, s: (0, 0)),
                pl.BlockSpec((rows, width), lambda j, s: (j, 0)),
                pl.BlockSpec((rows, HD), lambda j, s: (j, 0)),
                pl.BlockSpec((slot, HD), lambda j, s: (0, 0)),
                pl.BlockSpec((slot, HD), lambda j, s: (0, 0)),
                pl.BlockSpec((rows, 2 * HD), lambda j, s: (0, 0)),
            ],
            out_specs=[
                pl.BlockSpec((rows, width), lambda j, s: (j, 0)),
                pl.BlockSpec((slot, 2 * HD), lambda j, s: (0, 0)),
            ],
            scratch_shapes=[pltpu.VMEM((slot, HD), f32), pltpu.VMEM((slot, HD), f32)],
        ),
        out_shape=(
            jax.ShapeDtypeStruct((slot, width), bf16),
            jax.ShapeDtypeStruct((slot, 2 * HD), bf16),
        ),
        compiler_params=pltpu.CompilerParams(
            dimension_semantics=("arbitrary",), vmem_limit_bytes=VMEM_LIMIT
        ),
        cost_estimate=pl.CostEstimate(
            flops=10 * half, bytes_accessed=8 * 2**20, transcendentals=slot * slot * heads
        ),
    )(where, qr, kvt, dmixed, lse, cos2, sin2, shared)


def inverse_norm(values):
    return lax.rsqrt(jnp.mean(values * values, axis=-1, keepdims=True) + eps)


def rows_of(array, j, rows):
    return array[j * rows : (j + 1) * rows]


def on_device(
    layer_input,
    lengths,
    w_query,
    w_keyvalue,
    w_project,
    w_gate,
    w_up,
    w_down,
    gain_attn,
    gain_mlp,
    out_grad,
    kv_grad,
):
    rows, model_width = layer_input.shape
    ranks = lax.axis_size("tensor")
    rank = lax.axis_index("tensor").astype(jnp.int32)
    length = lengths[0]
    heads_width = w_query.shape[1]
    ff = w_gate.shape[1]
    cut = -(-ff // 256) * 128
    parts = ((0, cut), (cut, ff))

    order = jnp.bitwise_xor(rank, jnp.arange(ranks, dtype=jnp.int32))
    position = (order[:, None] * rows + jnp.arange(rows, dtype=jnp.int32)[None, :]).reshape(-1)
    frequency = rope_base ** (-(jnp.arange(HD // 2, dtype=f32) * 2.0 / HD))
    angles = position.astype(f32)[:, None] * frequency[None, :]
    cosine, sine = jnp.cos(angles), jnp.sin(angles)
    cos2 = jnp.concatenate([cosine, cosine], axis=1)
    sin2 = jnp.concatenate([-sine, sine], axis=1)
    own_mask = (position[:rows] < length).astype(f32)[:, None]
    where = jnp.stack([rank, length])

    gain_one, gain_two = gain_attn.astype(f32)[:, None], gain_mlp.astype(f32)[:, None]
    qkv_own = jnp.concatenate([w_query, w_keyvalue], axis=1).astype(f32)
    qkv_width = qkv_own.shape[1]
    attn_shard = jnp.concatenate([(qkv_own * gain_one).astype(bf16), w_project.T], axis=1)
    pair_own = [
        jnp.concatenate([w_gate[:, a:b], w_up[:, a:b]], axis=1).astype(f32) for a, b in parts
    ]
    pair_shards = [(own * gain_two).astype(bf16) for own in pair_own]

    residual = layer_input.astype(f32)
    inputs = gather_blocks(layer_input)
    attn_full = gather_dp(attn_shard)
    down_full = gather_dp(after(w_down.T, *inputs))
    qkv_full, project_full = attn_full[:, :qkv_width], attn_full[:, qkv_width:]
    top = out_grad.astype(f32) * own_mask
    top_blocks = gather_blocks(after(top.astype(bf16), *inputs))
    pairs = [gather_dp(after(pair_shards[0], *top_blocks))]

    def norm(block):
        block = block.astype(f32)
        return (block * inverse_norm(block)).astype(bf16)

    normed_one = jnp.concatenate([norm(b) for b in inputs], axis=0)
    qkv = dot(normed_one, qkv_full, 1, 0)
    qr, kvt, mixed, lse = attend(where, qkv, cos2, sin2, rows)
    top_all = jnp.concatenate(top_blocks, axis=0)
    mixed_sent = after(mixed, top_all)
    after_attn = residual + scatter_sum(
        dot(mixed[:rows], project_full, 1, 1),
        dot(mixed_sent[rows:], project_full, 1, 1).astype(bf16),
    )

    inv_two = inverse_norm(after_attn)
    unit_two = after_attn * inv_two
    normed_blocks = gather_blocks(unit_two.astype(bf16))
    pairs.append(gather_dp(after(pair_shards[1], *normed_blocks)))
    normed_two = jnp.concatenate(normed_blocks, axis=0)
    hidden_grad = dot(top_all, down_full, 1, 0)
    hiddens, pair_grads, pair_sums = [], [], []
    for (a, b), pair in zip(parts, pairs):
        both = dot(normed_two, pair, 1, 0)
        gate, up = both[:, : b - a], both[:, b - a :]
        sig = jax.nn.sigmoid(gate)
        grad = hidden_grad[:, a:b]
        hiddens.append((gate * sig * up).astype(bf16))
        gate_grad = (grad * up * sig * (1.0 + gate * (1.0 - sig))).astype(bf16)
        up_grad = (grad * gate * sig).astype(bf16)
        pair_grads.append(jnp.concatenate([gate_grad, up_grad], axis=1))
        pair_sums.append(scatter_dp(dot(normed_two, pair_grads[-1], 0, 0).astype(bf16)))
    hidden = jnp.concatenate(hiddens, axis=1)

    scaled = scatter_sum(
        sum(dot(g[:rows], w, 1, 1) for g, w in zip(pair_grads, pairs)),
        sum(dot(g[rows:], w, 1, 1) for g, w in zip(pair_grads, pairs)).astype(bf16),
    )
    attn_top = top + inv_two * (
        scaled - unit_two * jnp.mean(scaled * unit_two, axis=-1, keepdims=True)
    )
    attn_top_blocks = gather_blocks(attn_top.astype(bf16))
    attn_top_all = jnp.concatenate(attn_top_blocks, axis=0)
    down_sum = scatter_dp(dot(top_all, hidden, 0, 0).astype(bf16))
    down_rest = dot(hidden[rows:], down_full, 1, 1).astype(bf16)
    after_mlp = after_attn + scatter_sum(
        dot(hidden[:rows], down_full, 1, 1), after(down_rest, *attn_top_blocks)
    )
    output = (after_mlp * own_mask).astype(bf16)

    mixed_grad = dot(attn_top_all, project_full, 1, 0).astype(bf16)
    shared = kv_grad.astype(f32) * own_mask
    query_grad, kv_back = attend_back(where, qr, kvt, mixed_grad, lse, cos2, sin2, shared, rows)
    qkv_back = jnp.concatenate([query_grad, kv_back], axis=1)
    attn_grad = jnp.concatenate(
        [
            dot(normed_one, qkv_back, 0, 0).astype(bf16),
            dot(attn_top_all, mixed, 0, 0).astype(bf16),
        ],
        axis=1,
    )
    attn_sum = scatter_dp(attn_grad)
    qkv_sum, project_sum = attn_sum[:, :qkv_width], attn_sum[:, qkv_width:]
    scaled_one = scatter_sum(
        dot(qkv_back[:rows], qkv_full, 1, 1), dot(qkv_back[rows:], qkv_full, 1, 1).astype(bf16)
    )
    inv_one = inverse_norm(residual)
    unit_one = residual * inv_one
    input_grad = attn_top + inv_one * (
        scaled_one - unit_one * jnp.mean(scaled_one * unit_one, axis=-1, keepdims=True)
    )

    gain_two_part = sum(
        jnp.sum(own * total, axis=1, keepdims=True) for own, total in zip(pair_own, pair_sums)
    )
    scaled_sums = [total * gain_two for total in pair_sums]
    grad_gate = jnp.concatenate([s[:, : b - a] for (a, b), s in zip(parts, scaled_sums)], axis=1)
    grad_up = jnp.concatenate([s[:, b - a :] for (a, b), s in zip(parts, scaled_sums)], axis=1)
    gain_one_part = jnp.sum(
        qkv_own[:, :heads_width] * qkv_sum[:, :heads_width], axis=1, keepdims=True
    ) + jnp.sum(qkv_own[:, heads_width:] * qkv_sum[:, heads_width:], axis=1, keepdims=True)
    small = jnp.concatenate(
        [qkv_sum[:, heads_width:] * gain_one, gain_one_part, gain_two_part], axis=1
    )
    step = 1
    while step < ranks:
        small = small + hop(small, step)
        step *= 2
    return (
        output,
        input_grad,
        qkv_sum[:, :heads_width] * gain_one,
        small[:, : 2 * HD],
        project_sum.T,
        grad_gate,
        grad_up,
        down_sum.T,
        small[:, 2 * HD],
        small[:, 2 * HD + 1],
    )


def solution(mesh):
    placed = (
        P(("dp", "tensor"), None),
        P("dp"),
        P("dp", "tensor"),
        P("dp", None),
        P("tensor", "dp"),
        P("dp", "tensor"),
        P("dp", "tensor"),
        P("tensor", "dp"),
        P("dp"),
        P("dp"),
        P(("dp", "tensor"), None),
        P(("dp", "tensor"), None),
    )
    return jax.shard_map(
        on_device,
        mesh=mesh,
        in_specs=placed,
        out_specs=(
            P(("dp", "tensor"), None),
            P(("dp", "tensor"), None),
            P("dp", "tensor"),
            P("dp", None),
            P("tensor", "dp"),
            P("dp", "tensor"),
            P("dp", "tensor"),
            P("tensor", "dp"),
            P("dp"),
            P("dp"),
        ),
        check_vma=False,
    )
```

```python
import functools
import math

import jax
import jax.numpy as jnp
from jax import lax
from jax.experimental import pallas as pl
from jax.experimental.pallas import tpu as pltpu
from jax.sharding import PartitionSpec as P

HD = 128
eps = 1e-05
rope_base = 10000.0
neg_big = -1e30
inv_root = 1.0 / math.sqrt(HD)
f32 = jnp.float32
bf16 = jnp.bfloat16


def dot(a, b, ca, cb):
    return lax.dot_general(a, b, (((ca,), (cb,)), ((), ())), preferred_element_type=f32)


def hop(value, step):
    size = lax.axis_size("tensor")
    return lax.ppermute(value, "tensor", [(i, i ^ step) for i in range(size)])


def after(value, *others):
    return lax.optimization_barrier((value, *others))[0]


def near_blocks(own):
    size = lax.axis_size("tensor")
    return [hop(own, j) for j in range(1, 3 if size == 4 else size)]


def all_blocks(own, near):
    if lax.axis_size("tensor") != 4:
        return [own, *near]
    half = own.shape[0] // 2
    one, two = near
    return [own, one, two, hop(two[:half], 1), hop(one[half:], 2)]


def send_sums(rest):
    size = lax.axis_size("tensor")
    rows = rest.shape[0] // (size - 1)
    one, *others = (rows_of(rest, j, rows) for j in range(size - 1))
    if size != 4:
        return [hop(block, j + 1) for j, block in enumerate([one, *others])]
    two, three = others
    half = rows // 2
    return [
        hop(jnp.concatenate([one[:half], three[:half]], axis=0), 1),
        hop(jnp.concatenate([two[half:], three[half:]], axis=0), 2),
    ]


def finish_sums(own, rest, arrived):
    arrived = [block.astype(f32) for block in arrived]
    if lax.axis_size("tensor") != 4:
        return own + sum(arrived)
    rows = own.shape[0]
    half = rows // 2
    one, two = rows_of(rest, 0, rows), rows_of(rest, 1, rows)
    upper, lower = arrived
    upper_far = hop((two[:half].astype(f32) + upper[half:]).astype(bf16), 2).astype(f32)
    lower_near = hop((one[half:].astype(f32) + lower[half:]).astype(bf16), 1).astype(f32)
    return jnp.concatenate(
        [own[:half] + upper[:half] + upper_far, own[half:] + lower[:half] + lower_near], axis=0
    )


def gather_dp(shard):
    return lax.all_gather(shard, "dp", axis=0, tiled=True)


def scatter_dp(partial):
    return lax.psum_scatter(partial, "dp", scatter_dimension=0, tiled=True).astype(f32)


def lines_of():
    size = lax.axis_size("dp")
    index = lax.axis_index("dp").astype(jnp.int32)
    return size // 2, index // 2, index % 2


def swap_cores(value):
    return lax.ppermute(value, "dp", [(i, i ^ 1) for i in range(lax.axis_size("dp"))])


def shift_lines(value, step):
    size = lax.axis_size("dp")
    return lax.ppermute(value, "dp", [(i, (i + 2 * step) % size) for i in range(size)])


def send_lines(shard):
    return [shard] + [shift_lines(shard, step) for step in range(1, lines_of()[0])]


def join_lines(pieces, *ready):
    lines, line, core = lines_of()
    rows = pieces[0].shape[0]
    whole = jnp.zeros((2 * lines * rows, pieces[0].shape[1]), pieces[0].dtype)
    for step, piece in enumerate(pieces):
        base = 2 * ((line - step) % lines)
        other = swap_cores(after(piece, *ready) if ready else piece)
        whole = lax.dynamic_update_slice(whole, piece, ((base + core) * rows, 0))
        whole = lax.dynamic_update_slice(whole, other, ((base + 1 - core) * rows, 0))
    return whole


pick = functools.partial(lax.dynamic_index_in_dim, keepdims=False)


def sum_cores(partial, *ready):
    lines, _, core = lines_of()
    blocks = partial.reshape(lines, 2, -1, partial.shape[1])
    other = after(swap_cores(pick(blocks, 1 - core, 1)), *ready)
    return pick(blocks, core, 1).astype(f32) + other.astype(f32)


def sum_lines(chip, *ready):
    lines, line, _ = lines_of()
    total, sent = pick(chip, line, 0), chip.astype(bf16)
    for step in range(1, lines):
        arrived = shift_lines(pick(sent, (line + step) % lines, 0), step)
        total = total + after(arrived, *ready).astype(f32)
    return total


def turn(u, cos2, sin2):
    return u * cos2 + pltpu.roll(u, HD // 2, 1) * sin2


def attend_kernel(where_ref, q_ref, kv_ref, cos_ref, sin_ref, qr_ref, kvt_ref, mixed_ref, lse_ref):
    rows, width = q_ref.shape
    heads = width // HD
    ranks = kv_ref.shape[0] // rows
    j = pl.program_id(0)
    rank, length = where_ref[0], where_ref[1]
    block = jnp.bitwise_xor(rank, j)

    @pl.when(j == 0)
    def _():
        for i in range(ranks):
            here = slice(i * rows, (i + 1) * rows)
            there = pl.ds(pl.multiple_of(jnp.bitwise_xor(rank, i) * rows, rows), rows)
            key = turn(kv_ref[here, :HD], cos_ref[here, :], sin_ref[here, :])
            kvt_ref[there, :HD] = key.astype(bf16)
            kvt_ref[there, HD:] = kv_ref[here, HD:].astype(bf16)

    mine = pl.ds(pl.multiple_of(j * rows, rows), rows)
    cos2, sin2 = cos_ref[mine, :], sin_ref[mine, :]
    for h in range(heads):
        head = slice(h * HD, (h + 1) * HD)
        qr_ref[:, head] = turn(q_ref[:, head], cos2, sin2).astype(bf16)
    limit = jnp.minimum(block * rows + lax.broadcasted_iota(jnp.int32, (rows, 1), 0), length - 1)
    for w in range(ranks):

        @pl.when(block == w)
        def _(w=w):
            span = (w + 1) * rows
            allowed = lax.broadcasted_iota(jnp.int32, (rows, span), 1) <= limit
            for h in range(heads):
                head = slice(h * HD, (h + 1) * HD)
                scores = dot(qr_ref[:, head], kvt_ref[:span, :HD], 1, 1) * inv_root
                scores = jnp.where(allowed, scores, neg_big)
                top = jnp.max(scores, axis=1, keepdims=True)
                weights = jnp.exp(scores - top)
                total = jnp.sum(weights, axis=1, keepdims=True)
                probs = (weights * (1.0 / total)).astype(bf16)
                mixed_ref[:, head] = dot(probs, kvt_ref[:span, HD:], 1, 0).astype(bf16)
                lse_ref[:, h : h + 1] = top + jnp.log(total)


def attend_back_kernel(
    where_ref,
    qr_ref,
    kvt_ref,
    dm_ref,
    lse_ref,
    cos_ref,
    sin_ref,
    shared_ref,
    dq_ref,
    dkv_ref,
    dk_acc,
    dv_acc,
):
    rows, width = qr_ref.shape
    heads = width // HD
    ranks = kvt_ref.shape[0] // rows
    j = pl.program_id(0)
    rank, length = where_ref[0], where_ref[1]
    block = jnp.bitwise_xor(rank, j)

    @pl.when(j == 0)
    def _():
        dk_acc[...] = jnp.zeros_like(dk_acc)
        dv_acc[...] = jnp.zeros_like(dv_acc)

    mine = pl.ds(pl.multiple_of(j * rows, rows), rows)
    cos2, sin2 = cos_ref[mine, :], sin_ref[mine, :]
    limit = jnp.minimum(block * rows + lax.broadcasted_iota(jnp.int32, (rows, 1), 0), length - 1)
    for w in range(ranks):

        @pl.when(block == w)
        def _(w=w):
            span = (w + 1) * rows
            allowed = lax.broadcasted_iota(jnp.int32, (rows, span), 1) <= limit
            keys, vals = kvt_ref[:span, :HD], kvt_ref[:span, HD:]
            for h in range(heads):
                head = slice(h * HD, (h + 1) * HD)
                q, dm = qr_ref[:, head], dm_ref[:, head]
                scores = jnp.where(allowed, dot(q, keys, 1, 1) * inv_root, neg_big)
                probs = jnp.exp(scores - lse_ref[:, h : h + 1])
                dp = dot(dm, vals, 1, 1)
                center = jnp.sum(probs * dp, axis=1, keepdims=True)
                ds = (probs * (dp - center)).astype(bf16)
                dq = dot(ds, keys, 1, 0) * inv_root
                dq_ref[:, head] = turn(dq, cos2, -sin2).astype(bf16)
                dk_acc[:span, :] += dot(ds, q, 0, 0)
                dv_acc[:span, :] += dot(probs.astype(bf16), dm, 0, 0)

    @pl.when(j == ranks - 1)
    def _():
        for i in range(ranks):
            here = slice(i * rows, (i + 1) * rows)
            there = pl.ds(pl.multiple_of(jnp.bitwise_xor(rank, i) * rows, rows), rows)
            dk, dv = dk_acc[there, :] * inv_root, dv_acc[there, :]
            if i == 0:
                dk, dv = dk + shared_ref[:, :HD], dv + shared_ref[:, HD:]
            dkv_ref[here, :HD] = turn(dk, cos_ref[here, :], -sin_ref[here, :]).astype(bf16)
            dkv_ref[here, HD:] = dv.astype(bf16)


VMEM_LIMIT = 48 * 2**20


def attend(where, qkv, cos2, sin2, rows):
    slot, width = qkv.shape[0], qkv.shape[1] - 2 * HD
    heads = width // HD
    half = slot * slot * heads * HD
    return pl.pallas_call(
        attend_kernel,
        name="attend",
        grid_spec=pltpu.PrefetchScalarGridSpec(
            num_scalar_prefetch=1,
            grid=(slot // rows,),
            in_specs=[
                pl.BlockSpec((rows, width), lambda j, s: (j, 0)),
                pl.BlockSpec((slot, 2 * HD), lambda j, s: (0, width // (2 * HD))),
                pl.BlockSpec((slot, HD), lambda j, s: (0, 0)),
                pl.BlockSpec((slot, HD), lambda j, s: (0, 0)),
            ],
            out_specs=[
                pl.BlockSpec((rows, width), lambda j, s: (j, 0)),
                pl.BlockSpec((slot, 2 * HD), lambda j, s: (0, 0)),
                pl.BlockSpec((rows, width), lambda j, s: (j, 0)),
                pl.BlockSpec((rows, HD), lambda j, s: (j, 0)),
            ],
        ),
        out_shape=(
            jax.ShapeDtypeStruct((slot, width), bf16),
            jax.ShapeDtypeStruct((slot, 2 * HD), bf16),
            jax.ShapeDtypeStruct((slot, width), bf16),
            jax.ShapeDtypeStruct((slot, HD), f32),
        ),
        compiler_params=pltpu.CompilerParams(
            dimension_semantics=("arbitrary",), vmem_limit_bytes=VMEM_LIMIT
        ),
        cost_estimate=pl.CostEstimate(
            flops=4 * half, bytes_accessed=8 * 2**20, transcendentals=slot * slot * heads
        ),
    )(where, qkv, qkv, cos2, sin2)


def attend_back(where, qr, kvt, dmixed, lse, cos2, sin2, shared, rows):
    slot, width = qr.shape
    heads = width // HD
    half = slot * slot * heads * HD
    return pl.pallas_call(
        attend_back_kernel,
        name="attend_back",
        grid_spec=pltpu.PrefetchScalarGridSpec(
            num_scalar_prefetch=1,
            grid=(slot // rows,),
            in_specs=[
                pl.BlockSpec((rows, width), lambda j, s: (j, 0)),
                pl.BlockSpec((slot, 2 * HD), lambda j, s: (0, 0)),
                pl.BlockSpec((rows, width), lambda j, s: (j, 0)),
                pl.BlockSpec((rows, HD), lambda j, s: (j, 0)),
                pl.BlockSpec((slot, HD), lambda j, s: (0, 0)),
                pl.BlockSpec((slot, HD), lambda j, s: (0, 0)),
                pl.BlockSpec((rows, 2 * HD), lambda j, s: (0, 0)),
            ],
            out_specs=[
                pl.BlockSpec((rows, width), lambda j, s: (j, 0)),
                pl.BlockSpec((slot, 2 * HD), lambda j, s: (0, 0)),
            ],
            scratch_shapes=[pltpu.VMEM((slot, HD), f32), pltpu.VMEM((slot, HD), f32)],
        ),
        out_shape=(
            jax.ShapeDtypeStruct((slot, width), bf16),
            jax.ShapeDtypeStruct((slot, 2 * HD), bf16),
        ),
        compiler_params=pltpu.CompilerParams(
            dimension_semantics=("arbitrary",), vmem_limit_bytes=VMEM_LIMIT
        ),
        cost_estimate=pl.CostEstimate(
            flops=10 * half, bytes_accessed=8 * 2**20, transcendentals=slot * slot * heads
        ),
    )(where, qr, kvt, dmixed, lse, cos2, sin2, shared)


def inverse_norm(values):
    return lax.rsqrt(jnp.mean(values * values, axis=-1, keepdims=True) + eps)


def rows_of(array, j, rows):
    return array[j * rows : (j + 1) * rows]


def on_device(
    layer_input,
    lengths,
    w_query,
    w_keyvalue,
    w_project,
    w_gate,
    w_up,
    w_down,
    gain_attn,
    gain_mlp,
    out_grad,
    kv_grad,
):
    rows, model_width = layer_input.shape
    ranks = lax.axis_size("tensor")
    rank = lax.axis_index("tensor").astype(jnp.int32)
    length = lengths[0]
    heads_width = w_query.shape[1]
    ff = w_gate.shape[1]
    cut = -(-ff // 256) * 128
    parts = ((0, cut), (cut, ff))

    order = jnp.bitwise_xor(rank, jnp.arange(ranks, dtype=jnp.int32))
    position = (order[:, None] * rows + jnp.arange(rows, dtype=jnp.int32)[None, :]).reshape(-1)
    frequency = rope_base ** (-(jnp.arange(HD // 2, dtype=f32) * 2.0 / HD))
    angles = position.astype(f32)[:, None] * frequency[None, :]
    cosine, sine = jnp.cos(angles), jnp.sin(angles)
    cos2 = jnp.concatenate([cosine, cosine], axis=1)
    sin2 = jnp.concatenate([-sine, sine], axis=1)
    own_mask = (position[:rows] < length).astype(f32)[:, None]
    where = jnp.stack([rank, length])

    gain_one, gain_two = gain_attn.astype(f32)[:, None], gain_mlp.astype(f32)[:, None]
    qkv_own = jnp.concatenate([w_query, w_keyvalue], axis=1).astype(f32)
    qkv_width = qkv_own.shape[1]
    pair_own = [
        jnp.concatenate([w_gate[:, a:b], w_up[:, a:b]], axis=1).astype(f32) for a, b in parts
    ]
    pair_shards = [(own * gain_two).astype(bf16) for own in pair_own]

    residual = layer_input.astype(f32)
    inputs = all_blocks(layer_input, near_blocks(layer_input))
    qkv_full = gather_dp((qkv_own * gain_one).astype(bf16))
    project_full = join_lines(send_lines(w_project.T))
    pairs = [gather_dp(after(pair_shards[0], *inputs))]
    down_pieces = send_lines(after(w_down.T, *inputs))
    top = out_grad.astype(f32) * own_mask
    top_own = after(top.astype(bf16), *inputs)
    top_near = near_blocks(top_own)

    def norm(block):
        block = block.astype(f32)
        return (block * inverse_norm(block)).astype(bf16)

    normed_one = jnp.concatenate([norm(b) for b in inputs], axis=0)
    qkv = dot(after(normed_one, project_full), qkv_full, 1, 0)
    qr, kvt, mixed, lse = attend(where, qkv, cos2, sin2, rows)
    pairs.append(gather_dp(after(pair_shards[1], mixed)))
    mixed_rest = dot(after(mixed[rows:], *top_near), project_full, 1, 1).astype(bf16)
    mixed_sent = send_sums(mixed_rest)
    top_all = jnp.concatenate(all_blocks(top_own, top_near), axis=0)
    down_full = join_lines(down_pieces, *mixed_sent)
    after_attn = residual + finish_sums(
        dot(mixed[:rows], project_full, 1, 1), mixed_rest, mixed_sent
    )

    inv_two = inverse_norm(after_attn)
    unit_two = after_attn * inv_two
    normed_own = after(unit_two.astype(bf16), top_all)
    grads = [dot(top_all, down_full[:, a:b], 1, 0) for a, b in parts]
    normed_two = jnp.concatenate(all_blocks(normed_own, near_blocks(normed_own)), axis=0)
    normed = after(normed_two, *grads)
    hiddens, pair_grads, pair_partials = [], [], []
    for (a, b), pair, grad in zip(parts, pairs, grads):
        both = dot(normed, pair, 1, 0)
        gate, up = both[:, : b - a], both[:, b - a :]
        sig = jax.nn.sigmoid(gate)
        hiddens.append((gate * sig * up).astype(bf16))
        gate_grad = (grad * up * sig * (1.0 + gate * (1.0 - sig))).astype(bf16)
        up_grad = (grad * gate * sig).astype(bf16)
        pair_grads.append(jnp.concatenate([gate_grad, up_grad], axis=1))
        if len(hiddens) == 1:
            pair_partials.append(dot(normed_two, pair_grads[0], 0, 0).astype(bf16))
            normed = after(normed_two, pair_partials[0])
    hidden = jnp.concatenate(hiddens, axis=1)

    rest = sum(dot(g[rows:], w, 1, 1) for g, w in zip(pair_grads, pairs)).astype(bf16)
    rest_sent = send_sums(rest)
    pair_partials.append(dot(normed_two, after(pair_grads[1], rest), 0, 0).astype(bf16))
    pair_sums = [scatter_dp(partial) for partial in pair_partials]
    own_grads = [g[:rows] for g in pair_grads]
    own_grads[0] = after(own_grads[0], pair_partials[1])
    scaled = finish_sums(sum(dot(g, w, 1, 1) for g, w in zip(own_grads, pairs)), rest, rest_sent)
    attn_top = top + inv_two * (
        scaled - unit_two * jnp.mean(scaled * unit_two, axis=-1, keepdims=True)
    )
    attn_top_own = attn_top.astype(bf16)
    attn_top_blocks = all_blocks(attn_top_own, near_blocks(attn_top_own))
    attn_top_all = jnp.concatenate(attn_top_blocks, axis=0)
    down_chip = sum_cores(dot(top_all, hidden, 0, 0).astype(bf16))
    down_rest = after(dot(hidden[rows:], down_full, 1, 1).astype(bf16), *attn_top_blocks)

    mixed_grad = dot(after(attn_top_all, down_chip, pair_sums[0]), project_full, 1, 0).astype(bf16)
    project_partial = dot(attn_top_all, mixed, 0, 0).astype(bf16)
    shared = kv_grad.astype(f32) * own_mask
    query_grad, kv_back = attend_back(
        where, qr, kvt, after(mixed_grad, project_partial), lse, cos2, sin2, shared, rows
    )
    down_sum = sum_lines(down_chip, query_grad)
    project_chip = sum_cores(project_partial, query_grad)
    project_sum = sum_lines(project_chip)
    down_sent = [after(block, query_grad) for block in send_sums(down_rest)]
    after_mlp = after_attn + finish_sums(
        dot(hidden[:rows], down_full, 1, 1), down_rest, down_sent
    )
    output = (after_mlp * own_mask).astype(bf16)
    qkv_back = after(jnp.concatenate([query_grad, kv_back], axis=1), project_chip)
    qkv_partial = dot(normed_one, qkv_back, 0, 0).astype(bf16)
    qkv_sum = scatter_dp(after(qkv_partial, *pair_sums, down_sum))
    qkv_rest = dot(after(qkv_back[rows:], qkv_partial, *down_sent), qkv_full, 1, 1).astype(bf16)
    scaled_one = finish_sums(
        dot(qkv_back[:rows], qkv_full, 1, 1), qkv_rest, send_sums(qkv_rest)
    )
    inv_one = inverse_norm(residual)
    unit_one = residual * inv_one
    input_grad = attn_top + inv_one * (
        scaled_one - unit_one * jnp.mean(scaled_one * unit_one, axis=-1, keepdims=True)
    )

    gain_two_part = sum(
        jnp.sum(own * total, axis=1, keepdims=True) for own, total in zip(pair_own, pair_sums)
    )
    scaled_sums = [total * gain_two for total in pair_sums]
    grad_gate = jnp.concatenate([s[:, : b - a] for (a, b), s in zip(parts, scaled_sums)], axis=1)
    grad_up = jnp.concatenate([s[:, b - a :] for (a, b), s in zip(parts, scaled_sums)], axis=1)
    gain_one_part = jnp.sum(
        qkv_own[:, :heads_width] * qkv_sum[:, :heads_width], axis=1, keepdims=True
    ) + jnp.sum(qkv_own[:, heads_width:] * qkv_sum[:, heads_width:], axis=1, keepdims=True)
    small = jnp.concatenate(
        [qkv_sum[:, heads_width:] * gain_one, gain_one_part, gain_two_part], axis=1
    )
    step = 1
    while step < ranks:
        small = small + hop(small, step)
        step *= 2
    return (
        output,
        input_grad,
        qkv_sum[:, :heads_width] * gain_one,
        small[:, : 2 * HD],
        project_sum.T,
        grad_gate,
        grad_up,
        down_sum.T,
        small[:, 2 * HD],
        small[:, 2 * HD + 1],
    )


def solution(mesh):
    placed = (
        P(("dp", "tensor"), None),
        P("dp"),
        P("dp", "tensor"),
        P("dp", None),
        P("tensor", "dp"),
        P("dp", "tensor"),
        P("dp", "tensor"),
        P("tensor", "dp"),
        P("dp"),
        P("dp"),
        P(("dp", "tensor"), None),
        P(("dp", "tensor"), None),
    )
    return jax.shard_map(
        on_device,
        mesh=mesh,
        in_specs=placed,
        out_specs=(
            P(("dp", "tensor"), None),
            P(("dp", "tensor"), None),
            P("dp", "tensor"),
            P("dp", None),
            P("tensor", "dp"),
            P("dp", "tensor"),
            P("dp", "tensor"),
            P("tensor", "dp"),
            P("dp"),
            P("dp"),
        ),
        check_vma=False,
    )
```

```python
import functools
import math

import jax
import jax.numpy as jnp
from jax import lax
from jax.experimental import pallas as pl
from jax.experimental.pallas import tpu as pltpu
from jax.sharding import PartitionSpec as P

HD = 128
eps = 1e-05
rope_base = 10000.0
neg_big = -1e30
inv_root = 1.0 / math.sqrt(HD)
f32 = jnp.float32
bf16 = jnp.bfloat16


def dot(a, b, ca, cb):
    return lax.dot_general(a, b, (((ca,), (cb,)), ((), ())), preferred_element_type=f32)


def hop(value, step):
    size = lax.axis_size("tensor")
    return lax.ppermute(value, "tensor", [(i, i ^ step) for i in range(size)])


def after(value, *others):
    return lax.optimization_barrier((value, *others))[0]


def near_blocks(own):
    size = lax.axis_size("tensor")
    return [hop(own, j) for j in range(1, 3 if size == 4 else size)]


def all_blocks(own, near):
    if lax.axis_size("tensor") != 4:
        return [own, *near]
    half = own.shape[0] // 2
    one, two = near
    return [own, one, two, hop(two[:half], 1), hop(one[half:], 2)]


def send_sums(rest):
    size = lax.axis_size("tensor")
    rows = rest.shape[0] // (size - 1)
    one, *others = (rows_of(rest, j, rows) for j in range(size - 1))
    if size != 4:
        return [hop(block, j + 1) for j, block in enumerate([one, *others])]
    two, three = others
    half = rows // 2
    return [
        hop(jnp.concatenate([one[:half], three[:half]], axis=0), 1),
        hop(jnp.concatenate([two[half:], three[half:]], axis=0), 2),
    ]


def finish_sums(own, rest, arrived):
    arrived = [block.astype(f32) for block in arrived]
    if lax.axis_size("tensor") != 4:
        return own + sum(arrived)
    rows = own.shape[0]
    half = rows // 2
    one, two = rows_of(rest, 0, rows), rows_of(rest, 1, rows)
    upper, lower = arrived
    upper_far = hop((two[:half].astype(f32) + upper[half:]).astype(bf16), 2).astype(f32)
    lower_near = hop((one[half:].astype(f32) + lower[half:]).astype(bf16), 1).astype(f32)
    return jnp.concatenate(
        [own[:half] + upper[:half] + upper_far, own[half:] + lower[:half] + lower_near], axis=0
    )


def gather_dp(shard):
    return lax.all_gather(shard, "dp", axis=0, tiled=True)


def scatter_dp(partial):
    return lax.psum_scatter(partial, "dp", scatter_dimension=0, tiled=True).astype(f32)


def turn(u, cos2, sin2):
    return u * cos2 + pltpu.roll(u, HD // 2, 1) * sin2


def attend_kernel(where_ref, q_ref, kv_ref, cos_ref, sin_ref, qr_ref, kvt_ref, mixed_ref, lse_ref):
    rows, width = q_ref.shape
    heads = width // HD
    ranks = kv_ref.shape[0] // rows
    j = pl.program_id(0)
    rank, length = where_ref[0], where_ref[1]
    block = jnp.bitwise_xor(rank, j)

    @pl.when(j == 0)
    def _():
        for i in range(ranks):
            here = slice(i * rows, (i + 1) * rows)
            there = pl.ds(pl.multiple_of(jnp.bitwise_xor(rank, i) * rows, rows), rows)
            key = turn(kv_ref[here, :HD], cos_ref[here, :], sin_ref[here, :])
            kvt_ref[there, :HD] = key.astype(bf16)
            kvt_ref[there, HD:] = kv_ref[here, HD:].astype(bf16)

    mine = pl.ds(pl.multiple_of(j * rows, rows), rows)
    cos2, sin2 = cos_ref[mine, :], sin_ref[mine, :]
    for h in range(heads):
        head = slice(h * HD, (h + 1) * HD)
        qr_ref[:, head] = turn(q_ref[:, head], cos2, sin2).astype(bf16)
    limit = jnp.minimum(block * rows + lax.broadcasted_iota(jnp.int32, (rows, 1), 0), length - 1)
    for w in range(ranks):

        @pl.when(block == w)
        def _(w=w):
            span = (w + 1) * rows
            allowed = lax.broadcasted_iota(jnp.int32, (rows, span), 1) <= limit
            for h in range(heads):
                head = slice(h * HD, (h + 1) * HD)
                scores = dot(qr_ref[:, head], kvt_ref[:span, :HD], 1, 1) * inv_root
                scores = jnp.where(allowed, scores, neg_big)
                top = jnp.max(scores, axis=1, keepdims=True)
                weights = jnp.exp(scores - top)
                total = jnp.sum(weights, axis=1, keepdims=True)
                probs = (weights * (1.0 / total)).astype(bf16)
                mixed_ref[:, head] = dot(probs, kvt_ref[:span, HD:], 1, 0).astype(bf16)
                lse_ref[:, h : h + 1] = top + jnp.log(total)


def attend_back_kernel(
    where_ref,
    qr_ref,
    kvt_ref,
    dm_ref,
    lse_ref,
    cos_ref,
    sin_ref,
    shared_ref,
    dq_ref,
    dkv_ref,
    dk_acc,
    dv_acc,
):
    rows, width = qr_ref.shape
    heads = width // HD
    ranks = kvt_ref.shape[0] // rows
    j = pl.program_id(0)
    rank, length = where_ref[0], where_ref[1]
    block = jnp.bitwise_xor(rank, j)

    @pl.when(j == 0)
    def _():
        dk_acc[...] = jnp.zeros_like(dk_acc)
        dv_acc[...] = jnp.zeros_like(dv_acc)

    mine = pl.ds(pl.multiple_of(j * rows, rows), rows)
    cos2, sin2 = cos_ref[mine, :], sin_ref[mine, :]
    limit = jnp.minimum(block * rows + lax.broadcasted_iota(jnp.int32, (rows, 1), 0), length - 1)
    for w in range(ranks):

        @pl.when(block == w)
        def _(w=w):
            span = (w + 1) * rows
            allowed = lax.broadcasted_iota(jnp.int32, (rows, span), 1) <= limit
            keys, vals = kvt_ref[:span, :HD], kvt_ref[:span, HD:]
            for h in range(heads):
                head = slice(h * HD, (h + 1) * HD)
                q, dm = qr_ref[:, head], dm_ref[:, head]
                scores = jnp.where(allowed, dot(q, keys, 1, 1) * inv_root, neg_big)
                probs = jnp.exp(scores - lse_ref[:, h : h + 1])
                dp = dot(dm, vals, 1, 1)
                center = jnp.sum(probs * dp, axis=1, keepdims=True)
                ds = (probs * (dp - center)).astype(bf16)
                dq = dot(ds, keys, 1, 0) * inv_root
                dq_ref[:, head] = turn(dq, cos2, -sin2).astype(bf16)
                dk_acc[:span, :] += dot(ds, q, 0, 0)
                dv_acc[:span, :] += dot(probs.astype(bf16), dm, 0, 0)

    @pl.when(j == ranks - 1)
    def _():
        for i in range(ranks):
            here = slice(i * rows, (i + 1) * rows)
            there = pl.ds(pl.multiple_of(jnp.bitwise_xor(rank, i) * rows, rows), rows)
            dk, dv = dk_acc[there, :] * inv_root, dv_acc[there, :]
            if i == 0:
                dk, dv = dk + shared_ref[:, :HD], dv + shared_ref[:, HD:]
            dkv_ref[here, :HD] = turn(dk, cos_ref[here, :], -sin_ref[here, :]).astype(bf16)
            dkv_ref[here, HD:] = dv.astype(bf16)


VMEM_LIMIT = 48 * 2**20


def attend(where, qkv, cos2, sin2, rows):
    slot, width = qkv.shape[0], qkv.shape[1] - 2 * HD
    heads = width // HD
    half = slot * slot * heads * HD
    return pl.pallas_call(
        attend_kernel,
        name="attend",
        grid_spec=pltpu.PrefetchScalarGridSpec(
            num_scalar_prefetch=1,
            grid=(slot // rows,),
            in_specs=[
                pl.BlockSpec((rows, width), lambda j, s: (j, 0)),
                pl.BlockSpec((slot, 2 * HD), lambda j, s: (0, width // (2 * HD))),
                pl.BlockSpec((slot, HD), lambda j, s: (0, 0)),
                pl.BlockSpec((slot, HD), lambda j, s: (0, 0)),
            ],
            out_specs=[
                pl.BlockSpec((rows, width), lambda j, s: (j, 0)),
                pl.BlockSpec((slot, 2 * HD), lambda j, s: (0, 0)),
                pl.BlockSpec((rows, width), lambda j, s: (j, 0)),
                pl.BlockSpec((rows, HD), lambda j, s: (j, 0)),
            ],
        ),
        out_shape=(
            jax.ShapeDtypeStruct((slot, width), bf16),
            jax.ShapeDtypeStruct((slot, 2 * HD), bf16),
            jax.ShapeDtypeStruct((slot, width), bf16),
            jax.ShapeDtypeStruct((slot, HD), f32),
        ),
        compiler_params=pltpu.CompilerParams(
            dimension_semantics=("arbitrary",), vmem_limit_bytes=VMEM_LIMIT
        ),
        cost_estimate=pl.CostEstimate(
            flops=4 * half, bytes_accessed=8 * 2**20, transcendentals=slot * slot * heads
        ),
    )(where, qkv, qkv, cos2, sin2)


def attend_back(where, qr, kvt, dmixed, lse, cos2, sin2, shared, rows):
    slot, width = qr.shape
    heads = width // HD
    half = slot * slot * heads * HD
    return pl.pallas_call(
        attend_back_kernel,
        name="attend_back",
        grid_spec=pltpu.PrefetchScalarGridSpec(
            num_scalar_prefetch=1,
            grid=(slot // rows,),
            in_specs=[
                pl.BlockSpec((rows, width), lambda j, s: (j, 0)),
                pl.BlockSpec((slot, 2 * HD), lambda j, s: (0, 0)),
                pl.BlockSpec((rows, width), lambda j, s: (j, 0)),
                pl.BlockSpec((rows, HD), lambda j, s: (j, 0)),
                pl.BlockSpec((slot, HD), lambda j, s: (0, 0)),
                pl.BlockSpec((slot, HD), lambda j, s: (0, 0)),
                pl.BlockSpec((rows, 2 * HD), lambda j, s: (0, 0)),
            ],
            out_specs=[
                pl.BlockSpec((rows, width), lambda j, s: (j, 0)),
                pl.BlockSpec((slot, 2 * HD), lambda j, s: (0, 0)),
            ],
            scratch_shapes=[pltpu.VMEM((slot, HD), f32), pltpu.VMEM((slot, HD), f32)],
        ),
        out_shape=(
            jax.ShapeDtypeStruct((slot, width), bf16),
            jax.ShapeDtypeStruct((slot, 2 * HD), bf16),
        ),
        compiler_params=pltpu.CompilerParams(
            dimension_semantics=("arbitrary",), vmem_limit_bytes=VMEM_LIMIT
        ),
        cost_estimate=pl.CostEstimate(
            flops=10 * half, bytes_accessed=8 * 2**20, transcendentals=slot * slot * heads
        ),
    )(where, qr, kvt, dmixed, lse, cos2, sin2, shared)


def inverse_norm(values):
    return lax.rsqrt(jnp.mean(values * values, axis=-1, keepdims=True) + eps)


def rows_of(array, j, rows):
    return array[j * rows : (j + 1) * rows]


def on_device(
    layer_input,
    lengths,
    w_query,
    w_keyvalue,
    w_project,
    w_gate,
    w_up,
    w_down,
    gain_attn,
    gain_mlp,
    out_grad,
    kv_grad,
):
    rows, model_width = layer_input.shape
    ranks = lax.axis_size("tensor")
    rank = lax.axis_index("tensor").astype(jnp.int32)
    length = lengths[0]
    heads_width = w_query.shape[1]
    ff = w_gate.shape[1]
    cut = -(-ff // 256) * 128
    parts = ((0, cut), (cut, ff))

    order = jnp.bitwise_xor(rank, jnp.arange(ranks, dtype=jnp.int32))
    position = (order[:, None] * rows + jnp.arange(rows, dtype=jnp.int32)[None, :]).reshape(-1)
    frequency = rope_base ** (-(jnp.arange(HD // 2, dtype=f32) * 2.0 / HD))
    angles = position.astype(f32)[:, None] * frequency[None, :]
    cosine, sine = jnp.cos(angles), jnp.sin(angles)
    cos2 = jnp.concatenate([cosine, cosine], axis=1)
    sin2 = jnp.concatenate([-sine, sine], axis=1)
    own_mask = (position[:rows] < length).astype(f32)[:, None]
    where = jnp.stack([rank, length])

    gain_one, gain_two = gain_attn.astype(f32)[:, None], gain_mlp.astype(f32)[:, None]
    qkv_own = jnp.concatenate([w_query, w_keyvalue], axis=1).astype(f32)
    qkv_width = qkv_own.shape[1]
    attn_shard = jnp.concatenate([(qkv_own * gain_one).astype(bf16), w_project.T], axis=1)
    pair_own = [
        jnp.concatenate([w_gate[:, a:b], w_up[:, a:b]], axis=1).astype(f32) for a, b in parts
    ]
    ff_shards = [
        jnp.concatenate([(own * gain_two).astype(bf16), w_down[a:b].T], axis=1)
        for (a, b), own in zip(parts, pair_own)
    ]

    residual = layer_input.astype(f32)
    near = near_blocks(layer_input)
    inputs = all_blocks(layer_input, near)
    attn_full = gather_dp(attn_shard)
    ff_full = [gather_dp(after(ff_shards[0], *near))]
    qkv_full, project_full = attn_full[:, :qkv_width], attn_full[:, qkv_width:]
    top = out_grad.astype(f32) * own_mask
    top_own = after(top.astype(bf16), *inputs)
    top_near = near_blocks(top_own)

    def norm(block):
        block = block.astype(f32)
        return (block * inverse_norm(block)).astype(bf16)

    normed_one = jnp.concatenate([norm(b) for b in inputs], axis=0)
    qkv = dot(normed_one, qkv_full, 1, 0)
    qr, kvt, mixed, lse = attend(where, qkv, cos2, sin2, rows)
    ff_full.append(gather_dp(after(ff_shards[1], mixed)))
    mixed_rest = dot(after(mixed[rows:], *top_near), project_full, 1, 1).astype(bf16)
    mixed_sent = send_sums(mixed_rest)
    top_all = jnp.concatenate(all_blocks(top_own, top_near), axis=0)
    after_attn = residual + finish_sums(
        dot(mixed[:rows], project_full, 1, 1), mixed_rest, mixed_sent
    )

    inv_two = inverse_norm(after_attn)
    unit_two = after_attn * inv_two
    normed_own = after(unit_two.astype(bf16), top_all)
    normed_two = jnp.concatenate(all_blocks(normed_own, near_blocks(normed_own)), axis=0)

    def feed(part, normed, full):
        width = part[1] - part[0]
        grad = dot(top_all, full[:, 2 * width :], 1, 0)
        both = dot(after(normed, grad), full[:, : 2 * width], 1, 0)
        gate, up = both[:, :width], both[:, width:]
        sig = jax.nn.sigmoid(gate)
        hidden = (gate * sig * up).astype(bf16)
        gate_grad = (grad * up * sig * (1.0 + gate * (1.0 - sig))).astype(bf16)
        up_grad = (grad * gate * sig).astype(bf16)
        return hidden, jnp.concatenate([gate_grad, up_grad], axis=1)

    def partial(hidden, grads):
        return jnp.concatenate(
            [
                dot(normed_two, grads, 0, 0).astype(bf16),
                dot(top_all, hidden, 0, 0).astype(bf16),
            ],
            axis=1,
        )

    pairs = [full[:, : 2 * (b - a)] for (a, b), full in zip(parts, ff_full)]
    downs = [full[:, 2 * (b - a) :] for (a, b), full in zip(parts, ff_full)]
    hidden0, grads0 = feed(parts[0], normed_two, ff_full[0])
    partial0 = partial(hidden0, grads0)
    rest0 = dot(after(grads0[rows:], partial0), pairs[0], 1, 1)
    hidden1, grads1 = feed(parts[1], after(normed_two, rest0), ff_full[1])
    rest = (rest0 + dot(grads1[rows:], pairs[1], 1, 1)).astype(bf16)
    rest_sent = send_sums(rest)
    partial1 = partial(after(hidden1, rest), after(grads1, rest))
    ff_sums = [scatter_dp(partial0), scatter_dp(partial1)]
    own = dot(after(grads0[:rows], partial1), pairs[0], 1, 1) + dot(grads1[:rows], pairs[1], 1, 1)
    scaled = finish_sums(own, rest, rest_sent)
    attn_top = top + inv_two * (
        scaled - unit_two * jnp.mean(scaled * unit_two, axis=-1, keepdims=True)
    )
    attn_top_own = attn_top.astype(bf16)
    attn_top_blocks = all_blocks(attn_top_own, near_blocks(attn_top_own))
    attn_top_all = jnp.concatenate(attn_top_blocks, axis=0)
    hidden = [hidden0, hidden1]
    down_rest = sum(dot(h[rows:], w, 1, 1) for h, w in zip(hidden, downs)).astype(bf16)
    down_rest = after(down_rest, *attn_top_blocks)

    mixed_grad = dot(after(attn_top_all, down_rest, ff_sums[0]), project_full, 1, 0).astype(bf16)
    shared = kv_grad.astype(f32) * own_mask
    query_grad, kv_back = attend_back(
        where, qr, kvt, mixed_grad, lse, cos2, sin2, shared, rows
    )
    down_sent = [after(block, query_grad) for block in send_sums(down_rest)]
    qkv_back = after(jnp.concatenate([query_grad, kv_back], axis=1), *down_sent)
    attn_partial = jnp.concatenate(
        [
            dot(normed_one, qkv_back, 0, 0).astype(bf16),
            dot(attn_top_all, mixed, 0, 0).astype(bf16),
        ],
        axis=1,
    )
    attn_sum = scatter_dp(after(attn_partial, ff_sums[1]))
    own_down = sum(dot(h[:rows], w, 1, 1) for h, w in zip(hidden, downs))
    after_mlp = after_attn + finish_sums(own_down, down_rest, down_sent)
    output = (after_mlp * own_mask).astype(bf16)
    qkv_rest = dot(after(qkv_back[rows:], attn_partial), qkv_full, 1, 1).astype(bf16)
    scaled_one = finish_sums(
        dot(qkv_back[:rows], qkv_full, 1, 1), qkv_rest, send_sums(qkv_rest)
    )
    inv_one = inverse_norm(residual)
    unit_one = residual * inv_one
    input_grad = attn_top + inv_one * (
        scaled_one - unit_one * jnp.mean(scaled_one * unit_one, axis=-1, keepdims=True)
    )

    qkv_sum, project_sum = attn_sum[:, :qkv_width], attn_sum[:, qkv_width:]
    pair_sums = [total[:, : own.shape[1]] for own, total in zip(pair_own, ff_sums)]
    down_sum = jnp.concatenate(
        [total[:, own.shape[1] :] for own, total in zip(pair_own, ff_sums)], axis=1
    )
    gain_two_part = sum(
        jnp.sum(own * total, axis=1, keepdims=True) for own, total in zip(pair_own, pair_sums)
    )
    scaled_sums = [total * gain_two for total in pair_sums]
    grad_gate = jnp.concatenate([s[:, : b - a] for (a, b), s in zip(parts, scaled_sums)], axis=1)
    grad_up = jnp.concatenate([s[:, b - a :] for (a, b), s in zip(parts, scaled_sums)], axis=1)
    gain_one_part = jnp.sum(
        qkv_own[:, :heads_width] * qkv_sum[:, :heads_width], axis=1, keepdims=True
    ) + jnp.sum(qkv_own[:, heads_width:] * qkv_sum[:, heads_width:], axis=1, keepdims=True)
    small = jnp.concatenate(
        [qkv_sum[:, heads_width:] * gain_one, gain_one_part, gain_two_part], axis=1
    )
    step = 1
    while step < ranks:
        small = small + hop(small, step)
        step *= 2
    return (
        output,
        input_grad,
        qkv_sum[:, :heads_width] * gain_one,
        small[:, : 2 * HD],
        project_sum.T,
        grad_gate,
        grad_up,
        down_sum.T,
        small[:, 2 * HD],
        small[:, 2 * HD + 1],
    )


def solution(mesh):
    placed = (
        P(("dp", "tensor"), None),
        P("dp"),
        P("dp", "tensor"),
        P("dp", None),
        P("tensor", "dp"),
        P("dp", "tensor"),
        P("dp", "tensor"),
        P("tensor", "dp"),
        P("dp"),
        P("dp"),
        P(("dp", "tensor"), None),
        P(("dp", "tensor"), None),
    )
    return jax.shard_map(
        on_device,
        mesh=mesh,
        in_specs=placed,
        out_specs=(
            P(("dp", "tensor"), None),
            P(("dp", "tensor"), None),
            P("dp", "tensor"),
            P("dp", None),
            P("tensor", "dp"),
            P("dp", "tensor"),
            P("dp", "tensor"),
            P("tensor", "dp"),
            P("dp"),
            P("dp"),
        ),
        check_vma=False,
    )
```

```python
import functools
import math

import jax
import jax.numpy as jnp
from jax import lax
from jax.experimental import pallas as pl
from jax.experimental.pallas import tpu as pltpu
from jax.sharding import PartitionSpec as P

HD = 128
eps = 1e-05
rope_base = 10000.0
neg_big = -1e30
inv_root = 1.0 / math.sqrt(HD)
f32 = jnp.float32
bf16 = jnp.bfloat16


def dot(a, b, ca, cb):
    return lax.dot_general(a, b, (((ca,), (cb,)), ((), ())), preferred_element_type=f32)


def hop(value, step):
    size = lax.axis_size("tensor")
    return lax.ppermute(value, "tensor", [(i, i ^ step) for i in range(size)])


def after(value, *others):
    return lax.optimization_barrier((value, *others))[0]


def near_blocks(own):
    size = lax.axis_size("tensor")
    return [hop(own, j) for j in range(1, 3 if size == 4 else size)]


def all_blocks(own, near):
    if lax.axis_size("tensor") != 4:
        return [own, *near]
    half = own.shape[0] // 2
    one, two = near
    return [own, one, two, hop(two[:half], 1), hop(one[half:], 2)]


def send_sums(rest):
    size = lax.axis_size("tensor")
    rows = rest.shape[0] // (size - 1)
    one, *others = (rows_of(rest, j, rows) for j in range(size - 1))
    if size != 4:
        return [hop(block, j + 1) for j, block in enumerate([one, *others])]
    two, three = others
    half = rows // 2
    return [
        hop(jnp.concatenate([one[:half], three[:half]], axis=0), 1),
        hop(jnp.concatenate([two[half:], three[half:]], axis=0), 2),
    ]


def finish_sums(own, rest, arrived):
    arrived = [block.astype(f32) for block in arrived]
    if lax.axis_size("tensor") != 4:
        return own + sum(arrived)
    rows = own.shape[0]
    half = rows // 2
    one, two = rows_of(rest, 0, rows), rows_of(rest, 1, rows)
    upper, lower = arrived
    upper_far = hop((two[:half].astype(f32) + upper[half:]).astype(bf16), 2).astype(f32)
    lower_near = hop((one[half:].astype(f32) + lower[half:]).astype(bf16), 1).astype(f32)
    return jnp.concatenate(
        [own[:half] + upper[:half] + upper_far, own[half:] + lower[:half] + lower_near], axis=0
    )


def gather_dp(shard):
    return lax.all_gather(shard, "dp", axis=0, tiled=True)


def scatter_dp(partial):
    return lax.psum_scatter(partial, "dp", scatter_dimension=0, tiled=True).astype(f32)


pick = functools.partial(lax.dynamic_index_in_dim, keepdims=False)


def turn(u, cos2, sin2):
    return u * cos2 + pltpu.roll(u, HD // 2, 1) * sin2


def attend_kernel(where_ref, q_ref, kv_ref, cos_ref, sin_ref, qr_ref, kvt_ref, mixed_ref, lse_ref):
    rows, width = q_ref.shape
    heads = width // HD
    ranks = kv_ref.shape[0] // rows
    j = pl.program_id(0)
    rank, length = where_ref[0], where_ref[1]
    block = jnp.bitwise_xor(rank, j)

    @pl.when(j == 0)
    def _():
        for i in range(ranks):
            here = slice(i * rows, (i + 1) * rows)
            there = pl.ds(pl.multiple_of(jnp.bitwise_xor(rank, i) * rows, rows), rows)
            key = turn(kv_ref[here, :HD], cos_ref[here, :], sin_ref[here, :])
            kvt_ref[there, :HD] = key.astype(bf16)
            kvt_ref[there, HD:] = kv_ref[here, HD:].astype(bf16)

    mine = pl.ds(pl.multiple_of(j * rows, rows), rows)
    cos2, sin2 = cos_ref[mine, :], sin_ref[mine, :]
    for h in range(heads):
        head = slice(h * HD, (h + 1) * HD)
        qr_ref[:, head] = turn(q_ref[:, head], cos2, sin2).astype(bf16)
    limit = jnp.minimum(block * rows + lax.broadcasted_iota(jnp.int32, (rows, 1), 0), length - 1)
    for w in range(ranks):

        @pl.when(block == w)
        def _(w=w):
            span = (w + 1) * rows
            allowed = lax.broadcasted_iota(jnp.int32, (rows, span), 1) <= limit
            for h in range(heads):
                head = slice(h * HD, (h + 1) * HD)
                scores = dot(qr_ref[:, head], kvt_ref[:span, :HD], 1, 1) * inv_root
                scores = jnp.where(allowed, scores, neg_big)
                top = jnp.max(scores, axis=1, keepdims=True)
                weights = jnp.exp(scores - top)
                total = jnp.sum(weights, axis=1, keepdims=True)
                probs = (weights * (1.0 / total)).astype(bf16)
                mixed_ref[:, head] = dot(probs, kvt_ref[:span, HD:], 1, 0).astype(bf16)
                lse_ref[:, h : h + 1] = top + jnp.log(total)


def attend_back_kernel(
    where_ref,
    qr_ref,
    kvt_ref,
    dm_ref,
    lse_ref,
    cos_ref,
    sin_ref,
    shared_ref,
    dq_ref,
    dkv_ref,
    dk_acc,
    dv_acc,
):
    rows, width = qr_ref.shape
    heads = width // HD
    ranks = kvt_ref.shape[0] // rows
    j = pl.program_id(0)
    rank, length = where_ref[0], where_ref[1]
    block = jnp.bitwise_xor(rank, j)

    @pl.when(j == 0)
    def _():
        dk_acc[...] = jnp.zeros_like(dk_acc)
        dv_acc[...] = jnp.zeros_like(dv_acc)

    mine = pl.ds(pl.multiple_of(j * rows, rows), rows)
    cos2, sin2 = cos_ref[mine, :], sin_ref[mine, :]
    limit = jnp.minimum(block * rows + lax.broadcasted_iota(jnp.int32, (rows, 1), 0), length - 1)
    for w in range(ranks):

        @pl.when(block == w)
        def _(w=w):
            span = (w + 1) * rows
            allowed = lax.broadcasted_iota(jnp.int32, (rows, span), 1) <= limit
            keys, vals = kvt_ref[:span, :HD], kvt_ref[:span, HD:]
            for h in range(heads):
                head = slice(h * HD, (h + 1) * HD)
                q, dm = qr_ref[:, head], dm_ref[:, head]
                scores = jnp.where(allowed, dot(q, keys, 1, 1) * inv_root, neg_big)
                probs = jnp.exp(scores - lse_ref[:, h : h + 1])
                dp = dot(dm, vals, 1, 1)
                center = jnp.sum(probs * dp, axis=1, keepdims=True)
                ds = (probs * (dp - center)).astype(bf16)
                dq = dot(ds, keys, 1, 0) * inv_root
                dq_ref[:, head] = turn(dq, cos2, -sin2).astype(bf16)
                dk_acc[:span, :] += dot(ds, q, 0, 0)
                dv_acc[:span, :] += dot(probs.astype(bf16), dm, 0, 0)

    @pl.when(j == ranks - 1)
    def _():
        for i in range(ranks):
            here = slice(i * rows, (i + 1) * rows)
            there = pl.ds(pl.multiple_of(jnp.bitwise_xor(rank, i) * rows, rows), rows)
            dk, dv = dk_acc[there, :] * inv_root, dv_acc[there, :]
            if i == 0:
                dk, dv = dk + shared_ref[:, :HD], dv + shared_ref[:, HD:]
            dkv_ref[here, :HD] = turn(dk, cos_ref[here, :], -sin_ref[here, :]).astype(bf16)
            dkv_ref[here, HD:] = dv.astype(bf16)


VMEM_LIMIT = 48 * 2**20


def attend(where, qkv, cos2, sin2, rows):
    slot, width = qkv.shape[0], qkv.shape[1] - 2 * HD
    heads = width // HD
    half = slot * slot * heads * HD
    return pl.pallas_call(
        attend_kernel,
        name="attend",
        grid_spec=pltpu.PrefetchScalarGridSpec(
            num_scalar_prefetch=1,
            grid=(slot // rows,),
            in_specs=[
                pl.BlockSpec((rows, width), lambda j, s: (j, 0)),
                pl.BlockSpec((slot, 2 * HD), lambda j, s: (0, width // (2 * HD))),
                pl.BlockSpec((slot, HD), lambda j, s: (0, 0)),
                pl.BlockSpec((slot, HD), lambda j, s: (0, 0)),
            ],
            out_specs=[
                pl.BlockSpec((rows, width), lambda j, s: (j, 0)),
                pl.BlockSpec((slot, 2 * HD), lambda j, s: (0, 0)),
                pl.BlockSpec((rows, width), lambda j, s: (j, 0)),
                pl.BlockSpec((rows, HD), lambda j, s: (j, 0)),
            ],
        ),
        out_shape=(
            jax.ShapeDtypeStruct((slot, width), bf16),
            jax.ShapeDtypeStruct((slot, 2 * HD), bf16),
            jax.ShapeDtypeStruct((slot, width), bf16),
            jax.ShapeDtypeStruct((slot, HD), f32),
        ),
        compiler_params=pltpu.CompilerParams(
            dimension_semantics=("arbitrary",), vmem_limit_bytes=VMEM_LIMIT
        ),
        cost_estimate=pl.CostEstimate(
            flops=4 * half, bytes_accessed=8 * 2**20, transcendentals=slot * slot * heads
        ),
    )(where, qkv, qkv, cos2, sin2)


def attend_back(where, qr, kvt, dmixed, lse, cos2, sin2, shared, rows):
    slot, width = qr.shape
    heads = width // HD
    half = slot * slot * heads * HD
    return pl.pallas_call(
        attend_back_kernel,
        name="attend_back",
        grid_spec=pltpu.PrefetchScalarGridSpec(
            num_scalar_prefetch=1,
            grid=(slot // rows,),
            in_specs=[
                pl.BlockSpec((rows, width), lambda j, s: (j, 0)),
                pl.BlockSpec((slot, 2 * HD), lambda j, s: (0, 0)),
                pl.BlockSpec((rows, width), lambda j, s: (j, 0)),
                pl.BlockSpec((rows, HD), lambda j, s: (j, 0)),
                pl.BlockSpec((slot, HD), lambda j, s: (0, 0)),
                pl.BlockSpec((slot, HD), lambda j, s: (0, 0)),
                pl.BlockSpec((rows, 2 * HD), lambda j, s: (0, 0)),
            ],
            out_specs=[
                pl.BlockSpec((rows, width), lambda j, s: (j, 0)),
                pl.BlockSpec((slot, 2 * HD), lambda j, s: (0, 0)),
            ],
            scratch_shapes=[pltpu.VMEM((slot, HD), f32), pltpu.VMEM((slot, HD), f32)],
        ),
        out_shape=(
            jax.ShapeDtypeStruct((slot, width), bf16),
            jax.ShapeDtypeStruct((slot, 2 * HD), bf16),
        ),
        compiler_params=pltpu.CompilerParams(
            dimension_semantics=("arbitrary",), vmem_limit_bytes=VMEM_LIMIT
        ),
        cost_estimate=pl.CostEstimate(
            flops=10 * half, bytes_accessed=8 * 2**20, transcendentals=slot * slot * heads
        ),
    )(where, qr, kvt, dmixed, lse, cos2, sin2, shared)


def inverse_norm(values):
    return lax.rsqrt(jnp.mean(values * values, axis=-1, keepdims=True) + eps)


def rows_of(array, j, rows):
    return array[j * rows : (j + 1) * rows]


def on_device(
    layer_input,
    lengths,
    w_query,
    w_keyvalue,
    w_project,
    w_gate,
    w_up,
    w_down,
    gain_attn,
    gain_mlp,
    out_grad,
    kv_grad,
):
    rows, model_width = layer_input.shape
    ranks = lax.axis_size("tensor")
    rank = lax.axis_index("tensor").astype(jnp.int32)
    length = lengths[0]
    heads_width = w_query.shape[1]
    ff = w_gate.shape[1]
    cut = -(-ff // 256) * 128
    parts = ((0, cut), (cut, ff))

    order = jnp.bitwise_xor(rank, jnp.arange(ranks, dtype=jnp.int32))
    position = (order[:, None] * rows + jnp.arange(rows, dtype=jnp.int32)[None, :]).reshape(-1)
    frequency = rope_base ** (-(jnp.arange(HD // 2, dtype=f32) * 2.0 / HD))
    angles = position.astype(f32)[:, None] * frequency[None, :]
    cosine, sine = jnp.cos(angles), jnp.sin(angles)
    cos2 = jnp.concatenate([cosine, cosine], axis=1)
    sin2 = jnp.concatenate([-sine, sine], axis=1)
    own_mask = (position[:rows] < length).astype(f32)[:, None]
    where = jnp.stack([rank, length])

    gain_one, gain_two = gain_attn.astype(f32)[:, None], gain_mlp.astype(f32)[:, None]
    qkv_own = jnp.concatenate([w_query, w_keyvalue], axis=1).astype(f32)
    shard_rows = qkv_own.shape[0]
    kv_rows = shard_rows // ranks
    scaled_own = (qkv_own * gain_one).astype(bf16)
    kv_part = lax.dynamic_slice_in_dim(scaled_own[:, heads_width:], rank * kv_rows, kv_rows)
    attn_shard = jnp.concatenate(
        [scaled_own[:, :heads_width], w_project.T, kv_part.reshape(-1, heads_width)], axis=0
    )
    pair_own = [
        jnp.concatenate([w_gate[:, a:b], w_up[:, a:b]], axis=1).astype(f32) for a, b in parts
    ]
    ff_shards = [
        jnp.concatenate([(own * gain_two).astype(bf16), w_down[a:b].T], axis=1)
        for (a, b), own in zip(parts, pair_own)
    ]

    residual = layer_input.astype(f32)
    near = near_blocks(layer_input)
    inputs = all_blocks(layer_input, near)
    attn_full = gather_dp(attn_shard)
    ff_full = [gather_dp(after(ff_shards[0], *near))]
    attn_full = attn_full.reshape(-1, *attn_shard.shape)
    query_full = attn_full[:, :shard_rows].reshape(model_width, heads_width)
    project_full = attn_full[:, shard_rows : 2 * shard_rows].reshape(model_width, heads_width)
    kv_part = attn_full[:, 2 * shard_rows :].reshape(-1, 2 * HD)
    kv_near = near_blocks(kv_part)
    kv_blocks = jnp.concatenate(all_blocks(kv_part, kv_near), axis=0)
    kv_blocks = kv_blocks.reshape(ranks, -1, kv_rows, 2 * HD)
    keyvalue_full = jnp.stack([pick(kv_blocks, order[j], 0) for j in range(ranks)], axis=1)
    qkv_full = jnp.concatenate([query_full, keyvalue_full.reshape(model_width, 2 * HD)], axis=1)
    top = out_grad.astype(f32) * own_mask
    top_own = after(top.astype(bf16), keyvalue_full)
    top_near = near_blocks(top_own)

    def norm(block):
        block = block.astype(f32)
        return (block * inverse_norm(block)).astype(bf16)

    normed_one = jnp.concatenate([norm(b) for b in inputs], axis=0)
    qkv = dot(normed_one, qkv_full, 1, 0)
    qr, kvt, mixed, lse = attend(where, qkv, cos2, sin2, rows)
    ff_full.append(gather_dp(after(ff_shards[1], mixed)))
    mixed_rest = dot(after(mixed[rows:], *top_near), project_full, 1, 1).astype(bf16)
    mixed_sent = send_sums(mixed_rest)
    top_near = [after(block, *mixed_sent) for block in top_near]
    top_all = jnp.concatenate(all_blocks(top_own, top_near), axis=0)
    after_attn = residual + finish_sums(
        dot(mixed[:rows], project_full, 1, 1), mixed_rest, mixed_sent
    )

    inv_two = inverse_norm(after_attn)
    unit_two = after_attn * inv_two
    normed_own = after(unit_two.astype(bf16), top_all)
    pairs = [full[:, : 2 * (b - a)] for (a, b), full in zip(parts, ff_full)]
    downs = [full[:, 2 * (b - a) :] for (a, b), full in zip(parts, ff_full)]
    first_grad = dot(top_all, downs[0], 1, 0)
    normed_near = [after(block, first_grad) for block in near_blocks(normed_own)]
    normed_two = jnp.concatenate(all_blocks(normed_own, normed_near), axis=0)

    def feed(normed, pair, grad):
        width = grad.shape[1]
        both = dot(after(normed, grad), pair, 1, 0)
        gate, up = both[:, :width], both[:, width:]
        sig = jax.nn.sigmoid(gate)
        hidden = (gate * sig * up).astype(bf16)
        gate_grad = (grad * up * sig * (1.0 + gate * (1.0 - sig))).astype(bf16)
        up_grad = (grad * gate * sig).astype(bf16)
        return hidden, jnp.concatenate([gate_grad, up_grad], axis=1)

    def partial(hidden, grads):
        return jnp.concatenate(
            [
                dot(normed_two, grads, 0, 0).astype(bf16),
                dot(top_all, hidden, 0, 0).astype(bf16),
            ],
            axis=1,
        )

    hidden0, grads0 = feed(normed_two, pairs[0], first_grad)
    partial0 = partial(hidden0, grads0)
    rest0 = dot(after(grads0[rows:], partial0), pairs[0], 1, 1)
    hidden1, grads1 = feed(after(normed_two, rest0), pairs[1], dot(top_all, downs[1], 1, 0))
    rest = (rest0 + dot(grads1[rows:], pairs[1], 1, 1)).astype(bf16)
    rest_sent = send_sums(rest)
    partial1 = partial(after(hidden1, rest), after(grads1, rest))
    ff_sums = [scatter_dp(partial0), scatter_dp(partial1)]
    own = dot(after(grads0[:rows], partial1), pairs[0], 1, 1) + dot(grads1[:rows], pairs[1], 1, 1)
    scaled = finish_sums(own, rest, rest_sent)
    attn_top = top + inv_two * (
        scaled - unit_two * jnp.mean(scaled * unit_two, axis=-1, keepdims=True)
    )
    attn_top_own = attn_top.astype(bf16)
    attn_top_blocks = all_blocks(attn_top_own, near_blocks(attn_top_own))
    attn_top_all = jnp.concatenate(attn_top_blocks, axis=0)
    hidden = [hidden0, hidden1]
    down_rest = sum(dot(h[rows:], w, 1, 1) for h, w in zip(hidden, downs)).astype(bf16)
    down_rest = after(down_rest, *attn_top_blocks)

    mixed_grad = dot(after(attn_top_all, down_rest, ff_sums[0]), project_full, 1, 0).astype(bf16)
    shared = kv_grad.astype(f32) * own_mask
    query_grad, kv_back = attend_back(
        where, qr, kvt, mixed_grad, lse, cos2, sin2, shared, rows
    )
    down_sent = [after(block, query_grad) for block in send_sums(down_rest)]
    qkv_back = after(jnp.concatenate([query_grad, kv_back], axis=1), *down_sent)
    kv_grads = dot(normed_one, qkv_back[:, heads_width:], 0, 0).astype(bf16)
    kv_grads = kv_grads.reshape(-1, ranks, kv_rows, 2 * HD)
    kv_own, *kv_rest = (pick(kv_grads, order[j], 1).reshape(-1, 2 * HD) for j in range(ranks))
    kv_rest = jnp.concatenate(kv_rest, axis=0)
    kv_sum = finish_sums(kv_own.astype(f32), kv_rest, send_sums(kv_rest)).astype(bf16)
    attn_partial = jnp.concatenate(
        [
            dot(normed_one, qkv_back[:, :heads_width], 0, 0)
            .astype(bf16)
            .reshape(-1, shard_rows, heads_width),
            dot(attn_top_all, mixed, 0, 0).astype(bf16).reshape(-1, shard_rows, heads_width),
            kv_sum.reshape(model_width // shard_rows, -1, heads_width),
        ],
        axis=1,
    ).reshape(-1, heads_width)
    attn_sum = scatter_dp(after(attn_partial, ff_sums[1]))
    own_down = sum(dot(h[:rows], w, 1, 1) for h, w in zip(hidden, downs))
    after_mlp = after_attn + finish_sums(own_down, down_rest, down_sent)
    output = (after_mlp * own_mask).astype(bf16)
    qkv_rest = dot(after(qkv_back[rows:], attn_partial), qkv_full, 1, 1).astype(bf16)
    scaled_one = finish_sums(
        dot(qkv_back[:rows], qkv_full, 1, 1), qkv_rest, send_sums(qkv_rest)
    )
    inv_one = inverse_norm(residual)
    unit_one = residual * inv_one
    input_grad = attn_top + inv_one * (
        scaled_one - unit_one * jnp.mean(scaled_one * unit_one, axis=-1, keepdims=True)
    )

    query_sum, project_sum = attn_sum[:shard_rows], attn_sum[shard_rows : 2 * shard_rows]
    kv_sum = attn_sum[2 * shard_rows :].reshape(kv_rows, 2 * HD)
    pair_sums = [total[:, : own.shape[1]] for own, total in zip(pair_own, ff_sums)]
    down_sum = jnp.concatenate(
        [total[:, own.shape[1] :] for own, total in zip(pair_own, ff_sums)], axis=1
    )
    gain_two_part = sum(
        jnp.sum(own * total, axis=1, keepdims=True) for own, total in zip(pair_own, pair_sums)
    )
    scaled_sums = [total * gain_two for total in pair_sums]
    grad_gate = jnp.concatenate([s[:, : b - a] for (a, b), s in zip(parts, scaled_sums)], axis=1)
    grad_up = jnp.concatenate([s[:, b - a :] for (a, b), s in zip(parts, scaled_sums)], axis=1)
    query_part = jnp.sum(qkv_own[:, :heads_width] * query_sum, axis=1, keepdims=True)
    kv_here = lax.dynamic_slice_in_dim(qkv_own[:, heads_width:], rank * kv_rows, kv_rows)
    gain_here = lax.dynamic_slice_in_dim(gain_one, rank * kv_rows, kv_rows)
    small = jnp.concatenate(
        [
            kv_sum * gain_here,
            jnp.sum(kv_here * kv_sum, axis=1, keepdims=True),
            jnp.concatenate([query_part, gain_two_part], axis=1).reshape(kv_rows, -1),
        ],
        axis=1,
    )
    blocks = jnp.stack([small] + [hop(small, j) for j in range(1, ranks)], axis=0)
    sums = jnp.sum(blocks[:, :, 2 * HD + 1 :], axis=0).reshape(shard_rows, 2)
    placed = jnp.concatenate([pick(blocks, order[j], 0) for j in range(ranks)], axis=0)
    return (
        output,
        input_grad,
        query_sum * gain_one,
        placed[:, : 2 * HD],
        project_sum.T,
        grad_gate,
        grad_up,
        down_sum.T,
        sums[:, 0] + placed[:, 2 * HD],
        sums[:, 1],
    )


def solution(mesh):
    placed = (
        P(("dp", "tensor"), None),
        P("dp"),
        P("dp", "tensor"),
        P("dp", None),
        P("tensor", "dp"),
        P("dp", "tensor"),
        P("dp", "tensor"),
        P("tensor", "dp"),
        P("dp"),
        P("dp"),
        P(("dp", "tensor"), None),
        P(("dp", "tensor"), None),
    )
    return jax.shard_map(
        on_device,
        mesh=mesh,
        in_specs=placed,
        out_specs=(
            P(("dp", "tensor"), None),
            P(("dp", "tensor"), None),
            P("dp", "tensor"),
            P("dp", None),
            P("tensor", "dp"),
            P("dp", "tensor"),
            P("dp", "tensor"),
            P("tensor", "dp"),
            P("dp"),
            P("dp"),
        ),
        check_vma=False,
    )
```

```python
import functools
import math

import jax
import jax.numpy as jnp
from jax import lax
from jax.experimental import pallas as pl
from jax.experimental.pallas import tpu as pltpu
from jax.sharding import PartitionSpec as P

HD = 128
eps = 1e-05
rope_base = 10000.0
neg_big = -1e30
inv_root = 1.0 / math.sqrt(HD)
f32 = jnp.float32
bf16 = jnp.bfloat16


def dot(a, b, ca, cb):
    return lax.dot_general(a, b, (((ca,), (cb,)), ((), ())), preferred_element_type=f32)


def hop(value, step):
    size = lax.axis_size("tensor")
    return lax.ppermute(value, "tensor", [(i, i ^ step) for i in range(size)])


def after(value, *others):
    return lax.optimization_barrier((value, *others))[0]


def near_blocks(own):
    size = lax.axis_size("tensor")
    return [hop(own, j) for j in range(1, 3 if size == 4 else size)]


def all_blocks(own, near):
    if lax.axis_size("tensor") != 4:
        return [own, *near]
    half = own.shape[0] // 2
    one, two = near
    return [own, one, two, hop(two[:half], 1), hop(one[half:], 2)]


def send_sums(rest):
    size = lax.axis_size("tensor")
    rows = rest.shape[0] // (size - 1)
    one, *others = (rows_of(rest, j, rows) for j in range(size - 1))
    if size != 4:
        return [hop(block, j + 1) for j, block in enumerate([one, *others])]
    two, three = others
    half = rows // 2
    return [
        hop(jnp.concatenate([one[:half], three[:half]], axis=0), 1),
        hop(jnp.concatenate([two[half:], three[half:]], axis=0), 2),
    ]


def finish_sums(own, rest, arrived):
    arrived = [block.astype(f32) for block in arrived]
    if lax.axis_size("tensor") != 4:
        return own + sum(arrived)
    rows = own.shape[0]
    half = rows // 2
    one, two = rows_of(rest, 0, rows), rows_of(rest, 1, rows)
    upper, lower = arrived
    upper_far = hop((two[:half].astype(f32) + upper[half:]).astype(bf16), 2).astype(f32)
    lower_near = hop((one[half:].astype(f32) + lower[half:]).astype(bf16), 1).astype(f32)
    return jnp.concatenate(
        [own[:half] + upper[:half] + upper_far, own[half:] + lower[:half] + lower_near], axis=0
    )


def gather_dp(shard):
    return lax.all_gather(shard, "dp", axis=0, tiled=True)


def scatter_dp(partial):
    return lax.psum_scatter(partial, "dp", scatter_dimension=0, tiled=True).astype(f32)


pick = functools.partial(lax.dynamic_index_in_dim, keepdims=False)


def turn(u, cos2, sin2):
    return u * cos2 + pltpu.roll(u, HD // 2, 1) * sin2


def attend_kernel(where_ref, q_ref, kv_ref, cos_ref, sin_ref, qr_ref, kvt_ref, mixed_ref, lse_ref):
    rows, width = q_ref.shape
    heads = width // HD
    ranks = kv_ref.shape[0] // rows
    j = pl.program_id(0)
    rank, length = where_ref[0], where_ref[1]
    block = jnp.bitwise_xor(rank, j)

    @pl.when(j == 0)
    def _():
        for i in range(ranks):
            here = slice(i * rows, (i + 1) * rows)
            there = pl.ds(pl.multiple_of(jnp.bitwise_xor(rank, i) * rows, rows), rows)
            key = turn(kv_ref[here, :HD], cos_ref[here, :], sin_ref[here, :])
            kvt_ref[there, :HD] = key.astype(bf16)
            kvt_ref[there, HD:] = kv_ref[here, HD:].astype(bf16)

    mine = pl.ds(pl.multiple_of(j * rows, rows), rows)
    cos2, sin2 = cos_ref[mine, :], sin_ref[mine, :]
    for h in range(heads):
        head = slice(h * HD, (h + 1) * HD)
        qr_ref[:, head] = turn(q_ref[:, head], cos2, sin2).astype(bf16)
    limit = jnp.minimum(block * rows + lax.broadcasted_iota(jnp.int32, (rows, 1), 0), length - 1)
    for w in range(ranks):

        @pl.when(block == w)
        def _(w=w):
            span = (w + 1) * rows
            allowed = lax.broadcasted_iota(jnp.int32, (rows, span), 1) <= limit
            for h in range(heads):
                head = slice(h * HD, (h + 1) * HD)
                scores = dot(qr_ref[:, head], kvt_ref[:span, :HD], 1, 1) * inv_root
                scores = jnp.where(allowed, scores, neg_big)
                top = jnp.max(scores, axis=1, keepdims=True)
                weights = jnp.exp(scores - top)
                total = jnp.sum(weights, axis=1, keepdims=True)
                probs = (weights * (1.0 / total)).astype(bf16)
                mixed_ref[:, head] = dot(probs, kvt_ref[:span, HD:], 1, 0).astype(bf16)
                lse_ref[:, h : h + 1] = top + jnp.log(total)


def attend_back_kernel(
    where_ref,
    qr_ref,
    kvt_ref,
    dm_ref,
    lse_ref,
    cos_ref,
    sin_ref,
    shared_ref,
    dq_ref,
    dkv_ref,
    dk_acc,
    dv_acc,
):
    rows, width = qr_ref.shape
    heads = width // HD
    ranks = kvt_ref.shape[0] // rows
    j = pl.program_id(0)
    rank, length = where_ref[0], where_ref[1]
    block = jnp.bitwise_xor(rank, j)

    @pl.when(j == 0)
    def _():
        dk_acc[...] = jnp.zeros_like(dk_acc)
        dv_acc[...] = jnp.zeros_like(dv_acc)

    mine = pl.ds(pl.multiple_of(j * rows, rows), rows)
    cos2, sin2 = cos_ref[mine, :], sin_ref[mine, :]
    limit = jnp.minimum(block * rows + lax.broadcasted_iota(jnp.int32, (rows, 1), 0), length - 1)
    for w in range(ranks):

        @pl.when(block == w)
        def _(w=w):
            span = (w + 1) * rows
            allowed = lax.broadcasted_iota(jnp.int32, (rows, span), 1) <= limit
            keys, vals = kvt_ref[:span, :HD], kvt_ref[:span, HD:]
            for h in range(heads):
                head = slice(h * HD, (h + 1) * HD)
                q, dm = qr_ref[:, head], dm_ref[:, head]
                scores = jnp.where(allowed, dot(q, keys, 1, 1) * inv_root, neg_big)
                probs = jnp.exp(scores - lse_ref[:, h : h + 1])
                dp = dot(dm, vals, 1, 1)
                center = jnp.sum(probs * dp, axis=1, keepdims=True)
                ds = (probs * (dp - center)).astype(bf16)
                dq = dot(ds, keys, 1, 0) * inv_root
                dq_ref[:, head] = turn(dq, cos2, -sin2).astype(bf16)
                dk_acc[:span, :] += dot(ds, q, 0, 0)
                dv_acc[:span, :] += dot(probs.astype(bf16), dm, 0, 0)

    @pl.when(j == ranks - 1)
    def _():
        for i in range(ranks):
            here = slice(i * rows, (i + 1) * rows)
            there = pl.ds(pl.multiple_of(jnp.bitwise_xor(rank, i) * rows, rows), rows)
            dk, dv = dk_acc[there, :] * inv_root, dv_acc[there, :]
            if i == 0:
                dk, dv = dk + shared_ref[:, :HD], dv + shared_ref[:, HD:]
            dkv_ref[here, :HD] = turn(dk, cos_ref[here, :], -sin_ref[here, :]).astype(bf16)
            dkv_ref[here, HD:] = dv.astype(bf16)


VMEM_LIMIT = 48 * 2**20


def attend(where, qkv, cos2, sin2, rows):
    slot, width = qkv.shape[0], qkv.shape[1] - 2 * HD
    heads = width // HD
    half = slot * slot * heads * HD
    return pl.pallas_call(
        attend_kernel,
        name="attend",
        grid_spec=pltpu.PrefetchScalarGridSpec(
            num_scalar_prefetch=1,
            grid=(slot // rows,),
            in_specs=[
                pl.BlockSpec((rows, width), lambda j, s: (j, 0)),
                pl.BlockSpec((slot, 2 * HD), lambda j, s: (0, width // (2 * HD))),
                pl.BlockSpec((slot, HD), lambda j, s: (0, 0)),
                pl.BlockSpec((slot, HD), lambda j, s: (0, 0)),
            ],
            out_specs=[
                pl.BlockSpec((rows, width), lambda j, s: (j, 0)),
                pl.BlockSpec((slot, 2 * HD), lambda j, s: (0, 0)),
                pl.BlockSpec((rows, width), lambda j, s: (j, 0)),
                pl.BlockSpec((rows, HD), lambda j, s: (j, 0)),
            ],
        ),
        out_shape=(
            jax.ShapeDtypeStruct((slot, width), bf16),
            jax.ShapeDtypeStruct((slot, 2 * HD), bf16),
            jax.ShapeDtypeStruct((slot, width), bf16),
            jax.ShapeDtypeStruct((slot, HD), f32),
        ),
        compiler_params=pltpu.CompilerParams(
            dimension_semantics=("arbitrary",), vmem_limit_bytes=VMEM_LIMIT
        ),
        cost_estimate=pl.CostEstimate(
            flops=4 * half, bytes_accessed=8 * 2**20, transcendentals=slot * slot * heads
        ),
    )(where, qkv, qkv, cos2, sin2)


def attend_back(where, qr, kvt, dmixed, lse, cos2, sin2, shared, rows):
    slot, width = qr.shape
    heads = width // HD
    half = slot * slot * heads * HD
    return pl.pallas_call(
        attend_back_kernel,
        name="attend_back",
        grid_spec=pltpu.PrefetchScalarGridSpec(
            num_scalar_prefetch=1,
            grid=(slot // rows,),
            in_specs=[
                pl.BlockSpec((rows, width), lambda j, s: (j, 0)),
                pl.BlockSpec((slot, 2 * HD), lambda j, s: (0, 0)),
                pl.BlockSpec((rows, width), lambda j, s: (j, 0)),
                pl.BlockSpec((rows, HD), lambda j, s: (j, 0)),
                pl.BlockSpec((slot, HD), lambda j, s: (0, 0)),
                pl.BlockSpec((slot, HD), lambda j, s: (0, 0)),
                pl.BlockSpec((rows, 2 * HD), lambda j, s: (0, 0)),
            ],
            out_specs=[
                pl.BlockSpec((rows, width), lambda j, s: (j, 0)),
                pl.BlockSpec((slot, 2 * HD), lambda j, s: (0, 0)),
            ],
            scratch_shapes=[pltpu.VMEM((slot, HD), f32), pltpu.VMEM((slot, HD), f32)],
        ),
        out_shape=(
            jax.ShapeDtypeStruct((slot, width), bf16),
            jax.ShapeDtypeStruct((slot, 2 * HD), bf16),
        ),
        compiler_params=pltpu.CompilerParams(
            dimension_semantics=("arbitrary",), vmem_limit_bytes=VMEM_LIMIT
        ),
        cost_estimate=pl.CostEstimate(
            flops=10 * half, bytes_accessed=8 * 2**20, transcendentals=slot * slot * heads
        ),
    )(where, qr, kvt, dmixed, lse, cos2, sin2, shared)


def inverse_norm(values):
    return lax.rsqrt(jnp.mean(values * values, axis=-1, keepdims=True) + eps)


def rows_of(array, j, rows):
    return array[j * rows : (j + 1) * rows]


def on_device(
    layer_input,
    lengths,
    w_query,
    w_keyvalue,
    w_project,
    w_gate,
    w_up,
    w_down,
    gain_attn,
    gain_mlp,
    out_grad,
    kv_grad,
):
    rows, model_width = layer_input.shape
    ranks = lax.axis_size("tensor")
    rank = lax.axis_index("tensor").astype(jnp.int32)
    length = lengths[0]
    heads_width = w_query.shape[1]
    ff = w_gate.shape[1]
    cut = -(-ff // 256) * 128
    parts = ((0, cut), (cut, ff))

    order = jnp.bitwise_xor(rank, jnp.arange(ranks, dtype=jnp.int32))
    position = (order[:, None] * rows + jnp.arange(rows, dtype=jnp.int32)[None, :]).reshape(-1)
    frequency = rope_base ** (-(jnp.arange(HD // 2, dtype=f32) * 2.0 / HD))
    angles = position.astype(f32)[:, None] * frequency[None, :]
    cosine, sine = jnp.cos(angles), jnp.sin(angles)
    cos2 = jnp.concatenate([cosine, cosine], axis=1)
    sin2 = jnp.concatenate([-sine, sine], axis=1)
    own_mask = (position[:rows] < length).astype(f32)[:, None]
    where = jnp.stack([rank, length])

    gain_one, gain_two = gain_attn.astype(f32)[:, None], gain_mlp.astype(f32)[:, None]
    qkv_own = jnp.concatenate([w_query, w_keyvalue], axis=1).astype(f32)
    shard_rows = qkv_own.shape[0]
    kv_rows = shard_rows // ranks
    scaled_own = (qkv_own * gain_one).astype(bf16)
    kv_part = lax.dynamic_slice_in_dim(scaled_own[:, heads_width:], rank * kv_rows, kv_rows)
    attn_shard = jnp.concatenate(
        [scaled_own[:, :heads_width], w_project.T, kv_part.reshape(-1, heads_width)], axis=0
    )
    pair_own = [
        jnp.concatenate([w_gate[:, a:b], w_up[:, a:b]], axis=1).astype(f32) for a, b in parts
    ]
    ff_shards = [
        jnp.concatenate([(own * gain_two).astype(bf16), w_down[a:b].T], axis=1)
        for (a, b), own in zip(parts, pair_own)
    ]

    residual = layer_input.astype(f32)
    near = near_blocks(layer_input)
    inputs = all_blocks(layer_input, near)
    attn_full = gather_dp(attn_shard)
    ff_full = [gather_dp(after(ff_shards[0], *inputs))]
    attn_full = attn_full.reshape(-1, *attn_shard.shape)
    query_full = attn_full[:, :shard_rows].reshape(model_width, heads_width)
    project_full = attn_full[:, shard_rows : 2 * shard_rows].reshape(model_width, heads_width)
    kv_part = attn_full[:, 2 * shard_rows :].reshape(-1, 2 * HD)
    kv_near = near_blocks(kv_part)
    kv_blocks = jnp.concatenate(all_blocks(kv_part, kv_near), axis=0)
    kv_blocks = kv_blocks.reshape(ranks, -1, kv_rows, 2 * HD)
    keyvalue_full = jnp.stack([pick(kv_blocks, order[j], 0) for j in range(ranks)], axis=1)
    qkv_full = jnp.concatenate([query_full, keyvalue_full.reshape(model_width, 2 * HD)], axis=1)
    top = out_grad.astype(f32) * own_mask
    top_own = after(top.astype(bf16), keyvalue_full)
    top_near = near_blocks(top_own)

    def norm(block):
        block = block.astype(f32)
        return (block * inverse_norm(block)).astype(bf16)

    normed_one = jnp.concatenate([norm(b) for b in inputs], axis=0)
    qkv = dot(normed_one, qkv_full, 1, 0)
    qr, kvt, mixed, lse = attend(where, qkv, cos2, sin2, rows)
    ff_full.append(gather_dp(after(ff_shards[1], mixed)))
    mixed_rest = dot(after(mixed[rows:], *top_near), project_full, 1, 1).astype(bf16)
    mixed_sent = send_sums(mixed_rest)
    top_near = [after(block, *mixed_sent) for block in top_near]
    top_all = jnp.concatenate(all_blocks(top_own, top_near), axis=0)
    after_attn = residual + finish_sums(
        dot(mixed[:rows], project_full, 1, 1), mixed_rest, mixed_sent
    )

    inv_two = inverse_norm(after_attn)
    unit_two = after_attn * inv_two
    normed_own = after(unit_two.astype(bf16), top_all)
    pairs = [full[:, : 2 * (b - a)] for (a, b), full in zip(parts, ff_full)]
    downs = [full[:, 2 * (b - a) :] for (a, b), full in zip(parts, ff_full)]
    first_grad = dot(top_all, downs[0], 1, 0)
    normed_near = [after(block, first_grad) for block in near_blocks(normed_own)]
    normed_two = jnp.concatenate(all_blocks(normed_own, normed_near), axis=0)

    def feed(normed, pair, grad):
        width = grad.shape[1]
        both = dot(after(normed, grad), pair, 1, 0)
        gate, up = both[:, :width], both[:, width:]
        sig = jax.nn.sigmoid(gate)
        hidden = (gate * sig * up).astype(bf16)
        gate_grad = (grad * up * sig * (1.0 + gate * (1.0 - sig))).astype(bf16)
        up_grad = (grad * gate * sig).astype(bf16)
        return hidden, jnp.concatenate([gate_grad, up_grad], axis=1)

    def partial(hidden, grads):
        return jnp.concatenate(
            [
                dot(normed_two, grads, 0, 0).astype(bf16),
                dot(top_all, hidden, 0, 0).astype(bf16),
            ],
            axis=1,
        )

    hidden0, grads0 = feed(normed_two, pairs[0], first_grad)
    partial0 = partial(hidden0, grads0)
    rest0 = dot(after(grads0[rows:], partial0), pairs[0], 1, 1)
    hidden1, grads1 = feed(after(normed_two, rest0), pairs[1], dot(top_all, downs[1], 1, 0))
    rest = (rest0 + dot(grads1[rows:], pairs[1], 1, 1)).astype(bf16)
    rest_sent = send_sums(rest)
    partial1 = partial(after(hidden1, rest), after(grads1, rest))
    ff_sums = [scatter_dp(partial0), scatter_dp(partial1)]
    own = dot(after(grads0[:rows], partial1), pairs[0], 1, 1) + dot(grads1[:rows], pairs[1], 1, 1)
    scaled = finish_sums(own, rest, rest_sent)
    attn_top = top + inv_two * (
        scaled - unit_two * jnp.mean(scaled * unit_two, axis=-1, keepdims=True)
    )
    attn_top_own = attn_top.astype(bf16)
    attn_top_blocks = all_blocks(attn_top_own, near_blocks(attn_top_own))
    attn_top_all = jnp.concatenate(attn_top_blocks, axis=0)
    hidden = [hidden0, hidden1]
    down_rest = sum(dot(h[rows:], w, 1, 1) for h, w in zip(hidden, downs)).astype(bf16)
    down_rest = after(down_rest, *attn_top_blocks)

    mixed_grad = dot(after(attn_top_all, down_rest, ff_sums[0]), project_full, 1, 0).astype(bf16)
    shared = kv_grad.astype(f32) * own_mask
    query_grad, kv_back = attend_back(
        where, qr, kvt, mixed_grad, lse, cos2, sin2, shared, rows
    )
    down_sent = [after(block, query_grad) for block in send_sums(down_rest)]
    qkv_back = after(jnp.concatenate([query_grad, kv_back], axis=1), *down_sent)
    kv_grads = dot(normed_one, qkv_back[:, heads_width:], 0, 0).astype(bf16)
    kv_grads = kv_grads.reshape(-1, ranks, kv_rows, 2 * HD)
    kv_own, *kv_rest = (pick(kv_grads, order[j], 1).reshape(-1, 2 * HD) for j in range(ranks))
    kv_rest = jnp.concatenate(kv_rest, axis=0)
    kv_sent = send_sums(kv_rest)
    qkv_rest = dot(after(qkv_back[rows:], kv_rest), qkv_full, 1, 1).astype(bf16)
    qkv_sent = send_sums(after(qkv_rest, *kv_sent, ff_sums[1]))
    query_back = after(qkv_back[:, :heads_width], qkv_rest)
    kv_sum = finish_sums(kv_own.astype(f32), kv_rest, kv_sent).astype(bf16)
    attn_partial = jnp.concatenate(
        [
            dot(normed_one, query_back, 0, 0).astype(bf16).reshape(-1, shard_rows, heads_width),
            dot(attn_top_all, mixed, 0, 0).astype(bf16).reshape(-1, shard_rows, heads_width),
            kv_sum.reshape(model_width // shard_rows, -1, heads_width),
        ],
        axis=1,
    ).reshape(-1, heads_width)
    attn_sum = scatter_dp(attn_partial)
    down_sent = [after(block, *kv_sent) for block in down_sent]
    own_down = sum(
        dot(after(h[:rows], attn_partial), w, 1, 1) for h, w in zip(hidden, downs)
    )
    after_mlp = after_attn + finish_sums(own_down, down_rest, down_sent)
    output = (after_mlp * own_mask).astype(bf16)
    scaled_one = finish_sums(dot(qkv_back[:rows], qkv_full, 1, 1), qkv_rest, qkv_sent)
    inv_one = inverse_norm(residual)
    unit_one = residual * inv_one
    input_grad = attn_top + inv_one * (
        scaled_one - unit_one * jnp.mean(scaled_one * unit_one, axis=-1, keepdims=True)
    )

    query_sum, project_sum = attn_sum[:shard_rows], attn_sum[shard_rows : 2 * shard_rows]
    kv_sum = attn_sum[2 * shard_rows :].reshape(kv_rows, 2 * HD)
    pair_sums = [total[:, : own.shape[1]] for own, total in zip(pair_own, ff_sums)]
    down_sum = jnp.concatenate(
        [total[:, own.shape[1] :] for own, total in zip(pair_own, ff_sums)], axis=1
    )
    gain_two_part = sum(
        jnp.sum(own * total, axis=1, keepdims=True) for own, total in zip(pair_own, pair_sums)
    )
    scaled_sums = [total * gain_two for total in pair_sums]
    grad_gate = jnp.concatenate([s[:, : b - a] for (a, b), s in zip(parts, scaled_sums)], axis=1)
    grad_up = jnp.concatenate([s[:, b - a :] for (a, b), s in zip(parts, scaled_sums)], axis=1)
    query_part = jnp.sum(qkv_own[:, :heads_width] * query_sum, axis=1, keepdims=True)
    kv_here = lax.dynamic_slice_in_dim(qkv_own[:, heads_width:], rank * kv_rows, kv_rows)
    gain_here = lax.dynamic_slice_in_dim(gain_one, rank * kv_rows, kv_rows)
    small = jnp.concatenate(
        [
            kv_sum * gain_here,
            jnp.sum(kv_here * kv_sum, axis=1, keepdims=True),
            jnp.concatenate([query_part, gain_two_part], axis=1).reshape(kv_rows, -1),
        ],
        axis=1,
    )
    blocks = jnp.stack([small] + [hop(small, j) for j in range(1, ranks)], axis=0)
    sums = jnp.sum(blocks[:, :, 2 * HD + 1 :], axis=0).reshape(shard_rows, 2)
    placed = jnp.concatenate([pick(blocks, order[j], 0) for j in range(ranks)], axis=0)
    return (
        output,
        input_grad,
        query_sum * gain_one,
        placed[:, : 2 * HD],
        project_sum.T,
        grad_gate,
        grad_up,
        down_sum.T,
        sums[:, 0] + placed[:, 2 * HD],
        sums[:, 1],
    )


def solution(mesh):
    placed = (
        P(("dp", "tensor"), None),
        P("dp"),
        P("dp", "tensor"),
        P("dp", None),
        P("tensor", "dp"),
        P("dp", "tensor"),
        P("dp", "tensor"),
        P("tensor", "dp"),
        P("dp"),
        P("dp"),
        P(("dp", "tensor"), None),
        P(("dp", "tensor"), None),
    )
    return jax.shard_map(
        on_device,
        mesh=mesh,
        in_specs=placed,
        out_specs=(
            P(("dp", "tensor"), None),
            P(("dp", "tensor"), None),
            P("dp", "tensor"),
            P("dp", None),
            P("tensor", "dp"),
            P("dp", "tensor"),
            P("dp", "tensor"),
            P("tensor", "dp"),
            P("dp"),
            P("dp"),
        ),
        check_vma=False,
    )
```

```python
import functools
import math

import jax
import jax.numpy as jnp
from jax import lax
from jax.experimental import pallas as pl
from jax.experimental.pallas import tpu as pltpu
from jax.sharding import PartitionSpec as P

HD = 128
eps = 1e-05
rope_base = 10000.0
neg_big = -1e30
inv_root = 1.0 / math.sqrt(HD)
f32 = jnp.float32
bf16 = jnp.bfloat16


def dot(a, b, ca, cb):
    return lax.dot_general(a, b, (((ca,), (cb,)), ((), ())), preferred_element_type=f32)


def hop(value, step):
    size = lax.axis_size("tensor")
    return lax.ppermute(value, "tensor", [(i, i ^ step) for i in range(size)])


def after(value, *others):
    return lax.optimization_barrier((value, *others))[0]


def near_blocks(own):
    size = lax.axis_size("tensor")
    return [hop(own, j) for j in range(1, 3 if size == 4 else size)]


def all_blocks(own, near):
    if lax.axis_size("tensor") != 4:
        return [own, *near]
    half = own.shape[0] // 2
    one, two = near
    return [own, one, two, hop(two[:half], 1), hop(one[half:], 2)]


def send_sums(rest):
    size = lax.axis_size("tensor")
    rows = rest.shape[0] // (size - 1)
    one, *others = (rows_of(rest, j, rows) for j in range(size - 1))
    if size != 4:
        return [hop(block, j + 1) for j, block in enumerate([one, *others])]
    two, three = others
    half = rows // 2
    return [
        hop(jnp.concatenate([one[:half], three[:half]], axis=0), 1),
        hop(jnp.concatenate([two[half:], three[half:]], axis=0), 2),
    ]


def finish_sums(own, rest, arrived):
    arrived = [block.astype(f32) for block in arrived]
    if lax.axis_size("tensor") != 4:
        return own + sum(arrived)
    rows = own.shape[0]
    half = rows // 2
    one, two = rows_of(rest, 0, rows), rows_of(rest, 1, rows)
    upper, lower = arrived
    upper_far = hop((two[:half].astype(f32) + upper[half:]).astype(bf16), 2).astype(f32)
    lower_near = hop((one[half:].astype(f32) + lower[half:]).astype(bf16), 1).astype(f32)
    return jnp.concatenate(
        [own[:half] + upper[:half] + upper_far, own[half:] + lower[:half] + lower_near], axis=0
    )


def gather_dp(shard):
    return lax.all_gather(shard, "dp", axis=0, tiled=True)


def scatter_dp(partial):
    return lax.psum_scatter(partial, "dp", scatter_dimension=0, tiled=True).astype(f32)


pick = functools.partial(lax.dynamic_index_in_dim, keepdims=False)


def turn(u, cos2, sin2):
    return u * cos2 + pltpu.roll(u, HD // 2, 1) * sin2


def attend_kernel(where_ref, q_ref, kv_ref, cos_ref, sin_ref, qr_ref, kvt_ref, mixed_ref, lse_ref):
    rows, width = q_ref.shape
    heads = width // HD
    ranks = kv_ref.shape[0] // rows
    j = pl.program_id(0)
    rank, length = where_ref[0], where_ref[1]
    block = jnp.bitwise_xor(rank, j)

    @pl.when(j == 0)
    def _():
        for i in range(ranks):
            here = slice(i * rows, (i + 1) * rows)
            there = pl.ds(pl.multiple_of(jnp.bitwise_xor(rank, i) * rows, rows), rows)
            key = turn(kv_ref[here, :HD], cos_ref[here, :], sin_ref[here, :])
            kvt_ref[there, :HD] = key.astype(bf16)
            kvt_ref[there, HD:] = kv_ref[here, HD:].astype(bf16)

    mine = pl.ds(pl.multiple_of(j * rows, rows), rows)
    cos2, sin2 = cos_ref[mine, :], sin_ref[mine, :]
    for h in range(heads):
        head = slice(h * HD, (h + 1) * HD)
        qr_ref[:, head] = turn(q_ref[:, head], cos2, sin2).astype(bf16)
    limit = jnp.minimum(block * rows + lax.broadcasted_iota(jnp.int32, (rows, 1), 0), length - 1)
    for w in range(ranks):

        @pl.when(block == w)
        def _(w=w):
            span = (w + 1) * rows
            allowed = lax.broadcasted_iota(jnp.int32, (rows, span), 1) <= limit
            for h in range(heads):
                head = slice(h * HD, (h + 1) * HD)
                scores = dot(qr_ref[:, head], kvt_ref[:span, :HD], 1, 1) * inv_root
                scores = jnp.where(allowed, scores, neg_big)
                top = jnp.max(scores, axis=1, keepdims=True)
                weights = jnp.exp(scores - top)
                total = jnp.sum(weights, axis=1, keepdims=True)
                probs = (weights * (1.0 / total)).astype(bf16)
                mixed_ref[:, head] = dot(probs, kvt_ref[:span, HD:], 1, 0).astype(bf16)
                lse_ref[:, h : h + 1] = top + jnp.log(total)


def attend_back_kernel(
    where_ref,
    qr_ref,
    kvt_ref,
    dm_ref,
    lse_ref,
    cos_ref,
    sin_ref,
    shared_ref,
    dq_ref,
    dkv_ref,
    dk_acc,
    dv_acc,
):
    rows, width = qr_ref.shape
    heads = width // HD
    ranks = kvt_ref.shape[0] // rows
    j = pl.program_id(0)
    rank, length = where_ref[0], where_ref[1]
    block = jnp.bitwise_xor(rank, j)

    @pl.when(j == 0)
    def _():
        dk_acc[...] = jnp.zeros_like(dk_acc)
        dv_acc[...] = jnp.zeros_like(dv_acc)

    mine = pl.ds(pl.multiple_of(j * rows, rows), rows)
    cos2, sin2 = cos_ref[mine, :], sin_ref[mine, :]
    limit = jnp.minimum(block * rows + lax.broadcasted_iota(jnp.int32, (rows, 1), 0), length - 1)
    for w in range(ranks):

        @pl.when(block == w)
        def _(w=w):
            span = (w + 1) * rows
            allowed = lax.broadcasted_iota(jnp.int32, (rows, span), 1) <= limit
            keys, vals = kvt_ref[:span, :HD], kvt_ref[:span, HD:]
            for h in range(heads):
                head = slice(h * HD, (h + 1) * HD)
                q, dm = qr_ref[:, head], dm_ref[:, head]
                scores = jnp.where(allowed, dot(q, keys, 1, 1) * inv_root, neg_big)
                probs = jnp.exp(scores - lse_ref[:, h : h + 1])
                dp = dot(dm, vals, 1, 1)
                center = jnp.sum(probs * dp, axis=1, keepdims=True)
                ds = (probs * (dp - center)).astype(bf16)
                dq = dot(ds, keys, 1, 0) * inv_root
                dq_ref[:, head] = turn(dq, cos2, -sin2).astype(bf16)
                dk_acc[:span, :] += dot(ds, q, 0, 0)
                dv_acc[:span, :] += dot(probs.astype(bf16), dm, 0, 0)

    @pl.when(j == ranks - 1)
    def _():
        for i in range(ranks):
            here = slice(i * rows, (i + 1) * rows)
            there = pl.ds(pl.multiple_of(jnp.bitwise_xor(rank, i) * rows, rows), rows)
            dk, dv = dk_acc[there, :] * inv_root, dv_acc[there, :]
            if i == 0:
                dk, dv = dk + shared_ref[:, :HD], dv + shared_ref[:, HD:]
            dkv_ref[here, :HD] = turn(dk, cos_ref[here, :], -sin_ref[here, :]).astype(bf16)
            dkv_ref[here, HD:] = dv.astype(bf16)


VMEM_LIMIT = 48 * 2**20


def attend(where, qkv, cos2, sin2, rows):
    slot, width = qkv.shape[0], qkv.shape[1] - 2 * HD
    heads = width // HD
    half = slot * slot * heads * HD
    return pl.pallas_call(
        attend_kernel,
        name="attend",
        grid_spec=pltpu.PrefetchScalarGridSpec(
            num_scalar_prefetch=1,
            grid=(slot // rows,),
            in_specs=[
                pl.BlockSpec((rows, width), lambda j, s: (j, 0)),
                pl.BlockSpec((slot, 2 * HD), lambda j, s: (0, width // (2 * HD))),
                pl.BlockSpec((slot, HD), lambda j, s: (0, 0)),
                pl.BlockSpec((slot, HD), lambda j, s: (0, 0)),
            ],
            out_specs=[
                pl.BlockSpec((rows, width), lambda j, s: (j, 0)),
                pl.BlockSpec((slot, 2 * HD), lambda j, s: (0, 0)),
                pl.BlockSpec((rows, width), lambda j, s: (j, 0)),
                pl.BlockSpec((rows, HD), lambda j, s: (j, 0)),
            ],
        ),
        out_shape=(
            jax.ShapeDtypeStruct((slot, width), bf16),
            jax.ShapeDtypeStruct((slot, 2 * HD), bf16),
            jax.ShapeDtypeStruct((slot, width), bf16),
            jax.ShapeDtypeStruct((slot, HD), f32),
        ),
        compiler_params=pltpu.CompilerParams(
            dimension_semantics=("arbitrary",), vmem_limit_bytes=VMEM_LIMIT
        ),
        cost_estimate=pl.CostEstimate(
            flops=4 * half, bytes_accessed=8 * 2**20, transcendentals=slot * slot * heads
        ),
    )(where, qkv, qkv, cos2, sin2)


def attend_back(where, qr, kvt, dmixed, lse, cos2, sin2, shared, rows):
    slot, width = qr.shape
    heads = width // HD
    half = slot * slot * heads * HD
    return pl.pallas_call(
        attend_back_kernel,
        name="attend_back",
        grid_spec=pltpu.PrefetchScalarGridSpec(
            num_scalar_prefetch=1,
            grid=(slot // rows,),
            in_specs=[
                pl.BlockSpec((rows, width), lambda j, s: (j, 0)),
                pl.BlockSpec((slot, 2 * HD), lambda j, s: (0, 0)),
                pl.BlockSpec((rows, width), lambda j, s: (j, 0)),
                pl.BlockSpec((rows, HD), lambda j, s: (j, 0)),
                pl.BlockSpec((slot, HD), lambda j, s: (0, 0)),
                pl.BlockSpec((slot, HD), lambda j, s: (0, 0)),
                pl.BlockSpec((rows, 2 * HD), lambda j, s: (0, 0)),
            ],
            out_specs=[
                pl.BlockSpec((rows, width), lambda j, s: (j, 0)),
                pl.BlockSpec((slot, 2 * HD), lambda j, s: (0, 0)),
            ],
            scratch_shapes=[pltpu.VMEM((slot, HD), f32), pltpu.VMEM((slot, HD), f32)],
        ),
        out_shape=(
            jax.ShapeDtypeStruct((slot, width), bf16),
            jax.ShapeDtypeStruct((slot, 2 * HD), bf16),
        ),
        compiler_params=pltpu.CompilerParams(
            dimension_semantics=("arbitrary",), vmem_limit_bytes=VMEM_LIMIT
        ),
        cost_estimate=pl.CostEstimate(
            flops=10 * half, bytes_accessed=8 * 2**20, transcendentals=slot * slot * heads
        ),
    )(where, qr, kvt, dmixed, lse, cos2, sin2, shared)


def inverse_norm(values):
    return lax.rsqrt(jnp.mean(values * values, axis=-1, keepdims=True) + eps)


def rows_of(array, j, rows):
    return array[j * rows : (j + 1) * rows]


def on_device(
    layer_input,
    lengths,
    w_query,
    w_keyvalue,
    w_project,
    w_gate,
    w_up,
    w_down,
    gain_attn,
    gain_mlp,
    out_grad,
    kv_grad,
):
    rows, model_width = layer_input.shape
    ranks = lax.axis_size("tensor")
    rank = lax.axis_index("tensor").astype(jnp.int32)
    length = lengths[0]
    heads_width = w_query.shape[1]
    ff = w_gate.shape[1]
    cut = -(-ff // 256) * 128
    parts = ((0, cut), (cut, ff))

    order = jnp.bitwise_xor(rank, jnp.arange(ranks, dtype=jnp.int32))
    position = (order[:, None] * rows + jnp.arange(rows, dtype=jnp.int32)[None, :]).reshape(-1)
    frequency = rope_base ** (-(jnp.arange(HD // 2, dtype=f32) * 2.0 / HD))
    angles = position.astype(f32)[:, None] * frequency[None, :]
    cosine, sine = jnp.cos(angles), jnp.sin(angles)
    cos2 = jnp.concatenate([cosine, cosine], axis=1)
    sin2 = jnp.concatenate([-sine, sine], axis=1)
    own_mask = (position[:rows] < length).astype(f32)[:, None]
    where = jnp.stack([rank, length])

    gain_one, gain_two = gain_attn.astype(f32)[:, None], gain_mlp.astype(f32)[:, None]
    qkv_own = jnp.concatenate([w_query, w_keyvalue], axis=1).astype(f32)
    shard_rows = qkv_own.shape[0]
    kv_rows = shard_rows // ranks
    scaled_own = (qkv_own * gain_one).astype(bf16)
    kv_part = lax.dynamic_slice_in_dim(scaled_own[:, heads_width:], rank * kv_rows, kv_rows)
    attn_shard = jnp.concatenate(
        [scaled_own[:, :heads_width], w_project.T, kv_part.reshape(-1, heads_width)], axis=0
    )
    pair_own = [
        jnp.concatenate([w_gate[:, a:b], w_up[:, a:b]], axis=1).astype(f32) for a, b in parts
    ]
    ff_shards = [
        jnp.concatenate([(own * gain_two).astype(bf16), w_down[a:b].T], axis=1)
        for (a, b), own in zip(parts, pair_own)
    ]

    residual = layer_input.astype(f32)
    near = near_blocks(layer_input)
    inputs = all_blocks(layer_input, near)
    attn_full = gather_dp(attn_shard)

    def norm(block):
        block = block.astype(f32)
        return (block * inverse_norm(block)).astype(bf16)

    normed_one = jnp.concatenate([norm(b) for b in inputs], axis=0)
    top = out_grad.astype(f32) * own_mask
    ready = normed_one, ff_shards[1], top.astype(bf16), cos2, sin2
    ff_full = [gather_dp(after(ff_shards[0], *ready))]
    attn_full = attn_full.reshape(-1, *attn_shard.shape)
    query_full = attn_full[:, :shard_rows].reshape(model_width, heads_width)
    project_full = attn_full[:, shard_rows : 2 * shard_rows].reshape(model_width, heads_width)
    kv_part = attn_full[:, 2 * shard_rows :].reshape(-1, 2 * HD)
    kv_near = near_blocks(kv_part)
    kv_blocks = jnp.concatenate(all_blocks(kv_part, kv_near), axis=0)
    kv_blocks = kv_blocks.reshape(ranks, -1, kv_rows, 2 * HD)
    keyvalue_full = jnp.stack([pick(kv_blocks, order[j], 0) for j in range(ranks)], axis=1)
    qkv_full = jnp.concatenate([query_full, keyvalue_full.reshape(model_width, 2 * HD)], axis=1)
    top_own = after(top.astype(bf16), keyvalue_full)
    top_near = near_blocks(top_own)
    qkv = dot(normed_one, qkv_full, 1, 0)
    qr, kvt, mixed, lse = attend(where, qkv, cos2, sin2, rows)
    ff_full.append(gather_dp(after(ff_shards[1], mixed)))
    mixed_rest = dot(after(mixed[rows:], *top_near), project_full, 1, 1).astype(bf16)
    mixed_sent = send_sums(mixed_rest)
    top_near = [after(block, *mixed_sent) for block in top_near]
    top_all = jnp.concatenate(all_blocks(top_own, top_near), axis=0)
    after_attn = residual + finish_sums(
        dot(mixed[:rows], project_full, 1, 1), mixed_rest, mixed_sent
    )

    inv_two = inverse_norm(after_attn)
    unit_two = after_attn * inv_two
    normed_own = after(unit_two.astype(bf16), top_all)
    pairs = [full[:, : 2 * (b - a)] for (a, b), full in zip(parts, ff_full)]
    downs = [full[:, 2 * (b - a) :] for (a, b), full in zip(parts, ff_full)]
    first_grad = dot(top_all, downs[0], 1, 0)
    normed_near = [after(block, first_grad) for block in near_blocks(normed_own)]
    normed_two = jnp.concatenate(all_blocks(normed_own, normed_near), axis=0)

    def feed(normed, pair, grad):
        width = grad.shape[1]
        both = dot(after(normed, grad), pair, 1, 0)
        gate, up = both[:, :width], both[:, width:]
        sig = jax.nn.sigmoid(gate)
        hidden = (gate * sig * up).astype(bf16)
        gate_grad = (grad * up * sig * (1.0 + gate * (1.0 - sig))).astype(bf16)
        up_grad = (grad * gate * sig).astype(bf16)
        return hidden, jnp.concatenate([gate_grad, up_grad], axis=1)

    def partial(hidden, grads):
        return jnp.concatenate(
            [
                dot(normed_two, grads, 0, 0).astype(bf16),
                dot(top_all, hidden, 0, 0).astype(bf16),
            ],
            axis=1,
        )

    hidden0, grads0 = feed(normed_two, pairs[0], first_grad)
    partial0 = partial(hidden0, grads0)
    rest0 = dot(after(grads0[rows:], partial0), pairs[0], 1, 1)
    hidden1, grads1 = feed(after(normed_two, rest0), pairs[1], dot(top_all, downs[1], 1, 0))
    rest = (rest0 + dot(grads1[rows:], pairs[1], 1, 1)).astype(bf16)
    rest_sent = send_sums(rest)
    partial1 = partial(after(hidden1, *rest_sent), after(grads1, *rest_sent))
    ff_sums = [scatter_dp(partial0), scatter_dp(partial1)]
    own = dot(after(grads0[:rows], partial1), pairs[0], 1, 1) + dot(grads1[:rows], pairs[1], 1, 1)
    scaled = finish_sums(own, rest, rest_sent)
    attn_top = top + inv_two * (
        scaled - unit_two * jnp.mean(scaled * unit_two, axis=-1, keepdims=True)
    )
    attn_top_own = attn_top.astype(bf16)
    attn_top_blocks = all_blocks(attn_top_own, near_blocks(attn_top_own))
    attn_top_all = jnp.concatenate(attn_top_blocks, axis=0)
    hidden = [hidden0, hidden1]
    down_rest = sum(dot(h[rows:], w, 1, 1) for h, w in zip(hidden, downs)).astype(bf16)
    down_rest = after(down_rest, *attn_top_blocks)

    mixed_grad = dot(after(attn_top_all, down_rest, ff_sums[0]), project_full, 1, 0).astype(bf16)
    shared = kv_grad.astype(f32) * own_mask
    query_grad, kv_back = attend_back(
        where, qr, kvt, mixed_grad, lse, cos2, sin2, shared, rows
    )
    down_sent = [after(block, query_grad) for block in send_sums(down_rest)]
    qkv_back = after(jnp.concatenate([query_grad, kv_back], axis=1), *down_sent)
    kv_grads = dot(normed_one, qkv_back[:, heads_width:], 0, 0).astype(bf16)
    kv_grads = kv_grads.reshape(-1, ranks, kv_rows, 2 * HD)
    kv_own, *kv_rest = (pick(kv_grads, order[j], 1).reshape(-1, 2 * HD) for j in range(ranks))
    kv_rest = jnp.concatenate(kv_rest, axis=0)
    kv_sent = send_sums(kv_rest)
    qkv_rest = dot(after(qkv_back[rows:], kv_rest), qkv_full, 1, 1).astype(bf16)
    qkv_sent = send_sums(after(qkv_rest, *kv_sent, ff_sums[1]))
    query_back = after(qkv_back[:, :heads_width], qkv_rest)
    kv_sum = finish_sums(kv_own.astype(f32), kv_rest, kv_sent).astype(bf16)
    attn_partial = jnp.concatenate(
        [
            dot(normed_one, query_back, 0, 0).astype(bf16).reshape(-1, shard_rows, heads_width),
            dot(attn_top_all, mixed, 0, 0).astype(bf16).reshape(-1, shard_rows, heads_width),
            kv_sum.reshape(model_width // shard_rows, -1, heads_width),
        ],
        axis=1,
    ).reshape(-1, heads_width)
    attn_sum = scatter_dp(attn_partial)
    down_sent = [after(block, *kv_sent) for block in down_sent]
    own_down = sum(
        dot(after(h[:rows], attn_partial), w, 1, 1) for h, w in zip(hidden, downs)
    )
    after_mlp = after_attn + finish_sums(own_down, down_rest, down_sent)
    output = (after_mlp * own_mask).astype(bf16)
    scaled_one = finish_sums(dot(qkv_back[:rows], qkv_full, 1, 1), qkv_rest, qkv_sent)
    inv_one = inverse_norm(residual)
    unit_one = residual * inv_one
    input_grad = attn_top + inv_one * (
        scaled_one - unit_one * jnp.mean(scaled_one * unit_one, axis=-1, keepdims=True)
    )

    query_sum, project_sum = attn_sum[:shard_rows], attn_sum[shard_rows : 2 * shard_rows]
    kv_sum = attn_sum[2 * shard_rows :].reshape(kv_rows, 2 * HD)
    ff_sums = [after(total, *qkv_sent) for total in ff_sums]
    pair_sums = [total[:, : own.shape[1]] for own, total in zip(pair_own, ff_sums)]
    down_sum = jnp.concatenate(
        [total[:, own.shape[1] :] for own, total in zip(pair_own, ff_sums)], axis=1
    )
    gain_two_part = sum(
        jnp.sum(own * total, axis=1, keepdims=True) for own, total in zip(pair_own, pair_sums)
    )
    scaled_sums = [total * gain_two for total in pair_sums]
    grad_gate = jnp.concatenate([s[:, : b - a] for (a, b), s in zip(parts, scaled_sums)], axis=1)
    grad_up = jnp.concatenate([s[:, b - a :] for (a, b), s in zip(parts, scaled_sums)], axis=1)
    query_part = jnp.sum(qkv_own[:, :heads_width] * query_sum, axis=1, keepdims=True)
    kv_here = lax.dynamic_slice_in_dim(qkv_own[:, heads_width:], rank * kv_rows, kv_rows)
    gain_here = lax.dynamic_slice_in_dim(gain_one, rank * kv_rows, kv_rows)
    small = jnp.concatenate(
        [
            kv_sum * gain_here,
            jnp.sum(kv_here * kv_sum, axis=1, keepdims=True),
            jnp.concatenate([query_part, gain_two_part], axis=1).reshape(kv_rows, -1),
        ],
        axis=1,
    )
    blocks = jnp.stack([small] + [hop(small, j) for j in range(1, ranks)], axis=0)
    sums = jnp.sum(blocks[:, :, 2 * HD + 1 :], axis=0).reshape(shard_rows, 2)
    placed = jnp.concatenate([pick(blocks, order[j], 0) for j in range(ranks)], axis=0)
    return (
        output,
        input_grad,
        query_sum * gain_one,
        placed[:, : 2 * HD],
        project_sum.T,
        grad_gate,
        grad_up,
        down_sum.T,
        sums[:, 0] + placed[:, 2 * HD],
        sums[:, 1],
    )


def solution(mesh):
    placed = (
        P(("dp", "tensor"), None),
        P("dp"),
        P("dp", "tensor"),
        P("dp", None),
        P("tensor", "dp"),
        P("dp", "tensor"),
        P("dp", "tensor"),
        P("tensor", "dp"),
        P("dp"),
        P("dp"),
        P(("dp", "tensor"), None),
        P(("dp", "tensor"), None),
    )
    return jax.shard_map(
        on_device,
        mesh=mesh,
        in_specs=placed,
        out_specs=(
            P(("dp", "tensor"), None),
            P(("dp", "tensor"), None),
            P("dp", "tensor"),
            P("dp", None),
            P("tensor", "dp"),
            P("dp", "tensor"),
            P("dp", "tensor"),
            P("tensor", "dp"),
            P("dp"),
            P("dp"),
        ),
        check_vma=False,
    )
```

```python
import functools
import math

import jax
import jax.numpy as jnp
from jax import lax
from jax.experimental import pallas as pl
from jax.experimental.pallas import tpu as pltpu
from jax.sharding import PartitionSpec as P

HD = 128
eps = 1e-05
rope_base = 10000.0
neg_big = -1e30
inv_root = 1.0 / math.sqrt(HD)
f32 = jnp.float32
bf16 = jnp.bfloat16


def dot(a, b, ca, cb):
    return lax.dot_general(a, b, (((ca,), (cb,)), ((), ())), preferred_element_type=f32)


def hop(value, step):
    size = lax.axis_size("tensor")
    return lax.ppermute(value, "tensor", [(i, i ^ step) for i in range(size)])


def after(value, *others):
    return lax.optimization_barrier((value, *others))[0]


def near_blocks(own):
    size = lax.axis_size("tensor")
    return [hop(own, j) for j in range(1, 3 if size == 4 else size)]


def all_blocks(own, near):
    if lax.axis_size("tensor") != 4:
        return [own, *near]
    half = own.shape[0] // 2
    one, two = near
    return [own, one, two, hop(two[:half], 1), hop(one[half:], 2)]


def send_sums(rest):
    size = lax.axis_size("tensor")
    rows = rest.shape[0] // (size - 1)
    one, *others = (rows_of(rest, j, rows) for j in range(size - 1))
    if size != 4:
        return [hop(block, j + 1) for j, block in enumerate([one, *others])]
    two, three = others
    half = rows // 2
    return [
        hop(jnp.concatenate([one[:half], three[:half]], axis=0), 1),
        hop(jnp.concatenate([two[half:], three[half:]], axis=0), 2),
    ]


def finish_sums(own, rest, arrived):
    if lax.axis_size("tensor") != 4:
        return own + sum(block.astype(f32) for block in arrived)
    rows = own.shape[0]
    half = rows // 2
    one, two = rows_of(rest, 0, rows), rows_of(rest, 1, rows)
    upper, lower = arrived
    upper_far = hop((two[:half].astype(f32) + upper[half:].astype(f32)).astype(bf16), 2)
    lower_near = hop((one[half:].astype(f32) + lower[half:].astype(f32)).astype(bf16), 1)
    return jnp.concatenate(
        [
            own[:half] + upper[:half].astype(f32) + upper_far.astype(f32),
            own[half:] + lower[:half].astype(f32) + lower_near.astype(f32),
        ],
        axis=0,
    )


def gather_dp(shard):
    return lax.all_gather(shard, "dp", axis=0, tiled=True)


def scatter_dp(partial):
    return lax.psum_scatter(partial, "dp", scatter_dimension=0, tiled=True)


pick = functools.partial(lax.dynamic_index_in_dim, keepdims=False)


def turn(u, cos2, sin2):
    return u * cos2 + pltpu.roll(u, HD // 2, 1) * sin2


def attend_kernel(where_ref, q_ref, kv_ref, cos_ref, sin_ref, qr_ref, kvt_ref, mixed_ref, lse_ref):
    rows, width = q_ref.shape
    heads = width // HD
    ranks = kv_ref.shape[0] // rows
    j = pl.program_id(0)
    rank, length = where_ref[0], where_ref[1]
    block = jnp.bitwise_xor(rank, j)

    @pl.when(j == 0)
    def _():
        for i in range(ranks):
            here = slice(i * rows, (i + 1) * rows)
            there = pl.ds(pl.multiple_of(jnp.bitwise_xor(rank, i) * rows, rows), rows)
            key = turn(kv_ref[here, :HD], cos_ref[here, :], sin_ref[here, :])
            kvt_ref[there, :HD] = key.astype(bf16)
            kvt_ref[there, HD:] = kv_ref[here, HD:].astype(bf16)

    mine = pl.ds(pl.multiple_of(j * rows, rows), rows)
    cos2, sin2 = cos_ref[mine, :], sin_ref[mine, :]
    for h in range(heads):
        head = slice(h * HD, (h + 1) * HD)
        qr_ref[:, head] = turn(q_ref[:, head], cos2, sin2).astype(bf16)
    limit = jnp.minimum(block * rows + lax.broadcasted_iota(jnp.int32, (rows, 1), 0), length - 1)
    for w in range(ranks):

        @pl.when(block == w)
        def _(w=w):
            span = (w + 1) * rows
            allowed = lax.broadcasted_iota(jnp.int32, (rows, span), 1) <= limit
            for h in range(heads):
                head = slice(h * HD, (h + 1) * HD)
                scores = dot(qr_ref[:, head], kvt_ref[:span, :HD], 1, 1) * inv_root
                scores = jnp.where(allowed, scores, neg_big)
                top = jnp.max(scores, axis=1, keepdims=True)
                weights = jnp.exp(scores - top)
                total = jnp.sum(weights, axis=1, keepdims=True)
                probs = (weights * (1.0 / total)).astype(bf16)
                mixed_ref[:, head] = dot(probs, kvt_ref[:span, HD:], 1, 0).astype(bf16)
                lse_ref[:, h : h + 1] = top + jnp.log(total)


def attend_back_kernel(
    where_ref,
    qr_ref,
    kvt_ref,
    dm_ref,
    lse_ref,
    cos_ref,
    sin_ref,
    shared_ref,
    dq_ref,
    dkv_ref,
    dk_acc,
    dv_acc,
):
    rows, width = qr_ref.shape
    heads = width // HD
    ranks = kvt_ref.shape[0] // rows
    j = pl.program_id(0)
    rank, length = where_ref[0], where_ref[1]
    block = jnp.bitwise_xor(rank, j)

    @pl.when(j == 0)
    def _():
        dk_acc[...] = jnp.zeros_like(dk_acc)
        dv_acc[...] = jnp.zeros_like(dv_acc)

    mine = pl.ds(pl.multiple_of(j * rows, rows), rows)
    cos2, sin2 = cos_ref[mine, :], sin_ref[mine, :]
    limit = jnp.minimum(block * rows + lax.broadcasted_iota(jnp.int32, (rows, 1), 0), length - 1)
    for w in range(ranks):

        @pl.when(block == w)
        def _(w=w):
            span = (w + 1) * rows
            allowed = lax.broadcasted_iota(jnp.int32, (rows, span), 1) <= limit
            keys, vals = kvt_ref[:span, :HD], kvt_ref[:span, HD:]
            for h in range(heads):
                head = slice(h * HD, (h + 1) * HD)
                q, dm = qr_ref[:, head], dm_ref[:, head]
                scores = jnp.where(allowed, dot(q, keys, 1, 1) * inv_root, neg_big)
                probs = jnp.exp(scores - lse_ref[:, h : h + 1])
                dp = dot(dm, vals, 1, 1)
                center = jnp.sum(probs * dp, axis=1, keepdims=True)
                ds = (probs * (dp - center)).astype(bf16)
                dq = dot(ds, keys, 1, 0) * inv_root
                dq_ref[:, head] = turn(dq, cos2, -sin2).astype(bf16)
                dk_acc[:span, :] += dot(ds, q, 0, 0)
                dv_acc[:span, :] += dot(probs.astype(bf16), dm, 0, 0)

    @pl.when(j == ranks - 1)
    def _():
        for i in range(ranks):
            here = slice(i * rows, (i + 1) * rows)
            there = pl.ds(pl.multiple_of(jnp.bitwise_xor(rank, i) * rows, rows), rows)
            dk, dv = dk_acc[there, :] * inv_root, dv_acc[there, :]
            if i == 0:
                dk, dv = dk + shared_ref[:, :HD], dv + shared_ref[:, HD:]
            dkv_ref[here, :HD] = turn(dk, cos_ref[here, :], -sin_ref[here, :]).astype(bf16)
            dkv_ref[here, HD:] = dv.astype(bf16)


VMEM_LIMIT = 48 * 2**20


def attend(where, qkv, cos2, sin2, rows):
    slot, width = qkv.shape[0], qkv.shape[1] - 2 * HD
    heads = width // HD
    half = slot * slot * heads * HD
    return pl.pallas_call(
        attend_kernel,
        name="attend",
        grid_spec=pltpu.PrefetchScalarGridSpec(
            num_scalar_prefetch=1,
            grid=(slot // rows,),
            in_specs=[
                pl.BlockSpec((rows, width), lambda j, s: (j, 0)),
                pl.BlockSpec((slot, 2 * HD), lambda j, s: (0, width // (2 * HD))),
                pl.BlockSpec((slot, HD), lambda j, s: (0, 0)),
                pl.BlockSpec((slot, HD), lambda j, s: (0, 0)),
            ],
            out_specs=[
                pl.BlockSpec((rows, width), lambda j, s: (j, 0)),
                pl.BlockSpec((slot, 2 * HD), lambda j, s: (0, 0)),
                pl.BlockSpec((rows, width), lambda j, s: (j, 0)),
                pl.BlockSpec((rows, HD), lambda j, s: (j, 0)),
            ],
        ),
        out_shape=(
            jax.ShapeDtypeStruct((slot, width), bf16),
            jax.ShapeDtypeStruct((slot, 2 * HD), bf16),
            jax.ShapeDtypeStruct((slot, width), bf16),
            jax.ShapeDtypeStruct((slot, HD), f32),
        ),
        compiler_params=pltpu.CompilerParams(
            dimension_semantics=("arbitrary",), vmem_limit_bytes=VMEM_LIMIT
        ),
        cost_estimate=pl.CostEstimate(
            flops=4 * half, bytes_accessed=8 * 2**20, transcendentals=slot * slot * heads
        ),
    )(where, qkv, qkv, cos2, sin2)


def attend_back(where, qr, kvt, dmixed, lse, cos2, sin2, shared, rows):
    slot, width = qr.shape
    heads = width // HD
    half = slot * slot * heads * HD
    return pl.pallas_call(
        attend_back_kernel,
        name="attend_back",
        grid_spec=pltpu.PrefetchScalarGridSpec(
            num_scalar_prefetch=1,
            grid=(slot // rows,),
            in_specs=[
                pl.BlockSpec((rows, width), lambda j, s: (j, 0)),
                pl.BlockSpec((slot, 2 * HD), lambda j, s: (0, 0)),
                pl.BlockSpec((rows, width), lambda j, s: (j, 0)),
                pl.BlockSpec((rows, HD), lambda j, s: (j, 0)),
                pl.BlockSpec((slot, HD), lambda j, s: (0, 0)),
                pl.BlockSpec((slot, HD), lambda j, s: (0, 0)),
                pl.BlockSpec((rows, 2 * HD), lambda j, s: (0, 0)),
            ],
            out_specs=[
                pl.BlockSpec((rows, width), lambda j, s: (j, 0)),
                pl.BlockSpec((slot, 2 * HD), lambda j, s: (0, 0)),
            ],
            scratch_shapes=[pltpu.VMEM((slot, HD), f32), pltpu.VMEM((slot, HD), f32)],
        ),
        out_shape=(
            jax.ShapeDtypeStruct((slot, width), bf16),
            jax.ShapeDtypeStruct((slot, 2 * HD), bf16),
        ),
        compiler_params=pltpu.CompilerParams(
            dimension_semantics=("arbitrary",), vmem_limit_bytes=VMEM_LIMIT
        ),
        cost_estimate=pl.CostEstimate(
            flops=10 * half, bytes_accessed=8 * 2**20, transcendentals=slot * slot * heads
        ),
    )(where, qr, kvt, dmixed, lse, cos2, sin2, shared)


def finish_kernel(first_ref, second_ref, gate_ref, up_ref, gain_ref, *out_refs):
    gate_out, up_out, down_out, part_out = out_refs
    gain, part, start = gain_ref[...], 0.0, 0
    for sum_ref in (first_ref, second_ref):
        width = sum_ref.shape[1] // 3
        here = slice(start, start + width)
        gate = sum_ref[:, :width].astype(f32)
        up = sum_ref[:, width : 2 * width].astype(f32)
        terms = gate_ref[:, here].astype(f32) * gate + up_ref[:, here].astype(f32) * up
        part = part + jnp.sum(terms, axis=1, keepdims=True)
        gate_out[:, here] = gate * gain
        up_out[:, here] = up * gain
        down_out[here, :] = sum_ref[:, 2 * width :].astype(f32).T
        start += width
    part_out[...] = part


def finish_ff(parts, sums, gate_own, up_own, gain):
    rows, ff = gate_own.shape
    widths = [b - a for a, b in parts]
    if rows % HD or any(width % HD for width in widths):
        sums = [total.astype(f32) for total in sums]
        gate = jnp.concatenate([t[:, :w] for t, w in zip(sums, widths)], axis=1)
        up = jnp.concatenate([t[:, w : 2 * w] for t, w in zip(sums, widths)], axis=1)
        down = jnp.concatenate([t[:, 2 * w :] for t, w in zip(sums, widths)], axis=1)
        terms = gate * gate_own.astype(f32) + up * up_own.astype(f32)
        return gate * gain, up * gain, down.T, jnp.sum(terms, axis=1, keepdims=True)
    across = lambda width: pl.BlockSpec((HD, width), lambda i: (i, 0))
    return pl.pallas_call(
        finish_kernel,
        name="finish_ff",
        grid=(rows // HD,),
        in_specs=[across(3 * w) for w in widths] + [across(ff), across(ff), across(1)],
        out_specs=[across(ff), across(ff), pl.BlockSpec((ff, HD), lambda i: (0, i)), across(1)],
        out_shape=(
            jax.ShapeDtypeStruct((rows, ff), f32),
            jax.ShapeDtypeStruct((rows, ff), f32),
            jax.ShapeDtypeStruct((ff, rows), f32),
            jax.ShapeDtypeStruct((rows, 1), f32),
        ),
        compiler_params=pltpu.CompilerParams(dimension_semantics=("arbitrary",)),
        cost_estimate=pl.CostEstimate(
            flops=8 * rows * ff, bytes_accessed=24 * rows * ff, transcendentals=0
        ),
    )(*sums, gate_own, up_own, gain)


def inverse_norm(values):
    return lax.rsqrt(jnp.mean(values * values, axis=-1, keepdims=True) + eps)


def rows_of(array, j, rows):
    return array[j * rows : (j + 1) * rows]


def on_device(
    layer_input,
    lengths,
    w_query,
    w_keyvalue,
    w_project,
    w_gate,
    w_up,
    w_down,
    gain_attn,
    gain_mlp,
    out_grad,
    kv_grad,
):
    rows, model_width = layer_input.shape
    ranks = lax.axis_size("tensor")
    rank = lax.axis_index("tensor").astype(jnp.int32)
    length = lengths[0]
    heads_width = w_query.shape[1]
    ff = w_gate.shape[1]
    cut = -(-ff // 256) * 128
    parts = ((0, cut), (cut, ff))

    order = jnp.bitwise_xor(rank, jnp.arange(ranks, dtype=jnp.int32))
    position = (order[:, None] * rows + jnp.arange(rows, dtype=jnp.int32)[None, :]).reshape(-1)
    frequency = rope_base ** (-(jnp.arange(HD // 2, dtype=f32) * 2.0 / HD))
    angles = position.astype(f32)[:, None] * frequency[None, :]
    cosine, sine = jnp.cos(angles), jnp.sin(angles)
    cos2 = jnp.concatenate([cosine, cosine], axis=1)
    sin2 = jnp.concatenate([-sine, sine], axis=1)
    own_mask = (position[:rows] < length).astype(f32)[:, None]
    where = jnp.stack([rank, length])

    gain_one, gain_two = gain_attn.astype(f32)[:, None], gain_mlp.astype(f32)[:, None]
    qkv_own = jnp.concatenate([w_query, w_keyvalue], axis=1).astype(f32)
    shard_rows = qkv_own.shape[0]
    kv_rows = shard_rows // ranks
    scaled_own = (qkv_own * gain_one).astype(bf16)
    kv_part = lax.dynamic_slice_in_dim(scaled_own[:, heads_width:], rank * kv_rows, kv_rows)
    attn_shard = jnp.concatenate(
        [scaled_own[:, :heads_width], w_project.T, kv_part.reshape(-1, heads_width)], axis=0
    )
    pair_own = [
        jnp.concatenate([w_gate[:, a:b], w_up[:, a:b]], axis=1).astype(f32) for a, b in parts
    ]
    ff_shards = [
        jnp.concatenate([(own * gain_two).astype(bf16), w_down[a:b].T], axis=1)
        for (a, b), own in zip(parts, pair_own)
    ]

    residual = layer_input.astype(f32)
    near = near_blocks(layer_input)
    inputs = all_blocks(layer_input, near)
    attn_full = gather_dp(attn_shard)

    def norm(block):
        block = block.astype(f32)
        return (block * inverse_norm(block)).astype(bf16)

    normed_one = jnp.concatenate([norm(b) for b in inputs], axis=0)
    top = out_grad.astype(f32) * own_mask
    ready = normed_one, ff_shards[1], top.astype(bf16), cos2, sin2
    ff_full = [gather_dp(after(ff_shards[0], *ready))]
    attn_full = attn_full.reshape(-1, *attn_shard.shape)
    query_full = attn_full[:, :shard_rows].reshape(model_width, heads_width)
    project_full = attn_full[:, shard_rows : 2 * shard_rows].reshape(model_width, heads_width)
    kv_part = attn_full[:, 2 * shard_rows :].reshape(-1, 2 * HD)
    kv_near = near_blocks(kv_part)
    kv_blocks = jnp.concatenate(all_blocks(kv_part, kv_near), axis=0)
    kv_blocks = kv_blocks.reshape(ranks, -1, kv_rows, 2 * HD)
    keyvalue_full = jnp.stack([pick(kv_blocks, order[j], 0) for j in range(ranks)], axis=1)
    qkv_full = jnp.concatenate([query_full, keyvalue_full.reshape(model_width, 2 * HD)], axis=1)
    top_own = after(top.astype(bf16), keyvalue_full)
    top_near = near_blocks(top_own)
    qkv = dot(normed_one, qkv_full, 1, 0)
    qr, kvt, mixed, lse = attend(where, qkv, cos2, sin2, rows)
    ff_full.append(gather_dp(after(ff_shards[1], mixed)))
    mixed_rest = dot(after(mixed[rows:], *top_near), project_full, 1, 1).astype(bf16)
    mixed_sent = send_sums(mixed_rest)
    top_near = [after(block, *mixed_sent) for block in top_near]
    top_all = jnp.concatenate(all_blocks(top_own, top_near), axis=0)
    after_attn = residual + finish_sums(
        dot(mixed[:rows], project_full, 1, 1), mixed_rest, mixed_sent
    )

    inv_two = inverse_norm(after_attn)
    unit_two = after_attn * inv_two
    normed_own = after(unit_two.astype(bf16), top_all)
    pairs = [full[:, : 2 * (b - a)] for (a, b), full in zip(parts, ff_full)]
    downs = [full[:, 2 * (b - a) :] for (a, b), full in zip(parts, ff_full)]
    first_grad = dot(top_all, downs[0], 1, 0)
    normed_near = [after(block, first_grad) for block in near_blocks(normed_own)]
    normed_two = jnp.concatenate(all_blocks(normed_own, normed_near), axis=0)

    def feed(normed, pair, grad):
        width = grad.shape[1]
        both = dot(after(normed, grad), pair, 1, 0)
        gate, up = both[:, :width], both[:, width:]
        sig = jax.nn.sigmoid(gate)
        hidden = (gate * sig * up).astype(bf16)
        gate_grad = (grad * up * sig * (1.0 + gate * (1.0 - sig))).astype(bf16)
        up_grad = (grad * gate * sig).astype(bf16)
        return hidden, jnp.concatenate([gate_grad, up_grad], axis=1)

    def partial(hidden, grads):
        return jnp.concatenate(
            [
                dot(normed_two, grads, 0, 0).astype(bf16),
                dot(top_all, hidden, 0, 0).astype(bf16),
            ],
            axis=1,
        )

    hidden0, grads0 = feed(normed_two, pairs[0], first_grad)
    partial0 = partial(hidden0, grads0)
    rest0 = dot(after(grads0[rows:], partial0), pairs[0], 1, 1)
    hidden1, grads1 = feed(after(normed_two, rest0), pairs[1], dot(top_all, downs[1], 1, 0))
    rest = (rest0 + dot(grads1[rows:], pairs[1], 1, 1)).astype(bf16)
    rest_sent = send_sums(rest)
    partial1 = partial(after(hidden1, *rest_sent), after(grads1, *rest_sent))
    ff_sums = [scatter_dp(partial0), scatter_dp(partial1)]
    own = dot(after(grads0[:rows], partial1), pairs[0], 1, 1) + dot(grads1[:rows], pairs[1], 1, 1)
    scaled = finish_sums(own, rest, rest_sent)
    attn_top = top + inv_two * (
        scaled - unit_two * jnp.mean(scaled * unit_two, axis=-1, keepdims=True)
    )
    attn_top_own = attn_top.astype(bf16)
    attn_top_blocks = all_blocks(attn_top_own, near_blocks(attn_top_own))
    attn_top_all = jnp.concatenate(attn_top_blocks, axis=0)
    hidden = [hidden0, hidden1]
    down_rest = sum(dot(h[rows:], w, 1, 1) for h, w in zip(hidden, downs)).astype(bf16)
    down_rest = after(down_rest, *attn_top_blocks)

    mixed_grad = dot(after(attn_top_all, down_rest, ff_sums[0]), project_full, 1, 0).astype(bf16)
    shared = kv_grad.astype(f32) * own_mask
    query_grad, kv_back = attend_back(
        where, qr, kvt, mixed_grad, lse, cos2, sin2, shared, rows
    )
    down_sent = [after(block, query_grad) for block in send_sums(down_rest)]
    qkv_back = after(jnp.concatenate([query_grad, kv_back], axis=1), *down_sent)
    kv_grads = dot(normed_one, qkv_back[:, heads_width:], 0, 0).astype(bf16)
    kv_grads = kv_grads.reshape(-1, ranks, kv_rows, 2 * HD)
    kv_own, *kv_rest = (pick(kv_grads, order[j], 1).reshape(-1, 2 * HD) for j in range(ranks))
    kv_rest = jnp.concatenate(kv_rest, axis=0)
    kv_sent = send_sums(kv_rest)
    qkv_rest = dot(after(qkv_back[rows:], kv_rest), qkv_full, 1, 1).astype(bf16)
    qkv_sent = send_sums(after(qkv_rest, *kv_sent, ff_sums[1]))
    query_back = after(qkv_back[:, :heads_width], qkv_rest)
    kv_sum = finish_sums(kv_own.astype(f32), kv_rest, kv_sent).astype(bf16)
    attn_partial = jnp.concatenate(
        [
            dot(normed_one, query_back, 0, 0).astype(bf16).reshape(-1, shard_rows, heads_width),
            dot(attn_top_all, mixed, 0, 0).astype(bf16).reshape(-1, shard_rows, heads_width),
            kv_sum.reshape(model_width // shard_rows, -1, heads_width),
        ],
        axis=1,
    ).reshape(-1, heads_width)
    attn_sum = scatter_dp(attn_partial).astype(f32)
    down_sent = [after(block, *qkv_sent) for block in down_sent]
    own_down = sum(
        dot(after(h[:rows], attn_partial), w, 1, 1) for h, w in zip(hidden, downs)
    )
    after_mlp = after_attn + finish_sums(own_down, down_rest, down_sent)
    output = (after_mlp * own_mask).astype(bf16)
    scaled_one = finish_sums(dot(qkv_back[:rows], qkv_full, 1, 1), qkv_rest, qkv_sent)
    query_sum, project_sum = attn_sum[:shard_rows], attn_sum[shard_rows : 2 * shard_rows]
    kv_sum = attn_sum[2 * shard_rows :].reshape(kv_rows, 2 * HD)
    grad_gate, grad_up, grad_down, gain_two_part = finish_ff(
        parts, ff_sums, w_gate, w_up, gain_two
    )
    query_part = jnp.sum(qkv_own[:, :heads_width] * query_sum, axis=1, keepdims=True)
    kv_here = lax.dynamic_slice_in_dim(qkv_own[:, heads_width:], rank * kv_rows, kv_rows)
    gain_here = lax.dynamic_slice_in_dim(gain_one, rank * kv_rows, kv_rows)
    small = jnp.concatenate(
        [
            kv_sum * gain_here,
            jnp.sum(kv_here * kv_sum, axis=1, keepdims=True),
            jnp.concatenate([query_part, gain_two_part], axis=1).reshape(kv_rows, -1),
        ],
        axis=1,
    )
    scaled_one = after(scaled_one, small)
    inv_one = inverse_norm(residual)
    unit_one = residual * inv_one
    input_grad = attn_top + inv_one * (
        scaled_one - unit_one * jnp.mean(scaled_one * unit_one, axis=-1, keepdims=True)
    )
    blocks = jnp.stack([small] + [hop(small, j) for j in range(1, ranks)], axis=0)
    sums = jnp.sum(blocks[:, :, 2 * HD + 1 :], axis=0).reshape(shard_rows, 2)
    placed = jnp.concatenate([pick(blocks, order[j], 0) for j in range(ranks)], axis=0)
    return (
        output,
        input_grad,
        query_sum * gain_one,
        placed[:, : 2 * HD],
        project_sum.T,
        grad_gate,
        grad_up,
        grad_down,
        sums[:, 0] + placed[:, 2 * HD],
        sums[:, 1],
    )


def solution(mesh):
    placed = (
        P(("dp", "tensor"), None),
        P("dp"),
        P("dp", "tensor"),
        P("dp", None),
        P("tensor", "dp"),
        P("dp", "tensor"),
        P("dp", "tensor"),
        P("tensor", "dp"),
        P("dp"),
        P("dp"),
        P(("dp", "tensor"), None),
        P(("dp", "tensor"), None),
    )
    return jax.shard_map(
        on_device,
        mesh=mesh,
        in_specs=placed,
        out_specs=(
            P(("dp", "tensor"), None),
            P(("dp", "tensor"), None),
            P("dp", "tensor"),
            P("dp", None),
            P("tensor", "dp"),
            P("dp", "tensor"),
            P("dp", "tensor"),
            P("tensor", "dp"),
            P("dp"),
            P("dp"),
        ),
        check_vma=False,
    )
```

```python
import functools
import math

import jax
import jax.numpy as jnp
from jax import lax
from jax.experimental import pallas as pl
from jax.experimental.pallas import tpu as pltpu
from jax.sharding import PartitionSpec as P

HD = 128
eps = 1e-05
rope_base = 10000.0
neg_big = -1e30
inv_root = 1.0 / math.sqrt(HD)
f32 = jnp.float32
bf16 = jnp.bfloat16


def dot(a, b, ca, cb):
    return lax.dot_general(a, b, (((ca,), (cb,)), ((), ())), preferred_element_type=f32)


def hop(value, step):
    size = lax.axis_size("tensor")
    return lax.ppermute(value, "tensor", [(i, i ^ step) for i in range(size)])


def after(value, *others):
    return lax.optimization_barrier((value, *others))[0]


def near_blocks(own):
    size = lax.axis_size("tensor")
    return [hop(own, j) for j in range(1, 3 if size == 4 else size)]


def all_blocks(own, near):
    if lax.axis_size("tensor") != 4:
        return [own, *near]
    half = own.shape[0] // 2
    one, two = near
    return [own, one, two, hop(two[:half], 1), hop(one[half:], 2)]


def send_sums(rest):
    size = lax.axis_size("tensor")
    rows = rest.shape[0] // (size - 1)
    one, *others = (rows_of(rest, j, rows) for j in range(size - 1))
    if size != 4:
        return [hop(block, j + 1) for j, block in enumerate([one, *others])]
    two, three = others
    half = rows // 2
    return [
        hop(jnp.concatenate([one[:half], three[:half]], axis=0), 1),
        hop(jnp.concatenate([two[half:], three[half:]], axis=0), 2),
    ]


def finish_sums(own, rest, arrived):
    if lax.axis_size("tensor") != 4:
        return own + sum(block.astype(f32) for block in arrived)
    rows = own.shape[0]
    half = rows // 2
    one, two = rows_of(rest, 0, rows), rows_of(rest, 1, rows)
    upper, lower = arrived
    upper_far = hop((two[:half].astype(f32) + upper[half:].astype(f32)).astype(bf16), 2)
    lower_near = hop((one[half:].astype(f32) + lower[half:].astype(f32)).astype(bf16), 1)
    return jnp.concatenate(
        [
            own[:half] + upper[:half].astype(f32) + upper_far.astype(f32),
            own[half:] + lower[:half].astype(f32) + lower_near.astype(f32),
        ],
        axis=0,
    )


def gather_dp(shard):
    return lax.all_gather(shard, "dp", axis=0, tiled=True)


def scatter_dp(partial):
    return lax.psum_scatter(partial, "dp", scatter_dimension=0, tiled=True)


pick = functools.partial(lax.dynamic_index_in_dim, keepdims=False)


def turn(u, cos2, sin2):
    return u * cos2 + pltpu.roll(u, HD // 2, 1) * sin2


def attend_kernel(where_ref, q_ref, kv_ref, cos_ref, sin_ref, qr_ref, kvt_ref, mixed_ref, lse_ref):
    rows, width = q_ref.shape
    heads = width // HD
    ranks = kv_ref.shape[0] // rows
    j = pl.program_id(0)
    rank, length = where_ref[0], where_ref[1]
    block = jnp.bitwise_xor(rank, j)

    @pl.when(j == 0)
    def _():
        for i in range(ranks):
            here = slice(i * rows, (i + 1) * rows)
            there = pl.ds(pl.multiple_of(jnp.bitwise_xor(rank, i) * rows, rows), rows)
            key = turn(kv_ref[here, :HD], cos_ref[here, :], sin_ref[here, :])
            kvt_ref[there, :HD] = key.astype(bf16)
            kvt_ref[there, HD:] = kv_ref[here, HD:].astype(bf16)

    mine = pl.ds(pl.multiple_of(j * rows, rows), rows)
    cos2, sin2 = cos_ref[mine, :], sin_ref[mine, :]
    for h in range(heads):
        head = slice(h * HD, (h + 1) * HD)
        qr_ref[:, head] = turn(q_ref[:, head], cos2, sin2).astype(bf16)
    limit = jnp.minimum(block * rows + lax.broadcasted_iota(jnp.int32, (rows, 1), 0), length - 1)
    for w in range(ranks):

        @pl.when(block == w)
        def _(w=w):
            span = (w + 1) * rows
            allowed = lax.broadcasted_iota(jnp.int32, (rows, span), 1) <= limit
            for h in range(heads):
                head = slice(h * HD, (h + 1) * HD)
                scores = dot(qr_ref[:, head], kvt_ref[:span, :HD], 1, 1) * inv_root
                scores = jnp.where(allowed, scores, neg_big)
                top = jnp.max(scores, axis=1, keepdims=True)
                weights = jnp.exp(scores - top)
                total = jnp.sum(weights, axis=1, keepdims=True)
                probs = (weights * (1.0 / total)).astype(bf16)
                mixed_ref[:, head] = dot(probs, kvt_ref[:span, HD:], 1, 0).astype(bf16)
                lse_ref[:, h : h + 1] = top + jnp.log(total)


def attend_back_kernel(
    where_ref,
    qr_ref,
    kvt_ref,
    dm_ref,
    lse_ref,
    cos_ref,
    sin_ref,
    shared_ref,
    dq_ref,
    dkv_ref,
    dk_acc,
    dv_acc,
):
    rows, width = qr_ref.shape
    heads = width // HD
    ranks = kvt_ref.shape[0] // rows
    j = pl.program_id(0)
    rank, length = where_ref[0], where_ref[1]
    block = jnp.bitwise_xor(rank, j)

    @pl.when(j == 0)
    def _():
        dk_acc[...] = jnp.zeros_like(dk_acc)
        dv_acc[...] = jnp.zeros_like(dv_acc)

    mine = pl.ds(pl.multiple_of(j * rows, rows), rows)
    cos2, sin2 = cos_ref[mine, :], sin_ref[mine, :]
    limit = jnp.minimum(block * rows + lax.broadcasted_iota(jnp.int32, (rows, 1), 0), length - 1)
    for w in range(ranks):

        @pl.when(block == w)
        def _(w=w):
            span = (w + 1) * rows
            allowed = lax.broadcasted_iota(jnp.int32, (rows, span), 1) <= limit
            keys, vals = kvt_ref[:span, :HD], kvt_ref[:span, HD:]
            for h in range(heads):
                head = slice(h * HD, (h + 1) * HD)
                q, dm = qr_ref[:, head], dm_ref[:, head]
                scores = jnp.where(allowed, dot(q, keys, 1, 1) * inv_root, neg_big)
                probs = jnp.exp(scores - lse_ref[:, h : h + 1])
                dp = dot(dm, vals, 1, 1)
                center = jnp.sum(probs * dp, axis=1, keepdims=True)
                ds = (probs * (dp - center)).astype(bf16)
                dq = dot(ds, keys, 1, 0) * inv_root
                dq_ref[:, head] = turn(dq, cos2, -sin2).astype(bf16)
                dk_acc[:span, :] += dot(ds, q, 0, 0)
                dv_acc[:span, :] += dot(probs.astype(bf16), dm, 0, 0)

    @pl.when(j == ranks - 1)
    def _():
        for i in range(ranks):
            here = slice(i * rows, (i + 1) * rows)
            there = pl.ds(pl.multiple_of(jnp.bitwise_xor(rank, i) * rows, rows), rows)
            dk, dv = dk_acc[there, :] * inv_root, dv_acc[there, :]
            if i == 0:
                dk, dv = dk + shared_ref[:, :HD], dv + shared_ref[:, HD:]
            dkv_ref[here, :HD] = turn(dk, cos_ref[here, :], -sin_ref[here, :]).astype(bf16)
            dkv_ref[here, HD:] = dv.astype(bf16)


VMEM_LIMIT = 48 * 2**20


def attend(where, qkv, cos2, sin2, rows):
    slot, width = qkv.shape[0], qkv.shape[1] - 2 * HD
    heads = width // HD
    half = slot * slot * heads * HD
    return pl.pallas_call(
        attend_kernel,
        name="attend",
        grid_spec=pltpu.PrefetchScalarGridSpec(
            num_scalar_prefetch=1,
            grid=(slot // rows,),
            in_specs=[
                pl.BlockSpec((rows, width), lambda j, s: (j, 0)),
                pl.BlockSpec((slot, 2 * HD), lambda j, s: (0, width // (2 * HD))),
                pl.BlockSpec((slot, HD), lambda j, s: (0, 0)),
                pl.BlockSpec((slot, HD), lambda j, s: (0, 0)),
            ],
            out_specs=[
                pl.BlockSpec((rows, width), lambda j, s: (j, 0)),
                pl.BlockSpec((slot, 2 * HD), lambda j, s: (0, 0)),
                pl.BlockSpec((rows, width), lambda j, s: (j, 0)),
                pl.BlockSpec((rows, HD), lambda j, s: (j, 0)),
            ],
        ),
        out_shape=(
            jax.ShapeDtypeStruct((slot, width), bf16),
            jax.ShapeDtypeStruct((slot, 2 * HD), bf16),
            jax.ShapeDtypeStruct((slot, width), bf16),
            jax.ShapeDtypeStruct((slot, HD), f32),
        ),
        compiler_params=pltpu.CompilerParams(
            dimension_semantics=("arbitrary",), vmem_limit_bytes=VMEM_LIMIT
        ),
        cost_estimate=pl.CostEstimate(
            flops=4 * half, bytes_accessed=8 * 2**20, transcendentals=slot * slot * heads
        ),
    )(where, qkv, qkv, cos2, sin2)


def attend_back(where, qr, kvt, dmixed, lse, cos2, sin2, shared, rows):
    slot, width = qr.shape
    heads = width // HD
    half = slot * slot * heads * HD
    return pl.pallas_call(
        attend_back_kernel,
        name="attend_back",
        grid_spec=pltpu.PrefetchScalarGridSpec(
            num_scalar_prefetch=1,
            grid=(slot // rows,),
            in_specs=[
                pl.BlockSpec((rows, width), lambda j, s: (j, 0)),
                pl.BlockSpec((slot, 2 * HD), lambda j, s: (0, 0)),
                pl.BlockSpec((rows, width), lambda j, s: (j, 0)),
                pl.BlockSpec((rows, HD), lambda j, s: (j, 0)),
                pl.BlockSpec((slot, HD), lambda j, s: (0, 0)),
                pl.BlockSpec((slot, HD), lambda j, s: (0, 0)),
                pl.BlockSpec((rows, 2 * HD), lambda j, s: (0, 0)),
            ],
            out_specs=[
                pl.BlockSpec((rows, width), lambda j, s: (j, 0)),
                pl.BlockSpec((slot, 2 * HD), lambda j, s: (0, 0)),
            ],
            scratch_shapes=[pltpu.VMEM((slot, HD), f32), pltpu.VMEM((slot, HD), f32)],
        ),
        out_shape=(
            jax.ShapeDtypeStruct((slot, width), bf16),
            jax.ShapeDtypeStruct((slot, 2 * HD), bf16),
        ),
        compiler_params=pltpu.CompilerParams(
            dimension_semantics=("arbitrary",), vmem_limit_bytes=VMEM_LIMIT
        ),
        cost_estimate=pl.CostEstimate(
            flops=10 * half, bytes_accessed=8 * 2**20, transcendentals=slot * slot * heads
        ),
    )(where, qr, kvt, dmixed, lse, cos2, sin2, shared)


def finish_kernel(first_ref, second_ref, gate_ref, up_ref, gain_ref, *out_refs):
    gate_out, up_out, down_out, part_out = out_refs
    gain, part, start = gain_ref[...], 0.0, 0
    for sum_ref in (first_ref, second_ref):
        width = sum_ref.shape[1] // 3
        here = slice(start, start + width)
        gate = sum_ref[:, :width].astype(f32)
        up = sum_ref[:, width : 2 * width].astype(f32)
        terms = gate_ref[:, here].astype(f32) * gate + up_ref[:, here].astype(f32) * up
        part = part + jnp.sum(terms, axis=1, keepdims=True)
        gate_out[:, here] = gate * gain
        up_out[:, here] = up * gain
        down_out[here, :] = sum_ref[:, 2 * width :].astype(f32).T
        start += width
    part_out[...] = part


def finish_attn_kernel(sum_ref, query_ref, gain_ref, query_out, project_out, part_out):
    rows = query_ref.shape[0]
    total = sum_ref[:rows, :].astype(f32)
    query_out[...] = total * gain_ref[...]
    part_out[...] = jnp.sum(query_ref[...].astype(f32) * total, axis=1, keepdims=True)
    project_out[...] = sum_ref[rows : 2 * rows, :].astype(f32).T


def finish_attn(total, query_own, gain):
    rows, width = query_own.shape
    return pl.pallas_call(
        finish_attn_kernel,
        name="finish_attn",
        out_shape=(
            jax.ShapeDtypeStruct((rows, width), f32),
            jax.ShapeDtypeStruct((width, rows), f32),
            jax.ShapeDtypeStruct((rows, 1), f32),
        ),
    )(total, query_own, gain)


def finish_ff(parts, sums, gate_own, up_own, gain):
    rows, ff = gate_own.shape
    widths = [b - a for a, b in parts]
    if rows % HD or any(width % HD for width in widths):
        sums = [total.astype(f32) for total in sums]
        gate = jnp.concatenate([t[:, :w] for t, w in zip(sums, widths)], axis=1)
        up = jnp.concatenate([t[:, w : 2 * w] for t, w in zip(sums, widths)], axis=1)
        down = jnp.concatenate([t[:, 2 * w :] for t, w in zip(sums, widths)], axis=1)
        terms = gate * gate_own.astype(f32) + up * up_own.astype(f32)
        return gate * gain, up * gain, down.T, jnp.sum(terms, axis=1, keepdims=True)
    across = lambda width: pl.BlockSpec((HD, width), lambda i: (i, 0))
    return pl.pallas_call(
        finish_kernel,
        name="finish_ff",
        grid=(rows // HD,),
        in_specs=[across(3 * w) for w in widths] + [across(ff), across(ff), across(1)],
        out_specs=[across(ff), across(ff), pl.BlockSpec((ff, HD), lambda i: (0, i)), across(1)],
        out_shape=(
            jax.ShapeDtypeStruct((rows, ff), f32),
            jax.ShapeDtypeStruct((rows, ff), f32),
            jax.ShapeDtypeStruct((ff, rows), f32),
            jax.ShapeDtypeStruct((rows, 1), f32),
        ),
        compiler_params=pltpu.CompilerParams(dimension_semantics=("arbitrary",)),
        cost_estimate=pl.CostEstimate(
            flops=8 * rows * ff, bytes_accessed=24 * rows * ff, transcendentals=0
        ),
    )(*sums, gate_own, up_own, gain)


def inverse_norm(values):
    return lax.rsqrt(jnp.mean(values * values, axis=-1, keepdims=True) + eps)


def rows_of(array, j, rows):
    return array[j * rows : (j + 1) * rows]


def on_device(
    layer_input,
    lengths,
    w_query,
    w_keyvalue,
    w_project,
    w_gate,
    w_up,
    w_down,
    gain_attn,
    gain_mlp,
    out_grad,
    kv_grad,
):
    rows, model_width = layer_input.shape
    ranks = lax.axis_size("tensor")
    rank = lax.axis_index("tensor").astype(jnp.int32)
    length = lengths[0]
    heads_width = w_query.shape[1]
    ff = w_gate.shape[1]
    cut = -(-ff // 256) * 128
    parts = ((0, cut), (cut, ff))

    order = jnp.bitwise_xor(rank, jnp.arange(ranks, dtype=jnp.int32))
    position = (order[:, None] * rows + jnp.arange(rows, dtype=jnp.int32)[None, :]).reshape(-1)
    frequency = rope_base ** (-(jnp.arange(HD // 2, dtype=f32) * 2.0 / HD))
    angles = position.astype(f32)[:, None] * frequency[None, :]
    cosine, sine = jnp.cos(angles), jnp.sin(angles)
    cos2 = jnp.concatenate([cosine, cosine], axis=1)
    sin2 = jnp.concatenate([-sine, sine], axis=1)
    own_mask = (position[:rows] < length).astype(f32)[:, None]
    where = jnp.stack([rank, length])

    gain_one, gain_two = gain_attn.astype(f32)[:, None], gain_mlp.astype(f32)[:, None]
    qkv_own = jnp.concatenate([w_query, w_keyvalue], axis=1).astype(f32)
    shard_rows = qkv_own.shape[0]
    kv_rows = shard_rows // ranks
    scaled_own = (qkv_own * gain_one).astype(bf16)
    kv_part = lax.dynamic_slice_in_dim(scaled_own[:, heads_width:], rank * kv_rows, kv_rows)
    attn_shard = jnp.concatenate(
        [scaled_own[:, :heads_width], w_project.T, kv_part.reshape(-1, heads_width)], axis=0
    )
    pair_own = [
        jnp.concatenate([w_gate[:, a:b], w_up[:, a:b]], axis=1).astype(f32) for a, b in parts
    ]
    ff_shards = [
        jnp.concatenate([(own * gain_two).astype(bf16), w_down[a:b].T], axis=1)
        for (a, b), own in zip(parts, pair_own)
    ]

    residual = layer_input.astype(f32)
    x_own = after(layer_input, attn_shard)
    inputs = all_blocks(x_own, near_blocks(x_own))
    attn_full = gather_dp(attn_shard)

    def norm(block):
        block = block.astype(f32)
        return (block * inverse_norm(block)).astype(bf16)

    normed_one = jnp.concatenate([norm(b) for b in inputs], axis=0)
    top = out_grad.astype(f32) * own_mask
    ready = normed_one, ff_shards[1], top.astype(bf16), cos2, sin2
    ff_full = [gather_dp(after(ff_shards[0], *ready))]
    attn_full = attn_full.reshape(-1, *attn_shard.shape)
    query_full = attn_full[:, :shard_rows].reshape(model_width, heads_width)
    project_full = attn_full[:, shard_rows : 2 * shard_rows].reshape(model_width, heads_width)
    kv_part = attn_full[:, 2 * shard_rows :].reshape(-1, 2 * HD)
    kv_near = near_blocks(kv_part)
    kv_blocks = jnp.concatenate(all_blocks(kv_part, kv_near), axis=0)
    kv_blocks = kv_blocks.reshape(ranks, -1, kv_rows, 2 * HD)
    keyvalue_full = jnp.stack([pick(kv_blocks, order[j], 0) for j in range(ranks)], axis=1)
    qkv_full = jnp.concatenate([query_full, keyvalue_full.reshape(model_width, 2 * HD)], axis=1)
    top_own = after(top.astype(bf16), keyvalue_full)
    top_near = near_blocks(top_own)
    qkv = dot(normed_one, qkv_full, 1, 0)
    qr, kvt, mixed, lse = attend(where, qkv, cos2, sin2, rows)
    ff_full.append(gather_dp(after(ff_shards[1], mixed)))
    mixed_rest = dot(after(mixed[rows:], *top_near), project_full, 1, 1).astype(bf16)
    mixed_sent = send_sums(mixed_rest)
    top_near = [after(block, *mixed_sent) for block in top_near]
    top_all = jnp.concatenate(all_blocks(top_own, top_near), axis=0)
    after_attn = residual + finish_sums(
        dot(mixed[:rows], project_full, 1, 1), mixed_rest, mixed_sent
    )

    inv_two = inverse_norm(after_attn)
    unit_two = after_attn * inv_two
    normed_own = after(unit_two.astype(bf16), top_all)
    pairs = [full[:, : 2 * (b - a)] for (a, b), full in zip(parts, ff_full)]
    downs = [full[:, 2 * (b - a) :] for (a, b), full in zip(parts, ff_full)]
    first_grad = dot(top_all, downs[0], 1, 0)
    normed_near = [after(block, first_grad) for block in near_blocks(normed_own)]
    normed_two = jnp.concatenate(all_blocks(normed_own, normed_near), axis=0)

    def feed(normed, pair, grad):
        width = grad.shape[1]
        both = dot(after(normed, grad), pair, 1, 0)
        gate, up = both[:, :width], both[:, width:]
        sig = jax.nn.sigmoid(gate)
        hidden = (gate * sig * up).astype(bf16)
        gate_grad = (grad * up * sig * (1.0 + gate * (1.0 - sig))).astype(bf16)
        up_grad = (grad * gate * sig).astype(bf16)
        return hidden, jnp.concatenate([gate_grad, up_grad], axis=1)

    def partial(hidden, grads):
        return jnp.concatenate(
            [
                dot(normed_two, grads, 0, 0).astype(bf16),
                dot(top_all, hidden, 0, 0).astype(bf16),
            ],
            axis=1,
        )

    hidden0, grads0 = feed(normed_two, pairs[0], first_grad)
    partial0 = partial(hidden0, grads0)
    rest0 = dot(after(grads0[rows:], partial0), pairs[0], 1, 1)
    hidden1, grads1 = feed(after(normed_two, rest0), pairs[1], dot(top_all, downs[1], 1, 0))
    rest = (rest0 + dot(grads1[rows:], pairs[1], 1, 1)).astype(bf16)
    rest_sent = send_sums(rest)
    partial1 = partial(after(hidden1, *rest_sent), after(grads1, *rest_sent))
    ff_sums = [scatter_dp(partial0), scatter_dp(partial1)]
    own = dot(after(grads0[:rows], partial1), pairs[0], 1, 1) + dot(grads1[:rows], pairs[1], 1, 1)
    scaled = finish_sums(own, rest, rest_sent)
    attn_top = top + inv_two * (
        scaled - unit_two * jnp.mean(scaled * unit_two, axis=-1, keepdims=True)
    )
    attn_top_own = attn_top.astype(bf16)
    attn_top_blocks = all_blocks(attn_top_own, near_blocks(attn_top_own))
    attn_top_all = jnp.concatenate(attn_top_blocks, axis=0)
    hidden = [hidden0, hidden1]
    down_rest = sum(dot(h[rows:], w, 1, 1) for h, w in zip(hidden, downs)).astype(bf16)
    down_rest = after(down_rest, *attn_top_blocks)

    mixed_grad = dot(after(attn_top_all, down_rest, ff_sums[0]), project_full, 1, 0).astype(bf16)
    shared = kv_grad.astype(f32) * own_mask
    query_grad, kv_back = attend_back(
        where, qr, kvt, mixed_grad, lse, cos2, sin2, shared, rows
    )
    down_sent = [after(block, query_grad) for block in send_sums(down_rest)]
    qkv_back = after(jnp.concatenate([query_grad, kv_back], axis=1), *down_sent)
    kv_grads = dot(normed_one, qkv_back[:, heads_width:], 0, 0).astype(bf16)
    kv_grads = kv_grads.reshape(-1, ranks, kv_rows, 2 * HD)
    kv_own, *kv_rest = (pick(kv_grads, order[j], 1).reshape(-1, 2 * HD) for j in range(ranks))
    kv_rest = jnp.concatenate(kv_rest, axis=0)
    kv_sent = send_sums(kv_rest)
    qkv_rest = dot(after(qkv_back[rows:], kv_rest), qkv_full, 1, 1).astype(bf16)
    qkv_sent = send_sums(after(qkv_rest, *kv_sent, ff_sums[1]))
    query_back = after(qkv_back[:, :heads_width], qkv_rest)
    kv_sum = finish_sums(kv_own.astype(f32), kv_rest, kv_sent).astype(bf16)
    attn_partial = jnp.concatenate(
        [
            dot(normed_one, query_back, 0, 0).astype(bf16).reshape(-1, shard_rows, heads_width),
            dot(attn_top_all, mixed, 0, 0).astype(bf16).reshape(-1, shard_rows, heads_width),
            kv_sum.reshape(model_width // shard_rows, -1, heads_width),
        ],
        axis=1,
    ).reshape(-1, heads_width)
    attn_sum = scatter_dp(attn_partial)
    down_sent = [after(block, *qkv_sent) for block in down_sent]
    own_down = sum(
        dot(after(h[:rows], attn_partial), w, 1, 1) for h, w in zip(hidden, downs)
    )
    after_mlp = after_attn + finish_sums(own_down, down_rest, down_sent)
    output = (after_mlp * own_mask).astype(bf16)
    scaled_one = finish_sums(dot(qkv_back[:rows], qkv_full, 1, 1), qkv_rest, qkv_sent)
    inv_one = inverse_norm(residual)
    unit_one = residual * inv_one
    input_grad = attn_top + inv_one * (
        scaled_one - unit_one * jnp.mean(scaled_one * unit_one, axis=-1, keepdims=True)
    )

    grad_gate, grad_up, grad_down, gain_two_part = finish_ff(
        parts, ff_sums, w_gate, w_up, gain_two
    )
    attn_sum = after(attn_sum, output, input_grad, gain_two_part)
    grad_query, grad_project, query_part = finish_attn(attn_sum, w_query, gain_one)
    kv_sum = attn_sum[2 * shard_rows :].astype(f32).reshape(kv_rows, 2 * HD)
    kv_here = lax.dynamic_slice_in_dim(qkv_own[:, heads_width:], rank * kv_rows, kv_rows)
    gain_here = lax.dynamic_slice_in_dim(gain_one, rank * kv_rows, kv_rows)
    small = jnp.concatenate(
        [
            kv_sum * gain_here,
            jnp.sum(kv_here * kv_sum, axis=1, keepdims=True),
            jnp.concatenate([query_part, gain_two_part], axis=1).reshape(kv_rows, -1),
        ],
        axis=1,
    )
    blocks = jnp.stack([small] + [hop(small, j) for j in range(1, ranks)], axis=0)
    sums = jnp.sum(blocks[:, :, 2 * HD + 1 :], axis=0).reshape(shard_rows, 2)
    placed = jnp.concatenate([pick(blocks, order[j], 0) for j in range(ranks)], axis=0)
    return (
        output,
        input_grad,
        grad_query,
        placed[:, : 2 * HD],
        grad_project,
        grad_gate,
        grad_up,
        grad_down,
        sums[:, 0] + placed[:, 2 * HD],
        sums[:, 1],
    )


def solution(mesh):
    placed = (
        P(("dp", "tensor"), None),
        P("dp"),
        P("dp", "tensor"),
        P("dp", None),
        P("tensor", "dp"),
        P("dp", "tensor"),
        P("dp", "tensor"),
        P("tensor", "dp"),
        P("dp"),
        P("dp"),
        P(("dp", "tensor"), None),
        P(("dp", "tensor"), None),
    )
    return jax.shard_map(
        on_device,
        mesh=mesh,
        in_specs=placed,
        out_specs=(
            P(("dp", "tensor"), None),
            P(("dp", "tensor"), None),
            P("dp", "tensor"),
            P("dp", None),
            P("tensor", "dp"),
            P("dp", "tensor"),
            P("dp", "tensor"),
            P("tensor", "dp"),
            P("dp"),
            P("dp"),
        ),
        check_vma=False,
    )
```

```python
import functools
import math

import jax
import jax.numpy as jnp
from jax import lax
from jax.experimental import pallas as pl
from jax.experimental.pallas import tpu as pltpu
from jax.sharding import PartitionSpec as P

HD = 128
eps = 1e-05
rope_base = 10000.0
neg_big = -1e30
inv_root = 1.0 / math.sqrt(HD)
f32 = jnp.float32
bf16 = jnp.bfloat16


def dot(a, b, ca, cb):
    return lax.dot_general(a, b, (((ca,), (cb,)), ((), ())), preferred_element_type=f32)


def hop(value, step):
    size = lax.axis_size("tensor")
    return lax.ppermute(value, "tensor", [(i, i ^ step) for i in range(size)])


def after(value, *others):
    return lax.optimization_barrier((value, *others))[0]


def near_blocks(own):
    size = lax.axis_size("tensor")
    return [hop(own, j) for j in range(1, 3 if size == 4 else size)]


def all_blocks(own, near):
    if lax.axis_size("tensor") != 4:
        return [own, *near]
    half = own.shape[0] // 2
    one, two = near
    return [own, one, two, hop(two[:half], 1), hop(one[half:], 2)]


def send_sums(rest):
    size = lax.axis_size("tensor")
    rows = rest.shape[0] // (size - 1)
    one, *others = (rows_of(rest, j, rows) for j in range(size - 1))
    if size != 4:
        return [hop(block, j + 1) for j, block in enumerate([one, *others])]
    two, three = others
    half = rows // 2
    return [
        hop(jnp.concatenate([one[:half], three[:half]], axis=0), 1),
        hop(jnp.concatenate([two[half:], three[half:]], axis=0), 2),
    ]


def finish_sums(own, rest, arrived):
    if lax.axis_size("tensor") != 4:
        return own + sum(block.astype(f32) for block in arrived)
    rows = own.shape[0]
    half = rows // 2
    one, two = rows_of(rest, 0, rows), rows_of(rest, 1, rows)
    upper, lower = arrived
    upper_far = hop((two[:half].astype(f32) + upper[half:].astype(f32)).astype(bf16), 2)
    lower_near = hop((one[half:].astype(f32) + lower[half:].astype(f32)).astype(bf16), 1)
    return jnp.concatenate(
        [
            own[:half] + upper[:half].astype(f32) + upper_far.astype(f32),
            own[half:] + lower[:half].astype(f32) + lower_near.astype(f32),
        ],
        axis=0,
    )


def gather_dp(shard):
    return lax.all_gather(shard, "dp", axis=0, tiled=True)


def scatter_dp(partial):
    return lax.psum_scatter(partial, "dp", scatter_dimension=0, tiled=True)


pick = functools.partial(lax.dynamic_index_in_dim, keepdims=False)


def turn(u, cos2, sin2):
    return u * cos2 + pltpu.roll(u, HD // 2, 1) * sin2


def attend_kernel(where_ref, q_ref, kv_ref, cos_ref, sin_ref, qr_ref, kvt_ref, mixed_ref, lse_ref):
    rows, width = q_ref.shape
    heads = width // HD
    ranks = kv_ref.shape[0] // rows
    j = pl.program_id(0)
    rank, length = where_ref[0], where_ref[1]
    block = jnp.bitwise_xor(rank, j)

    @pl.when(j == 0)
    def _():
        for i in range(ranks):
            here = slice(i * rows, (i + 1) * rows)
            there = pl.ds(pl.multiple_of(jnp.bitwise_xor(rank, i) * rows, rows), rows)
            key = turn(kv_ref[here, :HD], cos_ref[here, :], sin_ref[here, :])
            kvt_ref[there, :HD] = key.astype(bf16)
            kvt_ref[there, HD:] = kv_ref[here, HD:].astype(bf16)

    mine = pl.ds(pl.multiple_of(j * rows, rows), rows)
    cos2, sin2 = cos_ref[mine, :], sin_ref[mine, :]
    for h in range(heads):
        head = slice(h * HD, (h + 1) * HD)
        qr_ref[:, head] = turn(q_ref[:, head], cos2, sin2).astype(bf16)
    limit = jnp.minimum(block * rows + lax.broadcasted_iota(jnp.int32, (rows, 1), 0), length - 1)
    for w in range(ranks):

        @pl.when(block == w)
        def _(w=w):
            span = (w + 1) * rows
            allowed = lax.broadcasted_iota(jnp.int32, (rows, span), 1) <= limit
            for h in range(heads):
                head = slice(h * HD, (h + 1) * HD)
                scores = dot(qr_ref[:, head], kvt_ref[:span, :HD], 1, 1) * inv_root
                scores = jnp.where(allowed, scores, neg_big)
                top = jnp.max(scores, axis=1, keepdims=True)
                weights = jnp.exp(scores - top)
                total = jnp.sum(weights, axis=1, keepdims=True)
                probs = (weights * (1.0 / total)).astype(bf16)
                mixed_ref[:, head] = dot(probs, kvt_ref[:span, HD:], 1, 0).astype(bf16)
                lse_ref[:, h : h + 1] = top + jnp.log(total)


def attend_back_kernel(
    where_ref,
    qr_ref,
    kvt_ref,
    dm_ref,
    lse_ref,
    cos_ref,
    sin_ref,
    shared_ref,
    dq_ref,
    dkv_ref,
    dk_acc,
    dv_acc,
):
    rows, width = qr_ref.shape
    heads = width // HD
    ranks = kvt_ref.shape[0] // rows
    j = pl.program_id(0)
    rank, length = where_ref[0], where_ref[1]
    block = jnp.bitwise_xor(rank, j)

    @pl.when(j == 0)
    def _():
        dk_acc[...] = jnp.zeros_like(dk_acc)
        dv_acc[...] = jnp.zeros_like(dv_acc)

    mine = pl.ds(pl.multiple_of(j * rows, rows), rows)
    cos2, sin2 = cos_ref[mine, :], sin_ref[mine, :]
    limit = jnp.minimum(block * rows + lax.broadcasted_iota(jnp.int32, (rows, 1), 0), length - 1)
    for w in range(ranks):

        @pl.when(block == w)
        def _(w=w):
            span = (w + 1) * rows
            allowed = lax.broadcasted_iota(jnp.int32, (rows, span), 1) <= limit
            keys, vals = kvt_ref[:span, :HD], kvt_ref[:span, HD:]
            for h in range(heads):
                head = slice(h * HD, (h + 1) * HD)
                q, dm = qr_ref[:, head], dm_ref[:, head]
                scores = jnp.where(allowed, dot(q, keys, 1, 1) * inv_root, neg_big)
                probs = jnp.exp(scores - lse_ref[:, h : h + 1])
                dp = dot(dm, vals, 1, 1)
                center = jnp.sum(probs * dp, axis=1, keepdims=True)
                ds = (probs * (dp - center)).astype(bf16)
                dq = dot(ds, keys, 1, 0) * inv_root
                dq_ref[:, head] = turn(dq, cos2, -sin2).astype(bf16)
                dk_acc[:span, :] += dot(ds, q, 0, 0)
                dv_acc[:span, :] += dot(probs.astype(bf16), dm, 0, 0)

    @pl.when(j == ranks - 1)
    def _():
        for i in range(ranks):
            here = slice(i * rows, (i + 1) * rows)
            there = pl.ds(pl.multiple_of(jnp.bitwise_xor(rank, i) * rows, rows), rows)
            dk, dv = dk_acc[there, :] * inv_root, dv_acc[there, :]
            if i == 0:
                dk, dv = dk + shared_ref[:, :HD], dv + shared_ref[:, HD:]
            dkv_ref[here, :HD] = turn(dk, cos_ref[here, :], -sin_ref[here, :]).astype(bf16)
            dkv_ref[here, HD:] = dv.astype(bf16)


VMEM_LIMIT = 48 * 2**20


def attend(where, qkv, cos2, sin2, rows):
    slot, width = qkv.shape[0], qkv.shape[1] - 2 * HD
    heads = width // HD
    half = slot * slot * heads * HD
    return pl.pallas_call(
        attend_kernel,
        name="attend",
        grid_spec=pltpu.PrefetchScalarGridSpec(
            num_scalar_prefetch=1,
            grid=(slot // rows,),
            in_specs=[
                pl.BlockSpec((rows, width), lambda j, s: (j, 0)),
                pl.BlockSpec((slot, 2 * HD), lambda j, s: (0, width // (2 * HD))),
                pl.BlockSpec((slot, HD), lambda j, s: (0, 0)),
                pl.BlockSpec((slot, HD), lambda j, s: (0, 0)),
            ],
            out_specs=[
                pl.BlockSpec((rows, width), lambda j, s: (j, 0)),
                pl.BlockSpec((slot, 2 * HD), lambda j, s: (0, 0)),
                pl.BlockSpec((rows, width), lambda j, s: (j, 0)),
                pl.BlockSpec((rows, HD), lambda j, s: (j, 0)),
            ],
        ),
        out_shape=(
            jax.ShapeDtypeStruct((slot, width), bf16),
            jax.ShapeDtypeStruct((slot, 2 * HD), bf16),
            jax.ShapeDtypeStruct((slot, width), bf16),
            jax.ShapeDtypeStruct((slot, HD), f32),
        ),
        compiler_params=pltpu.CompilerParams(
            dimension_semantics=("arbitrary",), vmem_limit_bytes=VMEM_LIMIT
        ),
        cost_estimate=pl.CostEstimate(
            flops=4 * half, bytes_accessed=8 * 2**20, transcendentals=slot * slot * heads
        ),
    )(where, qkv, qkv, cos2, sin2)


def attend_back(where, qr, kvt, dmixed, lse, cos2, sin2, shared, rows):
    slot, width = qr.shape
    heads = width // HD
    half = slot * slot * heads * HD
    return pl.pallas_call(
        attend_back_kernel,
        name="attend_back",
        grid_spec=pltpu.PrefetchScalarGridSpec(
            num_scalar_prefetch=1,
            grid=(slot // rows,),
            in_specs=[
                pl.BlockSpec((rows, width), lambda j, s: (j, 0)),
                pl.BlockSpec((slot, 2 * HD), lambda j, s: (0, 0)),
                pl.BlockSpec((rows, width), lambda j, s: (j, 0)),
                pl.BlockSpec((rows, HD), lambda j, s: (j, 0)),
                pl.BlockSpec((slot, HD), lambda j, s: (0, 0)),
                pl.BlockSpec((slot, HD), lambda j, s: (0, 0)),
                pl.BlockSpec((rows, 2 * HD), lambda j, s: (0, 0)),
            ],
            out_specs=[
                pl.BlockSpec((rows, width), lambda j, s: (j, 0)),
                pl.BlockSpec((slot, 2 * HD), lambda j, s: (0, 0)),
            ],
            scratch_shapes=[pltpu.VMEM((slot, HD), f32), pltpu.VMEM((slot, HD), f32)],
        ),
        out_shape=(
            jax.ShapeDtypeStruct((slot, width), bf16),
            jax.ShapeDtypeStruct((slot, 2 * HD), bf16),
        ),
        compiler_params=pltpu.CompilerParams(
            dimension_semantics=("arbitrary",), vmem_limit_bytes=VMEM_LIMIT
        ),
        cost_estimate=pl.CostEstimate(
            flops=10 * half, bytes_accessed=8 * 2**20, transcendentals=slot * slot * heads
        ),
    )(where, qr, kvt, dmixed, lse, cos2, sin2, shared)


def finish_kernel(first_ref, second_ref, gate_ref, up_ref, gain_ref, *out_refs):
    gate_out, up_out, down_out, part_out = out_refs
    gain, part, start = gain_ref[...], 0.0, 0
    for sum_ref in (first_ref, second_ref):
        width = sum_ref.shape[1] // 3
        here = slice(start, start + width)
        gate = sum_ref[:, :width].astype(f32)
        up = sum_ref[:, width : 2 * width].astype(f32)
        terms = gate_ref[:, here].astype(f32) * gate + up_ref[:, here].astype(f32) * up
        part = part + jnp.sum(terms, axis=1, keepdims=True)
        gate_out[:, here] = gate * gain
        up_out[:, here] = up * gain
        down_out[here, :] = sum_ref[:, 2 * width :].astype(f32).T
        start += width
    part_out[...] = part


def finish_attn_kernel(sum_ref, query_ref, gain_ref, query_out, project_out, part_out):
    rows = query_ref.shape[0]
    total = sum_ref[:rows, :].astype(f32)
    query_out[...] = total * gain_ref[...]
    part_out[...] = jnp.sum(query_ref[...].astype(f32) * total, axis=1, keepdims=True)
    project_out[...] = sum_ref[rows : 2 * rows, :].astype(f32).T


def finish_attn(total, query_own, gain):
    rows, width = query_own.shape
    return pl.pallas_call(
        finish_attn_kernel,
        name="finish_attn",
        out_shape=(
            jax.ShapeDtypeStruct((rows, width), f32),
            jax.ShapeDtypeStruct((width, rows), f32),
            jax.ShapeDtypeStruct((rows, 1), f32),
        ),
    )(total, query_own, gain)


def finish_ff(parts, sums, gate_own, up_own, gain):
    rows, ff = gate_own.shape
    widths = [b - a for a, b in parts]
    if rows % HD or any(width % HD for width in widths):
        sums = [total.astype(f32) for total in sums]
        gate = jnp.concatenate([t[:, :w] for t, w in zip(sums, widths)], axis=1)
        up = jnp.concatenate([t[:, w : 2 * w] for t, w in zip(sums, widths)], axis=1)
        down = jnp.concatenate([t[:, 2 * w :] for t, w in zip(sums, widths)], axis=1)
        terms = gate * gate_own.astype(f32) + up * up_own.astype(f32)
        return gate * gain, up * gain, down.T, jnp.sum(terms, axis=1, keepdims=True)
    across = lambda width: pl.BlockSpec((HD, width), lambda i: (i, 0))
    return pl.pallas_call(
        finish_kernel,
        name="finish_ff",
        grid=(rows // HD,),
        in_specs=[across(3 * w) for w in widths] + [across(ff), across(ff), across(1)],
        out_specs=[across(ff), across(ff), pl.BlockSpec((ff, HD), lambda i: (0, i)), across(1)],
        out_shape=(
            jax.ShapeDtypeStruct((rows, ff), f32),
            jax.ShapeDtypeStruct((rows, ff), f32),
            jax.ShapeDtypeStruct((ff, rows), f32),
            jax.ShapeDtypeStruct((rows, 1), f32),
        ),
        compiler_params=pltpu.CompilerParams(dimension_semantics=("arbitrary",)),
        cost_estimate=pl.CostEstimate(
            flops=8 * rows * ff, bytes_accessed=24 * rows * ff, transcendentals=0
        ),
    )(*sums, gate_own, up_own, gain)


def inverse_norm(values):
    return lax.rsqrt(jnp.mean(values * values, axis=-1, keepdims=True) + eps)


def rows_of(array, j, rows):
    return array[j * rows : (j + 1) * rows]


def on_device(
    layer_input,
    lengths,
    w_query,
    w_keyvalue,
    w_project,
    w_gate,
    w_up,
    w_down,
    gain_attn,
    gain_mlp,
    out_grad,
    kv_grad,
):
    rows, model_width = layer_input.shape
    ranks = lax.axis_size("tensor")
    rank = lax.axis_index("tensor").astype(jnp.int32)
    length = lengths[0]
    heads_width = w_query.shape[1]
    ff = w_gate.shape[1]
    cut = -(-ff // 256) * 128
    parts = ((0, cut), (cut, ff))

    order = jnp.bitwise_xor(rank, jnp.arange(ranks, dtype=jnp.int32))
    position = (order[:, None] * rows + jnp.arange(rows, dtype=jnp.int32)[None, :]).reshape(-1)
    frequency = rope_base ** (-(jnp.arange(HD // 2, dtype=f32) * 2.0 / HD))
    angles = position.astype(f32)[:, None] * frequency[None, :]
    cosine, sine = jnp.cos(angles), jnp.sin(angles)
    cos2 = jnp.concatenate([cosine, cosine], axis=1)
    sin2 = jnp.concatenate([-sine, sine], axis=1)
    own_mask = (position[:rows] < length).astype(f32)[:, None]
    where = jnp.stack([rank, length])

    gain_one, gain_two = gain_attn.astype(f32)[:, None], gain_mlp.astype(f32)[:, None]
    qkv_own = jnp.concatenate([w_query, w_keyvalue], axis=1).astype(f32)
    shard_rows = qkv_own.shape[0]
    kv_rows = shard_rows // ranks
    scaled_own = (qkv_own * gain_one).astype(bf16)
    kv_part = lax.dynamic_slice_in_dim(scaled_own[:, heads_width:], rank * kv_rows, kv_rows)
    attn_shard = jnp.concatenate(
        [scaled_own[:, :heads_width], w_project.T, kv_part.reshape(-1, heads_width)], axis=0
    )
    pair_own = [
        jnp.concatenate([w_gate[:, a:b], w_up[:, a:b]], axis=1).astype(f32) for a, b in parts
    ]
    ff_shards = [
        jnp.concatenate([(own * gain_two).astype(bf16), w_down[a:b].T], axis=1)
        for (a, b), own in zip(parts, pair_own)
    ]

    residual = layer_input.astype(f32)
    x_own = after(layer_input, attn_shard)
    inputs = all_blocks(x_own, near_blocks(x_own))
    attn_full = gather_dp(attn_shard)

    def norm(block):
        block = block.astype(f32)
        return (block * inverse_norm(block)).astype(bf16)

    normed_one = jnp.concatenate([norm(b) for b in inputs], axis=0)
    top = out_grad.astype(f32) * own_mask
    ready = normed_one, ff_shards[1], top.astype(bf16), cos2, sin2
    ff_full = [gather_dp(after(ff_shards[0], *ready))]
    attn_full = attn_full.reshape(-1, *attn_shard.shape)
    query_full = attn_full[:, :shard_rows].reshape(model_width, heads_width)
    project_full = attn_full[:, shard_rows : 2 * shard_rows].reshape(model_width, heads_width)
    kv_part = attn_full[:, 2 * shard_rows :].reshape(-1, 2 * HD)
    kv_near = near_blocks(kv_part)
    kv_blocks = jnp.concatenate(all_blocks(kv_part, kv_near), axis=0)
    kv_blocks = kv_blocks.reshape(ranks, -1, kv_rows, 2 * HD)
    keyvalue_full = jnp.stack([pick(kv_blocks, order[j], 0) for j in range(ranks)], axis=1)
    qkv_full = jnp.concatenate([query_full, keyvalue_full.reshape(model_width, 2 * HD)], axis=1)
    top_own = after(top.astype(bf16), keyvalue_full)
    top_near = near_blocks(top_own)
    qkv = dot(normed_one, qkv_full, 1, 0)
    qr, kvt, mixed, lse = attend(where, qkv, cos2, sin2, rows)
    ff_full.append(gather_dp(after(ff_shards[1], mixed)))
    mixed_rest = dot(after(mixed[rows:], *top_near), project_full, 1, 1).astype(bf16)
    mixed_sent = send_sums(mixed_rest)
    top_near = [after(block, *mixed_sent) for block in top_near]
    top_all = jnp.concatenate(all_blocks(top_own, top_near), axis=0)
    after_attn = residual + finish_sums(
        dot(mixed[:rows], project_full, 1, 1), mixed_rest, mixed_sent
    )

    inv_two = inverse_norm(after_attn)
    unit_two = after_attn * inv_two
    normed_own = after(unit_two.astype(bf16), top_all)
    pairs = [full[:, : 2 * (b - a)] for (a, b), full in zip(parts, ff_full)]
    downs = [full[:, 2 * (b - a) :] for (a, b), full in zip(parts, ff_full)]
    first_grad = dot(top_all, downs[0], 1, 0)
    normed_near = [after(block, first_grad) for block in near_blocks(normed_own)]
    normed_two = jnp.concatenate(all_blocks(normed_own, normed_near), axis=0)

    def feed(normed, pair, grad):
        width = grad.shape[1]
        both = dot(after(normed, grad), pair, 1, 0)
        gate, up = both[:, :width], both[:, width:]
        sig = jax.nn.sigmoid(gate)
        hidden = (gate * sig * up).astype(bf16)
        gate_grad = (grad * up * sig * (1.0 + gate * (1.0 - sig))).astype(bf16)
        up_grad = (grad * gate * sig).astype(bf16)
        return hidden, jnp.concatenate([gate_grad, up_grad], axis=1)

    def partial(hidden, grads):
        return jnp.concatenate(
            [
                dot(normed_two, grads, 0, 0).astype(bf16),
                dot(top_all, hidden, 0, 0).astype(bf16),
            ],
            axis=1,
        )

    hidden0, grads0 = feed(normed_two, pairs[0], first_grad)
    partial0 = partial(hidden0, grads0)
    rest0 = dot(after(grads0[rows:], partial0), pairs[0], 1, 1)
    hidden1, grads1 = feed(after(normed_two, rest0), pairs[1], dot(top_all, downs[1], 1, 0))
    rest = (rest0 + dot(grads1[rows:], pairs[1], 1, 1)).astype(bf16)
    rest_sent = send_sums(rest)
    partial1 = partial(after(hidden1, *rest_sent), after(grads1, *rest_sent))
    ff_sums = [scatter_dp(partial0), scatter_dp(partial1)]
    own = dot(after(grads0[:rows], partial1), pairs[0], 1, 1) + dot(grads1[:rows], pairs[1], 1, 1)
    scaled = finish_sums(own, rest, rest_sent)
    attn_top = top + inv_two * (
        scaled - unit_two * jnp.mean(scaled * unit_two, axis=-1, keepdims=True)
    )
    attn_top_own = attn_top.astype(bf16)
    attn_top_blocks = all_blocks(attn_top_own, near_blocks(attn_top_own))
    attn_top_all = jnp.concatenate(attn_top_blocks, axis=0)
    hidden = [hidden0, hidden1]
    down_rest = sum(dot(h[rows:], w, 1, 1) for h, w in zip(hidden, downs)).astype(bf16)
    down_rest = after(down_rest, *attn_top_blocks)

    mixed_grad = dot(after(attn_top_all, down_rest, ff_sums[0]), project_full, 1, 0).astype(bf16)
    shared = kv_grad.astype(f32) * own_mask
    query_grad, kv_back = attend_back(
        where, qr, kvt, mixed_grad, lse, cos2, sin2, shared, rows
    )
    down_sent = [after(block, query_grad) for block in send_sums(down_rest)]
    qkv_back = after(jnp.concatenate([query_grad, kv_back], axis=1), *down_sent)
    kv_grads = dot(normed_one, qkv_back[:, heads_width:], 0, 0).astype(bf16)
    kv_grads = kv_grads.reshape(-1, ranks, kv_rows, 2 * HD)
    kv_own, *kv_rest = (pick(kv_grads, order[j], 1).reshape(-1, 2 * HD) for j in range(ranks))
    kv_rest = jnp.concatenate(kv_rest, axis=0)
    kv_sent = send_sums(kv_rest)
    qkv_rest = dot(after(qkv_back[rows:], kv_rest), qkv_full, 1, 1).astype(bf16)
    qkv_sent = send_sums(after(qkv_rest, *kv_sent, ff_sums[1]))
    query_back = after(qkv_back[:, :heads_width], qkv_rest)
    kv_sum = finish_sums(kv_own.astype(f32), kv_rest, kv_sent).astype(bf16)
    attn_partial = jnp.concatenate(
        [
            dot(normed_one, query_back, 0, 0).astype(bf16).reshape(-1, shard_rows, heads_width),
            dot(attn_top_all, mixed, 0, 0).astype(bf16).reshape(-1, shard_rows, heads_width),
            kv_sum.reshape(model_width // shard_rows, -1, heads_width),
        ],
        axis=1,
    ).reshape(-1, heads_width)
    attn_sum = scatter_dp(attn_partial)
    down_sent = [after(block, *qkv_sent) for block in down_sent]
    own_down = sum(
        dot(after(h[:rows], attn_partial), w, 1, 1) for h, w in zip(hidden, downs)
    )
    after_mlp = after_attn + finish_sums(own_down, down_rest, down_sent)
    scaled_one = finish_sums(dot(qkv_back[:rows], qkv_full, 1, 1), qkv_rest, qkv_sent)
    grad_gate, grad_up, grad_down, gain_two_part = finish_ff(
        parts, ff_sums, w_gate, w_up, gain_two
    )
    attn_sum = after(attn_sum, scaled_one, gain_two_part)
    grad_query, grad_project, query_part = finish_attn(attn_sum, w_query, gain_one)
    kv_sum = attn_sum[2 * shard_rows :].astype(f32).reshape(kv_rows, 2 * HD)
    kv_here = lax.dynamic_slice_in_dim(qkv_own[:, heads_width:], rank * kv_rows, kv_rows)
    gain_here = lax.dynamic_slice_in_dim(gain_one, rank * kv_rows, kv_rows)
    small = jnp.concatenate(
        [
            kv_sum * gain_here,
            jnp.sum(kv_here * kv_sum, axis=1, keepdims=True),
            jnp.concatenate([query_part, gain_two_part], axis=1).reshape(kv_rows, -1),
        ],
        axis=1,
    )
    scaled_one, after_mlp = after(scaled_one, small), after(after_mlp, small)
    output = (after_mlp * own_mask).astype(bf16)
    inv_one = inverse_norm(residual)
    unit_one = residual * inv_one
    input_grad = attn_top + inv_one * (
        scaled_one - unit_one * jnp.mean(scaled_one * unit_one, axis=-1, keepdims=True)
    )
    blocks = jnp.stack([small] + [hop(small, j) for j in range(1, ranks)], axis=0)
    sums = jnp.sum(blocks[:, :, 2 * HD + 1 :], axis=0).reshape(shard_rows, 2)
    placed = jnp.concatenate([pick(blocks, order[j], 0) for j in range(ranks)], axis=0)
    return (
        output,
        input_grad,
        grad_query,
        placed[:, : 2 * HD],
        grad_project,
        grad_gate,
        grad_up,
        grad_down,
        sums[:, 0] + placed[:, 2 * HD],
        sums[:, 1],
    )


def solution(mesh):
    placed = (
        P(("dp", "tensor"), None),
        P("dp"),
        P("dp", "tensor"),
        P("dp", None),
        P("tensor", "dp"),
        P("dp", "tensor"),
        P("dp", "tensor"),
        P("tensor", "dp"),
        P("dp"),
        P("dp"),
        P(("dp", "tensor"), None),
        P(("dp", "tensor"), None),
    )
    return jax.shard_map(
        on_device,
        mesh=mesh,
        in_specs=placed,
        out_specs=(
            P(("dp", "tensor"), None),
            P(("dp", "tensor"), None),
            P("dp", "tensor"),
            P("dp", None),
            P("tensor", "dp"),
            P("dp", "tensor"),
            P("dp", "tensor"),
            P("tensor", "dp"),
            P("dp"),
            P("dp"),
        ),
        check_vma=False,
    )
```

```python
import functools
import math

import jax
import jax.numpy as jnp
from jax import lax
from jax.experimental import pallas as pl
from jax.experimental.pallas import tpu as pltpu
from jax.sharding import PartitionSpec as P

HD = 128
eps = 1e-05
rope_base = 10000.0
neg_big = -1e30
inv_root = 1.0 / math.sqrt(HD)
f32 = jnp.float32
bf16 = jnp.bfloat16


def dot(a, b, ca, cb):
    return lax.dot_general(a, b, (((ca,), (cb,)), ((), ())), preferred_element_type=f32)


def hop(value, step):
    size = lax.axis_size("tensor")
    return lax.ppermute(value, "tensor", [(i, i ^ step) for i in range(size)])


def after(value, *others):
    return lax.optimization_barrier((value, *others))[0]


def near_blocks(own):
    size = lax.axis_size("tensor")
    return [hop(own, j) for j in range(1, 3 if size == 4 else size)]


def all_blocks(own, near):
    if lax.axis_size("tensor") != 4:
        return [own, *near]
    half = own.shape[0] // 2
    one, two = near
    return [own, one, two, hop(two[:half], 1), hop(one[half:], 2)]


def send_sums(rest):
    size = lax.axis_size("tensor")
    rows = rest.shape[0] // (size - 1)
    one, *others = (rows_of(rest, j, rows) for j in range(size - 1))
    if size != 4:
        return [hop(block, j + 1) for j, block in enumerate([one, *others])]
    two, three = others
    half = rows // 2
    return [
        hop(jnp.concatenate([one[:half], three[:half]], axis=0), 1),
        hop(jnp.concatenate([two[half:], three[half:]], axis=0), 2),
    ]


def finish_sums(own, rest, arrived):
    if lax.axis_size("tensor") != 4:
        return own + sum(block.astype(f32) for block in arrived)
    rows = own.shape[0]
    half = rows // 2
    one, two = rows_of(rest, 0, rows), rows_of(rest, 1, rows)
    upper, lower = arrived
    upper_far = hop((two[:half].astype(f32) + upper[half:].astype(f32)).astype(bf16), 2)
    lower_near = hop((one[half:].astype(f32) + lower[half:].astype(f32)).astype(bf16), 1)
    return jnp.concatenate(
        [
            own[:half] + upper[:half].astype(f32) + upper_far.astype(f32),
            own[half:] + lower[:half].astype(f32) + lower_near.astype(f32),
        ],
        axis=0,
    )


def gather_dp(shard):
    return lax.all_gather(shard, "dp", axis=0, tiled=True)


def scatter_dp(partial):
    return lax.psum_scatter(partial, "dp", scatter_dimension=0, tiled=True)


pick = functools.partial(lax.dynamic_index_in_dim, keepdims=False)


def turn(u, cos2, sin2):
    return u * cos2 + pltpu.roll(u, HD // 2, 1) * sin2


def attend_kernel(where_ref, q_ref, kv_ref, cos_ref, sin_ref, qr_ref, kvt_ref, mixed_ref, lse_ref):
    rows, width = q_ref.shape
    heads = width // HD
    ranks = kv_ref.shape[0] // rows
    j = pl.program_id(0)
    rank, length = where_ref[0], where_ref[1]
    block = jnp.bitwise_xor(rank, j)

    @pl.when(j == 0)
    def _():
        for i in range(ranks):
            here = slice(i * rows, (i + 1) * rows)
            there = pl.ds(pl.multiple_of(jnp.bitwise_xor(rank, i) * rows, rows), rows)
            key = turn(kv_ref[here, :HD], cos_ref[here, :], sin_ref[here, :])
            kvt_ref[there, :HD] = key.astype(bf16)
            kvt_ref[there, HD:] = kv_ref[here, HD:].astype(bf16)

    mine = pl.ds(pl.multiple_of(j * rows, rows), rows)
    cos2, sin2 = cos_ref[mine, :], sin_ref[mine, :]
    for h in range(heads):
        head = slice(h * HD, (h + 1) * HD)
        qr_ref[:, head] = turn(q_ref[:, head], cos2, sin2).astype(bf16)
    limit = jnp.minimum(block * rows + lax.broadcasted_iota(jnp.int32, (rows, 1), 0), length - 1)
    for w in range(ranks):

        @pl.when(block == w)
        def _(w=w):
            span = (w + 1) * rows
            allowed = lax.broadcasted_iota(jnp.int32, (rows, span), 1) <= limit
            for h in range(heads):
                head = slice(h * HD, (h + 1) * HD)
                scores = dot(qr_ref[:, head], kvt_ref[:span, :HD], 1, 1) * inv_root
                scores = jnp.where(allowed, scores, neg_big)
                top = jnp.max(scores, axis=1, keepdims=True)
                weights = jnp.exp(scores - top)
                total = jnp.sum(weights, axis=1, keepdims=True)
                probs = (weights * (1.0 / total)).astype(bf16)
                mixed_ref[:, head] = dot(probs, kvt_ref[:span, HD:], 1, 0).astype(bf16)
                lse_ref[:, h : h + 1] = top + jnp.log(total)


def attend_back_kernel(
    where_ref,
    qr_ref,
    kvt_ref,
    dm_ref,
    lse_ref,
    cos_ref,
    sin_ref,
    shared_ref,
    dq_ref,
    dkv_ref,
    dk_acc,
    dv_acc,
):
    rows, width = qr_ref.shape
    heads = width // HD
    ranks = kvt_ref.shape[0] // rows
    j = pl.program_id(0)
    rank, length = where_ref[0], where_ref[1]
    block = jnp.bitwise_xor(rank, j)

    @pl.when(j == 0)
    def _():
        dk_acc[...] = jnp.zeros_like(dk_acc)
        dv_acc[...] = jnp.zeros_like(dv_acc)

    mine = pl.ds(pl.multiple_of(j * rows, rows), rows)
    cos2, sin2 = cos_ref[mine, :], sin_ref[mine, :]
    limit = jnp.minimum(block * rows + lax.broadcasted_iota(jnp.int32, (rows, 1), 0), length - 1)
    for w in range(ranks):

        @pl.when(block == w)
        def _(w=w):
            span = (w + 1) * rows
            allowed = lax.broadcasted_iota(jnp.int32, (rows, span), 1) <= limit
            keys, vals = kvt_ref[:span, :HD], kvt_ref[:span, HD:]
            for h in range(heads):
                head = slice(h * HD, (h + 1) * HD)
                q, dm = qr_ref[:, head], dm_ref[:, head]
                scores = jnp.where(allowed, dot(q, keys, 1, 1) * inv_root, neg_big)
                probs = jnp.exp(scores - lse_ref[:, h : h + 1])
                dp = dot(dm, vals, 1, 1)
                center = jnp.sum(probs * dp, axis=1, keepdims=True)
                ds = (probs * (dp - center)).astype(bf16)
                dq = dot(ds, keys, 1, 0) * inv_root
                dq_ref[:, head] = turn(dq, cos2, -sin2).astype(bf16)
                dk_acc[:span, :] += dot(ds, q, 0, 0)
                dv_acc[:span, :] += dot(probs.astype(bf16), dm, 0, 0)

    @pl.when(j == ranks - 1)
    def _():
        for i in range(ranks):
            here = slice(i * rows, (i + 1) * rows)
            there = pl.ds(pl.multiple_of(jnp.bitwise_xor(rank, i) * rows, rows), rows)
            dk, dv = dk_acc[there, :] * inv_root, dv_acc[there, :]
            if i == 0:
                dk, dv = dk + shared_ref[:, :HD], dv + shared_ref[:, HD:]
            dkv_ref[here, :HD] = turn(dk, cos_ref[here, :], -sin_ref[here, :]).astype(bf16)
            dkv_ref[here, HD:] = dv.astype(bf16)


VMEM_LIMIT = 48 * 2**20


def attend(where, qkv, cos2, sin2, rows):
    slot, width = qkv.shape[0], qkv.shape[1] - 2 * HD
    heads = width // HD
    half = slot * slot * heads * HD
    return pl.pallas_call(
        attend_kernel,
        name="attend",
        grid_spec=pltpu.PrefetchScalarGridSpec(
            num_scalar_prefetch=1,
            grid=(slot // rows,),
            in_specs=[
                pl.BlockSpec((rows, width), lambda j, s: (j, 0)),
                pl.BlockSpec((slot, 2 * HD), lambda j, s: (0, width // (2 * HD))),
                pl.BlockSpec((slot, HD), lambda j, s: (0, 0)),
                pl.BlockSpec((slot, HD), lambda j, s: (0, 0)),
            ],
            out_specs=[
                pl.BlockSpec((rows, width), lambda j, s: (j, 0)),
                pl.BlockSpec((slot, 2 * HD), lambda j, s: (0, 0)),
                pl.BlockSpec((rows, width), lambda j, s: (j, 0)),
                pl.BlockSpec((rows, HD), lambda j, s: (j, 0)),
            ],
        ),
        out_shape=(
            jax.ShapeDtypeStruct((slot, width), bf16),
            jax.ShapeDtypeStruct((slot, 2 * HD), bf16),
            jax.ShapeDtypeStruct((slot, width), bf16),
            jax.ShapeDtypeStruct((slot, HD), f32),
        ),
        compiler_params=pltpu.CompilerParams(
            dimension_semantics=("arbitrary",), vmem_limit_bytes=VMEM_LIMIT
        ),
        cost_estimate=pl.CostEstimate(
            flops=4 * half, bytes_accessed=8 * 2**20, transcendentals=slot * slot * heads
        ),
    )(where, qkv, qkv, cos2, sin2)


def attend_back(where, qr, kvt, dmixed, lse, cos2, sin2, shared, rows):
    slot, width = qr.shape
    heads = width // HD
    half = slot * slot * heads * HD
    return pl.pallas_call(
        attend_back_kernel,
        name="attend_back",
        grid_spec=pltpu.PrefetchScalarGridSpec(
            num_scalar_prefetch=1,
            grid=(slot // rows,),
            in_specs=[
                pl.BlockSpec((rows, width), lambda j, s: (j, 0)),
                pl.BlockSpec((slot, 2 * HD), lambda j, s: (0, 0)),
                pl.BlockSpec((rows, width), lambda j, s: (j, 0)),
                pl.BlockSpec((rows, HD), lambda j, s: (j, 0)),
                pl.BlockSpec((slot, HD), lambda j, s: (0, 0)),
                pl.BlockSpec((slot, HD), lambda j, s: (0, 0)),
                pl.BlockSpec((rows, 2 * HD), lambda j, s: (0, 0)),
            ],
            out_specs=[
                pl.BlockSpec((rows, width), lambda j, s: (j, 0)),
                pl.BlockSpec((slot, 2 * HD), lambda j, s: (0, 0)),
            ],
            scratch_shapes=[pltpu.VMEM((slot, HD), f32), pltpu.VMEM((slot, HD), f32)],
        ),
        out_shape=(
            jax.ShapeDtypeStruct((slot, width), bf16),
            jax.ShapeDtypeStruct((slot, 2 * HD), bf16),
        ),
        compiler_params=pltpu.CompilerParams(
            dimension_semantics=("arbitrary",), vmem_limit_bytes=VMEM_LIMIT
        ),
        cost_estimate=pl.CostEstimate(
            flops=10 * half, bytes_accessed=8 * 2**20, transcendentals=slot * slot * heads
        ),
    )(where, qr, kvt, dmixed, lse, cos2, sin2, shared)


def finish_kernel(first_ref, second_ref, gate_ref, up_ref, gain_ref, *out_refs):
    gate_out, up_out, down_out, part_out = out_refs
    gain, part, start = gain_ref[...], 0.0, 0
    for sum_ref in (first_ref, second_ref):
        width = sum_ref.shape[1] // 3
        here = slice(start, start + width)
        gate = sum_ref[:, :width].astype(f32)
        up = sum_ref[:, width : 2 * width].astype(f32)
        terms = gate_ref[:, here].astype(f32) * gate + up_ref[:, here].astype(f32) * up
        part = part + jnp.sum(terms, axis=1, keepdims=True)
        gate_out[:, here] = gate * gain
        up_out[:, here] = up * gain
        down_out[here, :] = sum_ref[:, 2 * width :].astype(f32).T
        start += width
    part_out[...] = part


def finish_attn_kernel(sum_ref, query_ref, gain_ref, query_out, project_out, part_out):
    rows = query_ref.shape[0]
    total = sum_ref[:rows, :].astype(f32)
    query_out[...] = total * gain_ref[...]
    part_out[...] = jnp.sum(query_ref[...].astype(f32) * total, axis=1, keepdims=True)
    project_out[...] = sum_ref[rows : 2 * rows, :].astype(f32).T


def finish_attn(total, query_own, gain):
    rows, width = query_own.shape
    return pl.pallas_call(
        finish_attn_kernel,
        name="finish_attn",
        out_shape=(
            jax.ShapeDtypeStruct((rows, width), f32),
            jax.ShapeDtypeStruct((width, rows), f32),
            jax.ShapeDtypeStruct((rows, 1), f32),
        ),
    )(total, query_own, gain)


def finish_ff(parts, sums, gate_own, up_own, gain):
    rows, ff = gate_own.shape
    widths = [b - a for a, b in parts]
    if rows % HD or any(width % HD for width in widths):
        sums = [total.astype(f32) for total in sums]
        gate = jnp.concatenate([t[:, :w] for t, w in zip(sums, widths)], axis=1)
        up = jnp.concatenate([t[:, w : 2 * w] for t, w in zip(sums, widths)], axis=1)
        down = jnp.concatenate([t[:, 2 * w :] for t, w in zip(sums, widths)], axis=1)
        terms = gate * gate_own.astype(f32) + up * up_own.astype(f32)
        return gate * gain, up * gain, down.T, jnp.sum(terms, axis=1, keepdims=True)
    across = lambda width: pl.BlockSpec((HD, width), lambda i: (i, 0))
    return pl.pallas_call(
        finish_kernel,
        name="finish_ff",
        grid=(rows // HD,),
        in_specs=[across(3 * w) for w in widths] + [across(ff), across(ff), across(1)],
        out_specs=[across(ff), across(ff), pl.BlockSpec((ff, HD), lambda i: (0, i)), across(1)],
        out_shape=(
            jax.ShapeDtypeStruct((rows, ff), f32),
            jax.ShapeDtypeStruct((rows, ff), f32),
            jax.ShapeDtypeStruct((ff, rows), f32),
            jax.ShapeDtypeStruct((rows, 1), f32),
        ),
        compiler_params=pltpu.CompilerParams(dimension_semantics=("arbitrary",)),
        cost_estimate=pl.CostEstimate(
            flops=8 * rows * ff, bytes_accessed=24 * rows * ff, transcendentals=0
        ),
    )(*sums, gate_own, up_own, gain)


def inverse_norm(values):
    return lax.rsqrt(jnp.mean(values * values, axis=-1, keepdims=True) + eps)


def rows_of(array, j, rows):
    return array[j * rows : (j + 1) * rows]


def on_device(
    layer_input,
    lengths,
    w_query,
    w_keyvalue,
    w_project,
    w_gate,
    w_up,
    w_down,
    gain_attn,
    gain_mlp,
    out_grad,
    kv_grad,
):
    rows, model_width = layer_input.shape
    ranks = lax.axis_size("tensor")
    rank = lax.axis_index("tensor").astype(jnp.int32)
    length = lengths[0]
    heads_width = w_query.shape[1]
    ff = w_gate.shape[1]
    cut = -(-ff // 256) * 128
    parts = ((0, cut), (cut, ff))

    order = jnp.bitwise_xor(rank, jnp.arange(ranks, dtype=jnp.int32))
    position = (order[:, None] * rows + jnp.arange(rows, dtype=jnp.int32)[None, :]).reshape(-1)
    frequency = rope_base ** (-(jnp.arange(HD // 2, dtype=f32) * 2.0 / HD))
    angles = position.astype(f32)[:, None] * frequency[None, :]
    cosine, sine = jnp.cos(angles), jnp.sin(angles)
    cos2 = jnp.concatenate([cosine, cosine], axis=1)
    sin2 = jnp.concatenate([-sine, sine], axis=1)
    own_mask = (position[:rows] < length).astype(f32)[:, None]
    where = jnp.stack([rank, length])

    gain_one, gain_two = gain_attn.astype(f32)[:, None], gain_mlp.astype(f32)[:, None]
    qkv_own = jnp.concatenate([w_query, w_keyvalue], axis=1).astype(f32)
    shard_rows = qkv_own.shape[0]
    kv_rows = shard_rows // ranks
    scaled_own = (qkv_own * gain_one).astype(bf16)
    kv_part = lax.dynamic_slice_in_dim(scaled_own[:, heads_width:], rank * kv_rows, kv_rows)
    attn_shard = jnp.concatenate(
        [scaled_own[:, :heads_width], w_project.T, kv_part.reshape(-1, heads_width)], axis=0
    )
    pair_own = [
        jnp.concatenate([w_gate[:, a:b], w_up[:, a:b]], axis=1).astype(f32) for a, b in parts
    ]
    ff_shards = [
        jnp.concatenate([(own * gain_two).astype(bf16), w_down[a:b].T], axis=1)
        for (a, b), own in zip(parts, pair_own)
    ]

    residual = layer_input.astype(f32)
    x_own = after(layer_input, attn_shard)
    inputs = all_blocks(x_own, near_blocks(x_own))
    attn_full = gather_dp(attn_shard)

    def norm(block):
        block = block.astype(f32)
        return (block * inverse_norm(block)).astype(bf16)

    normed_one = jnp.concatenate([norm(b) for b in inputs], axis=0)
    top = out_grad.astype(f32) * own_mask
    ready = normed_one, ff_shards[1], top.astype(bf16), cos2, sin2
    ff_full = [gather_dp(after(ff_shards[0], *ready))]
    attn_full = attn_full.reshape(-1, *attn_shard.shape)
    query_full = attn_full[:, :shard_rows].reshape(model_width, heads_width)
    project_full = attn_full[:, shard_rows : 2 * shard_rows].reshape(model_width, heads_width)
    kv_part = attn_full[:, 2 * shard_rows :].reshape(-1, 2 * HD)
    kv_near = near_blocks(kv_part)
    kv_blocks = jnp.concatenate(all_blocks(kv_part, kv_near), axis=0)
    kv_blocks = kv_blocks.reshape(ranks, -1, kv_rows, 2 * HD)
    keyvalue_full = jnp.stack([pick(kv_blocks, order[j], 0) for j in range(ranks)], axis=1)
    qkv_full = jnp.concatenate([query_full, keyvalue_full.reshape(model_width, 2 * HD)], axis=1)
    top_own = after(top.astype(bf16), keyvalue_full)
    top_near = near_blocks(top_own)
    qkv = dot(normed_one, qkv_full, 1, 0)
    qr, kvt, mixed, lse = attend(where, qkv, cos2, sin2, rows)
    ff_full.append(gather_dp(after(ff_shards[1], mixed)))
    mixed_rest = dot(after(mixed[rows:], *top_near), project_full, 1, 1).astype(bf16)
    mixed_sent = send_sums(mixed_rest)
    top_near = [after(block, *mixed_sent) for block in top_near]
    top_all = jnp.concatenate(all_blocks(top_own, top_near), axis=0)
    after_attn = residual + finish_sums(
        dot(mixed[:rows], project_full, 1, 1), mixed_rest, mixed_sent
    )

    inv_two = inverse_norm(after_attn)
    unit_two = after_attn * inv_two
    normed_own = after(unit_two.astype(bf16), top_all)
    pairs = [full[:, : 2 * (b - a)] for (a, b), full in zip(parts, ff_full)]
    downs = [full[:, 2 * (b - a) :] for (a, b), full in zip(parts, ff_full)]
    first_grad = dot(top_all, downs[0], 1, 0)
    normed_near = [after(block, first_grad) for block in near_blocks(normed_own)]
    normed_two = jnp.concatenate(all_blocks(normed_own, normed_near), axis=0)

    def feed(normed, pair, grad):
        width = grad.shape[1]
        both = dot(after(normed, grad), pair, 1, 0)
        gate, up = both[:, :width], both[:, width:]
        sig = jax.nn.sigmoid(gate)
        hidden = (gate * sig * up).astype(bf16)
        gate_grad = (grad * up * sig * (1.0 + gate * (1.0 - sig))).astype(bf16)
        up_grad = (grad * gate * sig).astype(bf16)
        return hidden, jnp.concatenate([gate_grad, up_grad], axis=1)

    def partial(hidden, grads):
        return jnp.concatenate(
            [
                dot(normed_two, grads, 0, 0).astype(bf16),
                dot(top_all, hidden, 0, 0).astype(bf16),
            ],
            axis=1,
        )

    hidden0, grads0 = feed(normed_two, pairs[0], first_grad)
    partial0 = partial(hidden0, grads0)
    rest0 = dot(after(grads0[rows:], partial0), pairs[0], 1, 1)
    hidden1, grads1 = feed(after(normed_two, rest0), pairs[1], dot(top_all, downs[1], 1, 0))
    rest = (rest0 + dot(grads1[rows:], pairs[1], 1, 1)).astype(bf16)
    rest_sent = send_sums(rest)
    partial1 = partial(after(hidden1, *rest_sent), after(grads1, *rest_sent))
    ff_sums = [scatter_dp(partial0), scatter_dp(partial1)]
    own = dot(after(grads0[:rows], partial1), pairs[0], 1, 1) + dot(grads1[:rows], pairs[1], 1, 1)
    scaled = finish_sums(own, rest, rest_sent)
    attn_top = top + inv_two * (
        scaled - unit_two * jnp.mean(scaled * unit_two, axis=-1, keepdims=True)
    )
    attn_top_own = attn_top.astype(bf16)
    attn_top_blocks = all_blocks(attn_top_own, near_blocks(attn_top_own))
    attn_top_all = jnp.concatenate(attn_top_blocks, axis=0)
    hidden = [hidden0, hidden1]
    down_rest = sum(dot(h[rows:], w, 1, 1) for h, w in zip(hidden, downs)).astype(bf16)
    down_rest = after(down_rest, *attn_top_blocks)

    mixed_grad = dot(after(attn_top_all, down_rest, ff_sums[0]), project_full, 1, 0).astype(bf16)
    shared = kv_grad.astype(f32) * own_mask
    query_grad, kv_back = attend_back(
        where, qr, kvt, mixed_grad, lse, cos2, sin2, shared, rows
    )
    down_sent = [after(block, query_grad) for block in send_sums(down_rest)]
    qkv_back = after(jnp.concatenate([query_grad, kv_back], axis=1), *down_sent)
    kv_grads = dot(normed_one, qkv_back[:, heads_width:], 0, 0).astype(bf16)
    kv_grads = kv_grads.reshape(-1, ranks, kv_rows, 2 * HD)
    kv_own, *kv_rest = (pick(kv_grads, order[j], 1).reshape(-1, 2 * HD) for j in range(ranks))
    kv_rest = jnp.concatenate(kv_rest, axis=0)
    kv_sent = send_sums(kv_rest)
    qkv_rest = dot(after(qkv_back[rows:], *kv_sent), qkv_full, 1, 1).astype(bf16)
    qkv_sent = send_sums(after(qkv_rest, *kv_sent, ff_sums[1]))
    query_back = after(qkv_back[:, :heads_width], kv_rest)
    kv_sum = finish_sums(kv_own.astype(f32), kv_rest, kv_sent).astype(bf16)
    attn_partial = jnp.concatenate(
        [
            dot(normed_one, query_back, 0, 0).astype(bf16).reshape(-1, shard_rows, heads_width),
            dot(attn_top_all, mixed, 0, 0).astype(bf16).reshape(-1, shard_rows, heads_width),
            kv_sum.reshape(model_width // shard_rows, -1, heads_width),
        ],
        axis=1,
    ).reshape(-1, heads_width)
    attn_sum = scatter_dp(attn_partial)
    down_sent = [after(block, *qkv_sent) for block in down_sent]
    own_down = sum(
        dot(after(h[:rows], attn_partial), w, 1, 1) for h, w in zip(hidden, downs)
    )
    after_mlp = after_attn + finish_sums(own_down, down_rest, down_sent)
    output = (after_mlp * own_mask).astype(bf16)
    scaled_one = finish_sums(dot(qkv_back[:rows], qkv_full, 1, 1), qkv_rest, qkv_sent)
    inv_one = inverse_norm(residual)
    unit_one = residual * inv_one
    input_grad = attn_top + inv_one * (
        scaled_one - unit_one * jnp.mean(scaled_one * unit_one, axis=-1, keepdims=True)
    )

    grad_gate, grad_up, grad_down, gain_two_part = finish_ff(
        parts, ff_sums, w_gate, w_up, gain_two
    )
    attn_sum = after(attn_sum, output, input_grad, gain_two_part)
    grad_query, grad_project, query_part = finish_attn(attn_sum, w_query, gain_one)
    kv_sum = attn_sum[2 * shard_rows :].astype(f32).reshape(kv_rows, 2 * HD)
    kv_here = lax.dynamic_slice_in_dim(qkv_own[:, heads_width:], rank * kv_rows, kv_rows)
    gain_here = lax.dynamic_slice_in_dim(gain_one, rank * kv_rows, kv_rows)
    small = jnp.concatenate(
        [
            kv_sum * gain_here,
            jnp.sum(kv_here * kv_sum, axis=1, keepdims=True),
            jnp.concatenate([query_part, gain_two_part], axis=1).reshape(kv_rows, -1),
        ],
        axis=1,
    )
    blocks = jnp.stack([small] + [hop(small, j) for j in range(1, ranks)], axis=0)
    sums = jnp.sum(blocks[:, :, 2 * HD + 1 :], axis=0).reshape(shard_rows, 2)
    placed = jnp.concatenate([pick(blocks, order[j], 0) for j in range(ranks)], axis=0)
    return (
        output,
        input_grad,
        grad_query,
        placed[:, : 2 * HD],
        grad_project,
        grad_gate,
        grad_up,
        grad_down,
        sums[:, 0] + placed[:, 2 * HD],
        sums[:, 1],
    )


def solution(mesh):
    placed = (
        P(("dp", "tensor"), None),
        P("dp"),
        P("dp", "tensor"),
        P("dp", None),
        P("tensor", "dp"),
        P("dp", "tensor"),
        P("dp", "tensor"),
        P("tensor", "dp"),
        P("dp"),
        P("dp"),
        P(("dp", "tensor"), None),
        P(("dp", "tensor"), None),
    )
    return jax.shard_map(
        on_device,
        mesh=mesh,
        in_specs=placed,
        out_specs=(
            P(("dp", "tensor"), None),
            P(("dp", "tensor"), None),
            P("dp", "tensor"),
            P("dp", None),
            P("tensor", "dp"),
            P("dp", "tensor"),
            P("dp", "tensor"),
            P("tensor", "dp"),
            P("dp"),
            P("dp"),
        ),
        check_vma=False,
    )
```
